256 devices in a mesh: lat: 16 (over z, x_hi), lon: 16 (over x_lo, y, core).
Axes of the slice: x: 4 (x_hi: 2, x_lo: 2; x = x_hi * 2 + x_lo), y: 4, z: 8, core: 2. Of those that a mesh axis runs over, the one named last changes fastest.
Arguments:
- displacement: float32 [32, 384, 2048], P(None, 'lat', 'lon'), may hold values from -6 to 6
- materials: int32 [32, 384, 2048], P(None, 'lat', 'lon'), may hold values from 0 to 3
- ice_mask: int32 [384, 2048], P('lat', 'lon'), may hold values 0 or 1
- ice_height: float32 [384, 2048], P('lat', 'lon'), may hold values from 0.5 to 3
- shear: float32 [4], replicated, may hold values from 0.5 to 4
- restoring: float32 [4], replicated, may hold values from 0.5 to 2
- contrast: float32 [4], replicated, may hold values from 0.3 to 3
- green: float32 [256, 32, 32], P('lat'), may hold values from -1 to 1
Outputs:
- final_displacement: float32 [32, 384, 2048], P(None, 'lat', 'lon')
- potential: float32 [32, 384, 2048], P(None, 'lat', 'lon')
The draws below stay inside these ranges and needn't reach their ends.
All inputs are finite; a program needn't handle non-finite values. No bound on the sum of `ice_mask` on one device may be relied on, other than what follows from the above.
Results may differ from the reference program's by a relative error of at most 0.0003.
Values sent between devices are 32-bit elements; how exact they have to be, the bound alone decides.
A program may use at most 128 MiB of HBM per device.

```python
import math
import jax
import jax.numpy as jnp
from jax import lax

L = 32
LMAX = 256
NMAT = 4
ITERS = 2
SWEEPS = 4
NLAT = 384
NLON = 2048


def with_ends(values, key, low, high):
    longest = values.shape.index(max(values.shape))
    spots = []
    for shift in (0, 1):
        where = [jax.random.randint(jax.random.fold_in(key, axis), (), 0, length) for axis, length in enumerate(values.shape)]
        where[longest] = (where[longest] + shift) % values.shape[longest]
        spots.append(tuple(where))
    return values.at[spots[0]].set(low).at[spots[1]].set(high)


def levels(own_key, dims, cuts, low, top_value):
    def one(dim, blocks):
        steps = jax.random.uniform(jax.random.fold_in(jax.random.fold_in(own_key, 6), dim), (blocks,), jnp.float32, low / len(cuts), top_value / len(cuts))
        return jnp.repeat(jnp.exp(steps), dims[dim] // blocks).reshape((-1,) + (1,) * (len(dims) - dim - 1))

    factor_of = one(*cuts[0])
    for cut in cuts[1:]:
        factor_of = factor_of * one(*cut)
    return factor_of


def noise(stream_key, shape, deviation, bound, cuts=(), held_as=jnp.bfloat16):
    entries = jax.random.normal(stream_key, shape, jnp.float32) * deviation
    if len(cuts) > 0:
        entries = levels(stream_key, shape, cuts, -0.22, 0.18) * entries
    return jnp.clip(entries, min=-bound, max=bound).astype(held_as)


def setup_inputs(seed: int = 0) -> dict:
    streams_of = jax.random.split(jax.random.key(seed), 9)
    displacement = noise(streams_of[0], (L, NLAT, NLON), 1.0, 6.0, ((1, 16), (2, 16)), jnp.float32)
    materials = with_ends(jax.random.randint(streams_of[1], (L, NLAT, NLON), 0, NMAT), jax.random.fold_in(streams_of[1], 1), 0, NMAT - 1).astype(jnp.int32)
    ice_mask = with_ends((jax.random.randint(streams_of[2], (NLAT, NLON), 0, 3) < 1).astype(jnp.int32), jax.random.fold_in(streams_of[2], 1), 0, 1)
    ice_height = jnp.clip(jnp.exp(math.log(3.0) - 1.7917595 * jax.random.uniform(streams_of[3], (NLAT, NLON), jnp.float32) ** levels(streams_of[3], (NLAT, NLON), ((0, 16), (1, 16)), -0.2, 0.2)), 0.5, 3.0)
    shear = jnp.clip(jnp.exp(jax.random.uniform(streams_of[4], (NMAT,), jnp.float32, math.log(0.5), math.log(4.0))), 0.5, 4.0)
    restoring = jnp.clip(jnp.exp(jax.random.uniform(streams_of[5], (NMAT,), jnp.float32, math.log(0.5), math.log(2.0))), 0.5, 2.0)
    contrast = jnp.clip(jnp.exp(jax.random.uniform(streams_of[6], (NMAT,), jnp.float32, math.log(0.3), math.log(3.0))), 0.3, 3.0)
    green = noise(streams_of[7], (LMAX, L, L), L ** -0.5, 1.0, ((0, 16),), jnp.float32)
    return dict(displacement=displacement, materials=materials, ice_mask=ice_mask, ice_height=ice_height, shear=shear, restoring=restoring, contrast=contrast, green=green)


def legendre(theta):
    orders = jnp.arange(LMAX).astype(jnp.int32)
    order_f = orders.astype(jnp.float32)
    cosine = jnp.cos(theta)[:, None]
    sine = jnp.sin(theta)[:, None]
    safe = jnp.maximum(order_f, 1.0)
    growth = jnp.where(orders >= 2, 0.5 * jnp.log((2.0 * safe + 1.0) / (2.0 * safe)), 0.0)
    log_diag = jnp.where(orders >= 1, 0.5 * jnp.log(3.0) + jnp.cumsum(growth), 0.0)
    diagonal = jnp.exp(log_diag[None, :] + order_f[None, :] * jnp.log(sine))

    def advance(carry, degree):
        prev_one, prev_two = carry
        deg_f = degree.astype(jnp.float32)
        first = jnp.sqrt((4.0 * deg_f * deg_f - 1.0) / jnp.maximum(deg_f * deg_f - order_f * order_f, 1.0))
        second = jnp.sqrt(jnp.maximum((deg_f - 1.0) ** 2 - order_f * order_f, 0.0) / jnp.maximum(4.0 * (deg_f - 1.0) ** 2 - 1.0, 1.0))
        general = first * (cosine * prev_one - second * prev_two)
        start_next = jnp.sqrt(2.0 * order_f + 3.0) * cosine * diagonal
        value = jnp.where(orders == degree, diagonal, jnp.where(orders == degree - 1, start_next, jnp.where(orders < degree - 1, general, 0.0)))
        return ((value, prev_one), value)
    zeros = jnp.zeros((theta.shape[0], LMAX), jnp.float32)
    _, table = lax.scan(advance, (zeros, zeros), jnp.arange(LMAX).astype(jnp.int32))
    return table

def fourier_tables(columns, total):
    orders = jnp.arange(LMAX).astype(jnp.int32)
    phase = columns[:, None] * orders[None, :] % total
    angle = 2.0 * jnp.pi / total * phase.astype(jnp.float32)
    forward = jnp.concatenate([jnp.cos(angle), jnp.sin(angle)], axis=1) * (2.0 * jnp.pi / total)
    inverse = jnp.concatenate([jnp.cos(angle), jnp.sin(angle)], axis=1).T
    return (forward, inverse)

def lookup(materials, table):
    result = jnp.zeros(materials.shape, jnp.float32)
    for material in range(NMAT):
        result = result + jnp.where(materials == material, table[material], 0.0)
    return result

def sweep(field, force, stiff, restore):
    lat_pad = jnp.pad(field, ((0, 0), (1, 1), (0, 0)))
    layer_pad = jnp.pad(field, ((1, 1), (0, 0), (0, 0)))
    beside_all = lat_pad[:, 2:] + lat_pad[:, :-2] + jnp.roll(field, 1, 2) + jnp.roll(field, -1, 2)
    beside_all = beside_all + layer_pad[2:] + layer_pad[:-2]
    return (force + stiff * beside_all) / (6.0 * stiff + restore)

def reference(displacement, materials, ice_mask, ice_height, shear, restoring, contrast, green):
    highest = lax.Precision.HIGHEST
    stiff = lookup(materials, shear)
    restore = lookup(materials, restoring)
    rho_scale = lookup(materials, contrast)
    surface = (ice_mask.astype(jnp.float32) * ice_height)[None]
    load = jnp.concatenate([surface, jnp.zeros((L - 1, NLAT, NLON), jnp.float32)], axis=0)
    theta = (jnp.arange(NLAT).astype(jnp.float32) + 0.5) * (jnp.pi / NLAT)
    table = legendre(theta)
    weights = jnp.sin(theta) / (4.0 * NLAT)
    forward, inverse = fourier_tables(jnp.arange(NLON).astype(jnp.int32), NLON)
    field = displacement
    potential = jnp.zeros((L, NLAT, NLON), jnp.float32)
    for iteration in range(ITERS):
        force = load + potential
        for sweep_index in range(SWEEPS):
            field = sweep(field, force, stiff, restore)
        density = rho_scale * field
        spectrum = jnp.dot(density.reshape(L * NLAT, NLON), forward, precision=highest, preferred_element_type=jnp.float32).reshape(L, NLAT, 2, LMAX)
        spectrum = spectrum * weights[None, :, None, None]
        coeffs = jnp.einsum('lam,kacm->lkcm', table, spectrum, precision=highest)
        pot_coeffs = jnp.einsum('lkj,ljcm->lkcm', green, coeffs, precision=highest)
        synth = jnp.einsum('lam,lkcm->kacm', table, pot_coeffs, precision=highest)
        potential = jnp.dot(synth.reshape(L * NLAT, 2 * LMAX), inverse, precision=highest, preferred_element_type=jnp.float32).reshape(L, NLAT, NLON)
    return (field, potential)
```

```python
import functools
import math

import jax
import jax.numpy as jnp
from jax import lax
from jax.experimental import pallas as pl
from jax.experimental.pallas import tpu as pltpu
from jax.sharding import PartitionSpec as P

L = 32
LMAX = 256
NLAT = 384
NLON = 2048
SWEEPS = 4
N = 16
ROWS = 24
COLS = 128
F32 = jnp.float32
BF16 = jnp.bfloat16
MESH = pl.DeviceIdType.MESH


def iota(shape, dim):
    return lax.broadcasted_iota(jnp.int32, shape, dim)


def split(x):
    hi = x.astype(BF16)
    lo = (x - hi.astype(F32)).astype(BF16)
    return hi, lo


def dot(a, b):
    return jnp.dot(a, b, preferred_element_type=F32)


def dot_t(a, b):
    return lax.dot_general(a, b, (((1,), (1,)), ((), ())), preferred_element_type=F32)


def lookup(mat, table):
    out = jnp.where(mat == 0, table[0], 0.0)
    for material in range(1, 4):
        out = jnp.where(mat == material, table[material], out)
    return out


def kernel(
    u_in,
    mat_in,
    mask_in,
    ice_in,
    shear,
    restoring,
    contrast,
    green_in,
    u_out,
    pot_out,
    U,
    Bc,
    Rd,
    Ac,
    rho,
    dens,
    R1,
    FH,
    FL,
    WH,
    WL,
    C16,
    S16,
    wrow,
    Z,
    T2,
    R2,
    AH,
    C3,
    T3,
    R3,
    T4,
    R4,
    XH,
    Y,
    T5,
    R5,
    X5,
    T6,
    R6,
    GR,
    Pf,
    Ph,
    Pl,
    matf,
    load,
    loadx,
    E,
    EL,
    ER,
    PK,
    VT,
    VB,
    WT,
    WB,
    send_sem,
    recv_sem,
    hsend,
    hrecv,
    gsem,
):
    me_lat = lax.axis_index("lat")
    me_lon = lax.axis_index("lon")

    barrier = pltpu.get_barrier_semaphore()

    def greet(d, carry):
        pl.semaphore_signal(barrier, inc=1, device_id={"lon": lax.rem(me_lon + d, N)}, device_id_type=MESH)
        pl.semaphore_signal(barrier, inc=1, device_id={"lat": lax.rem(me_lat + d, N)}, device_id_type=MESH)
        return carry

    lax.fori_loop(1, N, greet, 0)
    pl.semaphore_signal(
        barrier, inc=1, device_id={"lat": me_lon, "lon": lax.rem(me_lat + 1, N)}, device_id_type=MESH
    )

    def tables():
        q = iota((COLS, LMAX), 0)
        m = iota((COLS, LMAX), 1)
        angle = (2.0 * math.pi / NLON) * ((q * m) & (NLON - 1)).astype(F32)
        hi, lo = split(jnp.cos(angle))
        FH[:, 0:LMAX] = hi
        FL[:, 0:LMAX] = lo
        hi, lo = split(jnp.sin(angle))
        FH[:, LMAX:] = hi
        FL[:, LMAX:] = lo
        p = iota((N, LMAX), 0)
        m = iota((N, LMAX), 1)
        angle = (2.0 * math.pi / N) * ((p * m) & (N - 1)).astype(F32)
        C16[...] = jnp.cos(angle)
        S16[...] = jnp.sin(angle)
        lane = iota((LMAX, 2 * COLS), 1)
        m = iota((LMAX, 2 * COLS), 0)
        q = jnp.where(lane < 128, lane, jnp.where(lane < 132, lane - 132 + NLON, lane - 4))
        angle = (2.0 * math.pi / NLON) * ((q * m) & (NLON - 1)).astype(F32)
        hi, lo = split(jnp.cos(angle))
        WH[0:LMAX, :] = hi
        WL[0:LMAX, :] = lo
        hi, lo = split(jnp.sin(angle))
        WH[LMAX:, :] = hi
        WL[LMAX:, :] = lo
        row = iota((ROWS, LMAX), 0) + me_lat * ROWS
        w = jnp.sin((row.astype(F32) + 0.5) * (math.pi / NLAT)) * (2.0 * math.pi / NLON / (4.0 * NLAT))
        wrow[0:ROWS, :] = w
        wrow[ROWS:, :] = w
        Z[...] = jnp.zeros_like(Z)
        C3[...] = jnp.zeros_like(C3)
        for b in range(2):
            U[b, 0] = jnp.zeros((32, 256), F32)
            U[b, L + 1] = jnp.zeros((32, 256), F32)

    def prepare():
        def one(k, carry):
            mat = mat_in[k]
            matf[k] = mat.astype(F32)
            rho[k] = lookup(mat, contrast)
            return carry

        lax.fori_loop(0, L, one, 0)
        load[...] = mask_in[...].astype(F32) * ice_in[...]

    lane24 = iota((ROWS, COLS), 1)

    def pack(read, g):
        def one(kk, acc):
            return jnp.where(lane24 // 8 == kk, pltpu.roll(read(16 * g + kk), 8 * kk + 4, 1), acc)

        return lax.fori_loop(0, 16, one, jnp.zeros((ROWS, COLS), F32))

    left = lax.rem(me_lon + N - 1, N)
    right = lax.rem(me_lon + 1, N)
    up = lax.rem(me_lat + N - 1, N)
    down = lax.rem(me_lat + 1, N)

    def edge_copies(it):
        first, count = (0, 5) if it == 0 else (5, 2)
        part = pl.ds(first, count)
        return [
            pltpu.make_async_remote_copy(
                E.at[part], ER.at[part], hsend.at[it, 0], hrecv.at[it, 0], device_id={"lon": left}, device_id_type=MESH
            ),
            pltpu.make_async_remote_copy(
                E.at[part], EL.at[part], hsend.at[it, 1], hrecv.at[it, 1], device_id={"lon": right}, device_id_type=MESH
            ),
        ]

    def row_copies(it):
        first, count = (0, 35) if it == 0 else (35, 17)
        part = pl.ds(first, count)
        return [
            pltpu.make_async_remote_copy(
                VT.at[part], WT.at[part], hsend.at[it, 2], hrecv.at[it, 2], device_id={"lat": up}, device_id_type=MESH
            ),
            pltpu.make_async_remote_copy(
                VB.at[part], WB.at[part], hsend.at[it, 3], hrecv.at[it, 3], device_id={"lat": down}, device_id_type=MESH
            ),
        ]

    def merge_edges(it):
        first, count = (0, 5) if it == 0 else (5, 2)
        for g in range(count):
            PK[g, 0:ROWS] = jnp.where(lane24 % 8 < 4, EL[first + g], ER[first + g])

    row8 = iota((8, COLS), 0)

    def pair_rows(t, a_top, a_bot, b_top, b_bot):
        VT[t] = jnp.where(row8 < 4, a_top, pltpu.roll(b_top, 4, 0))
        VB[t] = jnp.where(row8 < 4, pltpu.roll(a_bot, 4, 0), b_bot)

    def halo_rows(t):
        top, bot = WT[t], WB[t]
        first = jnp.where(row8 < 4, top, pltpu.roll(bot, 4, 0))
        second = jnp.where(row8 < 4, pltpu.roll(top, 4, 0), bot)
        return first, second

    rows32 = iota((32, 256), 0)
    global_row = me_lat * ROWS + jnp.where(rows32 < 28, rows32, rows32 - 32)
    inside = (global_row >= 0) & (global_row < NLAT)
    inside8 = inside[24:32, 0:COLS]

    def pair_u(base):
        def one(k, carry):
            pair_rows(
                base + k,
                U[0, k + 1, 0:8, 0:COLS],
                U[0, k + 1, 16:24, 0:COLS],
                U[0, k + 17, 0:8, 0:COLS],
                U[0, k + 17, 16:24, 0:COLS],
            )
            return carry

        lax.fori_loop(0, 16, one, 0)
        pair_rows(base + 16, PK[0, 0:8], PK[0, 16:24], PK[1, 0:8], PK[1, 16:24])

    def fill_u(base):
        first, second = halo_rows(base + 16)
        PK[0, 24:32] = jnp.where(inside8, first, 0.0)
        PK[1, 24:32] = jnp.where(inside8, second, 0.0)

        def one(k, carry):
            first, second = halo_rows(base + k)
            U[0, k + 1, 24:32, 0:COLS] = jnp.where(inside8, first, 0.0)
            U[0, k + 17, 24:32, 0:COLS] = jnp.where(inside8, second, 0.0)
            U[0, k + 1, :, COLS:] = pltpu.roll(PK[0], 124 - 8 * k, 1)
            U[0, k + 17, :, COLS:] = pltpu.roll(PK[1], 124 - 8 * k, 1)
            return carry

        lax.fori_loop(0, 16, one, 0)

    def legendre():
        lane = iota((N, 512), 1)
        order = (iota((N, 512), 0) + me_lat * N).astype(F32)
        aa = lane % 32
        a = (lane // 32) * ROWS + jnp.where(aa < 28, aa, aa - 32)
        a = jnp.clip(a, 0, NLAT - 1)
        theta = (a.astype(F32) + 0.5) * (math.pi / NLAT)
        cosine = jnp.cos(theta)
        sine = jnp.sin(theta)
        t = iota((N, LMAX), 1)
        m_int = iota((N, LMAX), 0) + me_lat * N
        t_f = jnp.maximum(t.astype(F32), 1.0)
        growth = jnp.where((t >= 2) & (t <= m_int), 0.5 * jnp.log((2.0 * t_f + 1.0) / (2.0 * t_f)), 0.0)
        log_diag = jnp.sum(growth, axis=1, keepdims=True) + 0.5 * math.log(3.0)
        log_diag = jnp.where(m_int[:, 0:1] >= 1, log_diag, 0.0)
        diagonal = jnp.exp(log_diag + order * jnp.log(sine))
        start = jnp.sqrt(2.0 * order + 3.0) * cosine * diagonal
        deg = iota((N, LMAX), 1).astype(F32)
        m_f = m_int.astype(F32)
        first = jnp.sqrt(
            jnp.maximum(4.0 * deg * deg - 1.0, 1.0) / jnp.maximum(deg * deg - m_f * m_f, 1.0)
        )
        second = jnp.sqrt(
            jnp.maximum((deg - 1.0) * (deg - 1.0) - m_f * m_f, 0.0)
            / jnp.maximum(4.0 * (deg - 1.0) * (deg - 1.0) - 1.0, 1.0)
        )
        order_i = iota((N, 512), 0) + me_lat * N

        def block(lb, carry):
            one, two = carry
            shift = lax.rem(LMAX - 8 * lb, LMAX)
            f = pltpu.roll(first, shift, 1)[:, 0:COLS]
            s = pltpu.roll(second, shift, 1)[:, 0:COLS]
            for r in range(8):
                degree = lb * 8 + r
                fb = jnp.broadcast_to(f[:, r : r + 1], (N, 512))
                sb = jnp.broadcast_to(s[:, r : r + 1], (N, 512))
                general = fb * (cosine * one - sb * two)
                value = jnp.where(
                    order_i == degree, diagonal, jnp.where(order_i == degree - 1, start, general)
                )
                for tile in range(4):
                    Pf[tile, pl.ds(pl.multiple_of(degree * N, N), N), :] = value[:, tile * COLS : (tile + 1) * COLS]
                one, two = value, one
            return one, two

        zeros = jnp.zeros((N, 512), F32)
        lax.fori_loop(0, LMAX // 8, block, (zeros, zeros))

    def legendre_split():
        def one(m, carry):
            for tile in range(4):
                value = Pf[tile, pl.ds(m, LMAX, stride=N), :]
                hi, lo = split(value)
                Ph[m, :, tile * COLS : (tile + 1) * COLS] = hi
                Pl[m, :, tile * COLS : (tile + 1) * COLS] = lo
            return carry

        lax.fori_loop(0, N, one, 0)

    def exchange(phase, axis, src, dst, peer, sender):
        return pltpu.make_async_remote_copy(
            src,
            dst,
            send_sem.at[phase, peer],
            recv_sem.at[phase, sender],
            device_id={axis: peer},
            device_id_type=MESH,
        )

    def slab(ref, index):
        return ref.at[pl.ds(pl.multiple_of(index * N, N), N)]

    def swap_start(phase, axis, me, src, dst):
        def one(d, carry):
            peer = lax.rem(me + d, N)
            exchange(phase, axis, slab(src, peer), slab(dst, me), peer, me).start()
            return carry

        lax.fori_loop(1, N, one, 0)
        mine = pl.ds(pl.multiple_of(me * N, N), N)
        dst[mine, :] = src[mine, :]

    def swap_wait(phase, axis, me, src, dst):
        def one(d, carry):
            peer = lax.rem(me + d, N)
            copy = exchange(phase, axis, slab(src, peer), slab(dst, peer), peer, peer)
            copy.wait_send()
            copy.wait_recv()
            return carry

        lax.fori_loop(1, N, one, 0)

    def sweep(src, dst):
        def one(k, carry):
            c = U[src, k + 1]
            around = (
                pltpu.roll(c, 1, 0)
                + pltpu.roll(c, 31, 0)
                + pltpu.roll(c, 1, 1)
                + pltpu.roll(c, 255, 1)
                + U[src, k]
                + U[src, k + 2]
            )
            U[dst, k + 1] = Ac[k] + Bc[k] * around
            return carry

        lax.fori_loop(0, L, one, 0)

    def coefficients():
        first, second = halo_rows(33)
        PK[2, 24:32] = first
        PK[3, 24:32] = second

        def one(k, carry):
            low = []
            first, second = halo_rows(17 + k)
            for kk, rows in ((k, first), (k + 16, second)):
                g = 2 if len(low) == 0 else 3
                low.append(g)
                main = jnp.concatenate([matf[kk], rows], axis=0)
                side = pltpu.roll(PK[g], 124 - 8 * k, 1)
                mat = jnp.concatenate([main, side], axis=1)
                st = lookup(mat, shear)
                re = lookup(mat, restoring)
                inv = jnp.where(inside, 1.0 / (6.0 * st + re), 0.0)
                Rd[kk] = inv
                Bc[kk] = st * inv
                Ac[kk] = jnp.zeros((32, 256), F32)
            return carry

        lax.fori_loop(0, 16, one, 0)
        first, second = halo_rows(34)
        PK[4, 24:32] = second
        loadx[0:ROWS, 0:COLS] = load[...]
        loadx[ROWS:, 0:COLS] = first
        loadx[:, COLS:] = pltpu.roll(PK[4], 124, 1)
        Ac[0] = loadx[...] * Rd[0]

    lane16 = iota((N, COLS), 1)
    rowmod = iota((64, LMAX), 0) % N
    rowmod_w = iota((64, 512), 0) % N

    def forward_fourier():
        def part(p, acc):
            acc_c, acc_s = acc
            x = R1[p].reshape(2 * ROWS, COLS)
            hi, lo = split(x)
            r = dot(jnp.concatenate([hi, lo], axis=0), FH[...])
            r = r[0 : 2 * ROWS] + r[2 * ROWS :] + dot(hi, FL[...])
            yc = r[:, 0:LMAX]
            ys = r[:, LMAX:]
            c = C16[pl.ds(p, 1), :]
            s = S16[pl.ds(p, 1), :]
            return acc_c + (c * yc - s * ys), acc_s + (s * yc + c * ys)

        def one(d, acc):
            p = lax.rem(me_lon + d, N)
            copy = exchange(0, "lon", dens.at[p], R1.at[p], p, p)
            copy.wait_send()
            copy.wait_recv()
            return part(p, acc)

        zeros = jnp.zeros((2 * ROWS, LMAX), F32)
        R1[me_lon] = dens[me_lon]
        acc_c, acc_s = lax.fori_loop(1, N, one, part(me_lon, (zeros, zeros)))
        for c, acc in ((0, acc_c), (1, acc_s)):
            acc = acc * wrow[...]
            for kk in range(2):
                Z[(2 * c + kk) * 32 : (2 * c + kk) * 32 + ROWS, :] = acc[kk * ROWS : (kk + 1) * ROWS]
        T2[...] = jnp.transpose(Z[...])

    def forward_legendre():
        for t in range(4):
            parts = [R2[(4 * t + ii) * N : (4 * t + ii + 1) * N, :] for ii in range(4)]
            for ck in range(4):
                out = None
                for ii in range(4):
                    turn = ((ii - ck) * 32) % COLS
                    v = parts[ii] if turn == 0 else pltpu.roll(parts[ii], turn, 1)
                    out = v if out is None else jnp.where(lane16 // 32 == ii, v, out)
                hi, lo = split(out)
                AH[ck * N : (ck + 1) * N, t * COLS : (t + 1) * COLS] = hi
                AH[64 + ck * N : 64 + (ck + 1) * N, t * COLS : (t + 1) * COLS] = lo

        def one(m, acc):
            r = dot_t(AH[...], Ph[m])
            r = r[0:64] + r[64:] + dot_t(AH[0:64], Pl[m])
            return jnp.where(rowmod == m, r, acc)

        C3[0:64, :] = lax.fori_loop(0, N, one, jnp.zeros((64, LMAX), F32))
        T3[...] = jnp.transpose(C3[...])

    def layer_sum():
        even = (lane16 // 16) % 2 == 0
        for l in range(N):
            r = R3[pl.ds(l, N, stride=N), :]
            r = jnp.concatenate([r, pltpu.roll(r, COLS - 16, 1)], axis=0)
            out = jnp.dot(GR[l], r, precision=lax.Precision.HIGHEST, preferred_element_type=F32)
            T4[pl.ds(l, N, stride=N), :] = jnp.where(even, out[0:N], pltpu.roll(out[N:], 16, 1))

    def inverse_legendre():
        hi, lo = split(jnp.transpose(R4[...])[0:64])
        XH[0:64, :] = hi
        XH[64:, :] = lo

        def one(m, carry):
            r = dot(XH[...], Ph[m])
            r = r[0:64] + r[64:] + dot(XH[0:64], Pl[m])
            Y[...] = jnp.where(rowmod_w == m, r, Y[...])
            return carry

        Y[...] = jnp.zeros_like(Y)
        lax.fori_loop(0, N, one, 0)
        for i in range(N):
            t, ii = i // 4, i % 4
            out = None
            for ck in range(4):
                turn = ((ck - ii) * 32) % COLS
                v = Y[ck * N : (ck + 1) * N, t * COLS : (t + 1) * COLS]
                v = v if turn == 0 else pltpu.roll(v, turn, 1)
                out = v if out is None else jnp.where(lane16 // 32 == ck, v, out)
            T5[i * N : (i + 1) * N, :] = out

    lane8 = iota((8, COLS), 1)

    def inverse_fourier():
        X5[...] = jnp.transpose(R5[...])

        def one(d, carry):
            p = lax.rem(me_lon + d, N)
            c = C16[pl.ds(p, 1), :]
            s = S16[pl.ds(p, 1), :]
            a = X5[0:64, :]
            b = X5[64:, :]
            x = jnp.concatenate([a * c + b * s, b * c - a * s], axis=1)
            hi, lo = split(x)
            r = dot(jnp.concatenate([hi, lo], axis=0), WH[...])
            r = r[0:64] + r[64:] + dot(hi, WL[...])
            T6[p, 0:64, :] = r[:, 0:COLS]
            side = r[0:8, COLS:]
            for t in range(1, 8):
                side = jnp.where(lane8 // 8 == t, pltpu.roll(r[8 * t : 8 * t + 8, COLS:], 8 * t, 1), side)
            T6[p, 64:72, :] = side

            @pl.when(d < N)
            def _():
                exchange(5, "lon", T6.at[p], R6.at[me_lon], p, me_lon).start()

            return carry

        lax.fori_loop(1, N + 1, one, 0)
        R6[me_lon] = T6[me_lon]

        def wait(d, carry):
            p = lax.rem(me_lon + d, N)
            copy = exchange(5, "lon", T6.at[p], R6.at[p], p, p)
            copy.wait_send()
            copy.wait_recv()
            return carry

        lax.fori_loop(1, N, wait, 0)

    def send_density():
        def one(q, carry):
            for kk in range(2):
                k = kk * N + q
                dens[q, kk] = rho[k] * U[0, k + 1, 0:ROWS, 0:COLS]
            return carry

        lax.fori_loop(0, N, one, 0)

        def start(d, carry):
            p = lax.rem(me_lon + d, N)
            exchange(0, "lon", dens.at[p], R1.at[me_lon], p, me_lon).start()
            return carry

        lax.fori_loop(1, N, start, 0)

    def load_u(k, carry):
        U[0, k + 1, 0:ROWS, 0:COLS] = u_in[k]
        return carry

    prepare()
    lax.fori_loop(0, L, load_u, 0)
    E[0] = pack(lambda k: u_in[k], 0)
    E[1] = pack(lambda k: u_in[k], 1)
    E[2] = pack(lambda k: matf[k], 0)
    E[3] = pack(lambda k: matf[k], 1)
    E[4] = pltpu.roll(load[...], 4, 1)
    pl.semaphore_wait(barrier, 2 * N - 1)
    edges = edge_copies(0)
    for copy in edges:
        copy.start()
    tables()
    for copy in edges:
        copy.wait()
    merge_edges(0)
    pair_u(0)

    def pair_mat(k, carry):
        pair_rows(17 + k, matf[k, 0:8], matf[k, 16:24], matf[k + 16, 0:8], matf[k + 16, 16:24])
        return carry

    lax.fori_loop(0, 16, pair_mat, 0)
    pair_rows(33, PK[2, 0:8], PK[2, 16:24], PK[3, 0:8], PK[3, 16:24])
    pair_rows(34, load[0:8], load[16:24], PK[4, 0:8], PK[4, 16:24])
    rows = row_copies(0)
    for copy in rows:
        copy.start()
    green = pltpu.make_async_remote_copy(
        green_in,
        GR,
        gsem.at[0],
        gsem.at[1],
        device_id={"lat": lax.rem(me_lon + N - 1, N), "lon": me_lat},
        device_id_type=MESH,
    )
    green.start()
    legendre()
    legendre_split()
    for copy in rows:
        copy.wait()
    fill_u(0)
    coefficients()

    for it in range(2):
        if it == 1:
            for copy in rows:
                copy.wait()
            fill_u(35)

            def force(j, carry):
                side = R6[j, 64:72, :]
                for kk in range(2):
                    k = kk * N + j
                    main = R6[j, kk * 32 : (kk + 1) * 32, :]
                    halo = jnp.concatenate(
                        [pltpu.roll(side, 124 - 8 * (4 * kk + g), 1) for g in range(4)], axis=0
                    )
                    Ac[k] = jnp.concatenate([main, halo], axis=1) * Rd[k]
                return carry

            lax.fori_loop(0, N, force, 0)
            Ac[0] = Ac[0] + loadx[...] * Rd[0]
        for s in range(SWEEPS):
            sweep(s % 2, (s + 1) % 2)
        send_density()
        if it == 0:
            E[5] = pack(lambda k: U[0, k + 1, 0:ROWS, 0:COLS], 0)
            E[6] = pack(lambda k: U[0, k + 1, 0:ROWS, 0:COLS], 1)
        else:

            def store_u(k, carry):
                u_out[k] = U[0, k + 1, 0:ROWS, 0:COLS]
                return carry

            lax.fori_loop(0, L, store_u, 0)
        forward_fourier()
        swap_start(1, "lat", me_lat, T2, R2)
        if it == 0:
            edges = edge_copies(1)
            for copy in edges:
                copy.start()
        swap_wait(1, "lat", me_lat, T2, R2)
        forward_legendre()
        swap_start(2, "lon", me_lon, T3, R3)
        if it == 0:
            for copy in edges:
                copy.wait()
            merge_edges(1)
            pair_u(35)
            rows = row_copies(1)
            for copy in rows:
                copy.start()
            green.wait()
        swap_wait(2, "lon", me_lon, T3, R3)
        layer_sum()
        swap_start(3, "lon", me_lon, T4, R4)
        swap_wait(3, "lon", me_lon, T4, R4)
        inverse_legendre()
        swap_start(4, "lat", me_lat, T5, R5)
        swap_wait(4, "lat", me_lat, T5, R5)
        inverse_fourier()

    def store_pot(j, carry):
        for kk in range(2):
            pot_out[kk * N + j] = R6[j, kk * 32 : kk * 32 + ROWS, :]
        return carry

    lax.fori_loop(0, N, store_pot, 0)


def on_device(displacement, materials, ice_mask, ice_height, shear, restoring, contrast, green):
    vmem = pl.BlockSpec(memory_space=pltpu.VMEM)
    smem = pl.BlockSpec(memory_space=pltpu.SMEM)
    field = jax.ShapeDtypeStruct((L, ROWS, COLS), F32)
    scratch = [
        ((2, L + 2, 32, 256), F32),
        ((L, 32, 256), F32),
        ((L, 32, 256), F32),
        ((L, 32, 256), F32),
        ((L, ROWS, COLS), F32),
        ((N, 2, ROWS, COLS), F32),
        ((N, 2, ROWS, COLS), F32),
        ((COLS, 512), BF16),
        ((COLS, 512), BF16),
        ((512, 256), BF16),
        ((512, 256), BF16),
        ((N, LMAX), F32),
        ((N, LMAX), F32),
        ((2 * ROWS, LMAX), F32),
        ((128, LMAX), F32),
        ((LMAX, COLS), F32),
        ((LMAX, COLS), F32),
        ((128, 512), BF16),
        ((128, LMAX), F32),
        ((LMAX, COLS), F32),
        ((LMAX, COLS), F32),
        ((LMAX, COLS), F32),
        ((LMAX, COLS), F32),
        ((128, LMAX), BF16),
        ((64, 512), F32),
        ((LMAX, COLS), F32),
        ((LMAX, COLS), F32),
        ((128, LMAX), F32),
        ((N, 72, COLS), F32),
        ((N, 72, COLS), F32),
        ((N, L, L), F32),
        ((4, LMAX * N, COLS), F32),
        ((N, LMAX, 512), BF16),
        ((N, LMAX, 512), BF16),
        ((L, ROWS, COLS), F32),
        ((ROWS, COLS), F32),
        ((32, 256), F32),
        ((7, ROWS, COLS), F32),
        ((7, ROWS, COLS), F32),
        ((7, ROWS, COLS), F32),
        ((5, 32, COLS), F32),
        ((52, 8, COLS), F32),
        ((52, 8, COLS), F32),
        ((52, 8, COLS), F32),
        ((52, 8, COLS), F32),
    ]
    return pl.pallas_call(
        kernel,
        out_shape=(field, field),
        in_specs=[vmem] * 4 + [smem] * 3 + [vmem],
        out_specs=(vmem, vmem),
        scratch_shapes=[pltpu.VMEM(shape, dtype) for shape, dtype in scratch]
        + [
            pltpu.SemaphoreType.DMA((6, N)),
            pltpu.SemaphoreType.DMA((6, N)),
            pltpu.SemaphoreType.DMA((2, 4)),
            pltpu.SemaphoreType.DMA((2, 4)),
            pltpu.SemaphoreType.DMA((2,)),
        ],
        compiler_params=pltpu.CompilerParams(
            collective_id=0, has_side_effects=True, vmem_limit_bytes=60 * 1024 * 1024
        ),
    )(displacement, materials, ice_mask, ice_height, shear, restoring, contrast, green)


def solution(mesh):
    in_specs = (
        P(None, "lat", "lon"),
        P(None, "lat", "lon"),
        P("lat", "lon"),
        P("lat", "lon"),
        P(),
        P(),
        P(),
        P("lat", None, None),
    )
    out_specs = (P(None, "lat", "lon"), P(None, "lat", "lon"))
    return jax.shard_map(
        on_device, mesh=mesh, in_specs=in_specs, out_specs=out_specs, check_vma=False
    )
```

```python
import functools
import math

import jax
import jax.numpy as jnp
from jax import lax
from jax.experimental import pallas as pl
from jax.experimental.pallas import tpu as pltpu
from jax.sharding import PartitionSpec as P

L = 32
LMAX = 256
NLAT = 384
NLON = 2048
SWEEPS = 4
N = 16
ROWS = 24
COLS = 128
F32 = jnp.float32
BF16 = jnp.bfloat16
MESH = pl.DeviceIdType.MESH


def iota(shape, dim):
    return lax.broadcasted_iota(jnp.int32, shape, dim)


def split(x):
    hi = x.astype(BF16)
    lo = (x - hi.astype(F32)).astype(BF16)
    return hi, lo


def dot(a, b):
    return jnp.dot(a, b, preferred_element_type=F32)


def dot_t(a, b):
    return lax.dot_general(a, b, (((1,), (1,)), ((), ())), preferred_element_type=F32)


def unrolled(total, factor, one):
    def body(step, carry):
        for part in range(factor):
            one(step * factor + part)
        return carry

    lax.fori_loop(0, total // factor, body, 0)


def lookup(mat, table):
    out = jnp.where(mat == 0, table[0], 0.0)
    for material in range(1, 4):
        out = jnp.where(mat == material, table[material], out)
    return out


def kernel(
    u_in,
    mat_in,
    mask_in,
    ice_in,
    shear,
    restoring,
    contrast,
    green_in,
    u_out,
    pot_out,
    U,
    Bc,
    Rd,
    Ac,
    rho,
    dens,
    R1,
    FH,
    FL,
    WH,
    WL,
    C16,
    S16,
    wrow,
    Z,
    T2,
    R2,
    AH,
    T3,
    R3,
    T4,
    R4,
    RH,
    RL,
    XH,
    Y,
    T5,
    R5,
    X5,
    T6,
    R6,
    GR,
    GX,
    Ph,
    Pl,
    matf,
    load,
    loadx,
    E,
    EL,
    ER,
    PK,
    VT,
    VB,
    WT,
    WB,
    send_sem,
    recv_sem,
    hsend,
    hrecv,
    gsem,
):
    me_lat = lax.axis_index("lat")
    me_lon = lax.axis_index("lon")

    barrier = pltpu.get_barrier_semaphore()

    def greet(d, carry):
        pl.semaphore_signal(barrier, inc=1, device_id={"lon": lax.rem(me_lon + d, N)}, device_id_type=MESH)
        pl.semaphore_signal(barrier, inc=1, device_id={"lat": lax.rem(me_lat + d, N)}, device_id_type=MESH)
        return carry

    lax.fori_loop(1, N, greet, 0)
    pl.semaphore_signal(
        barrier, inc=1, device_id={"lat": me_lon, "lon": lax.rem(me_lat + 1, N)}, device_id_type=MESH
    )

    def tables():
        q = iota((COLS, LMAX), 0)
        m = iota((COLS, LMAX), 1)
        angle = (2.0 * math.pi / NLON) * ((q * m) & (NLON - 1)).astype(F32)
        hi, lo = split(jnp.cos(angle))
        FH[:, 0:LMAX] = hi
        FL[:, 0:LMAX] = lo
        hi, lo = split(jnp.sin(angle))
        FH[:, LMAX:] = hi
        FL[:, LMAX:] = lo
        p = iota((N, LMAX), 0)
        m = iota((N, LMAX), 1)
        angle = (2.0 * math.pi / N) * ((p * m) & (N - 1)).astype(F32)
        C16[...] = jnp.cos(angle)
        S16[...] = jnp.sin(angle)
        lane = iota((LMAX, 2 * COLS), 1)
        m = iota((LMAX, 2 * COLS), 0)
        q = jnp.where(lane < 128, lane, jnp.where(lane < 132, lane - 132 + NLON, lane - 4))
        angle = (2.0 * math.pi / NLON) * ((q * m) & (NLON - 1)).astype(F32)
        hi, lo = split(jnp.cos(angle))
        WH[0:LMAX, :] = hi
        WL[0:LMAX, :] = lo
        hi, lo = split(jnp.sin(angle))
        WH[LMAX:, :] = hi
        WL[LMAX:, :] = lo
        row = iota((ROWS, LMAX), 0) + me_lat * ROWS
        w = jnp.sin((row.astype(F32) + 0.5) * (math.pi / NLAT)) * (2.0 * math.pi / NLON / (4.0 * NLAT))
        wrow[0:ROWS, :] = w
        wrow[ROWS:, :] = w
        Z[...] = jnp.zeros_like(Z)
        for b in range(2):
            U[b, 0] = jnp.zeros((32, 256), F32)
            U[b, L + 1] = jnp.zeros((32, 256), F32)

    def prepare():
        def one(k):
            mat = mat_in[k]
            matf[k] = mat.astype(F32)
            rho[k] = lookup(mat, contrast)
            U[0, k + 1, 0:ROWS, 0:COLS] = u_in[k]

        unrolled(L, 4, one)
        load[...] = mask_in[...].astype(F32) * ice_in[...]

    lane24 = iota((ROWS, COLS), 1)

    def pack(read, g):
        acc = jnp.zeros((ROWS, COLS), F32)
        for kk in range(16):
            acc = jnp.where(lane24 // 8 == kk, pltpu.roll(read(16 * g + kk), (8 * kk + 4) % COLS, 1), acc)
        return acc

    left = lax.rem(me_lon + N - 1, N)
    right = lax.rem(me_lon + 1, N)
    up = lax.rem(me_lat + N - 1, N)
    down = lax.rem(me_lat + 1, N)

    def edge_copies(it):
        first, count = (0, 5) if it == 0 else (5, 2)
        part = pl.ds(first, count)
        return [
            pltpu.make_async_remote_copy(
                E.at[part], ER.at[part], hsend.at[it, 0], hrecv.at[it, 0], device_id={"lon": left}, device_id_type=MESH
            ),
            pltpu.make_async_remote_copy(
                E.at[part], EL.at[part], hsend.at[it, 1], hrecv.at[it, 1], device_id={"lon": right}, device_id_type=MESH
            ),
        ]

    def row_copies(it):
        first, count = (0, 35) if it == 0 else (35, 17)
        part = pl.ds(first, count)
        return [
            pltpu.make_async_remote_copy(
                VT.at[part], WT.at[part], hsend.at[it, 2], hrecv.at[it, 2], device_id={"lat": up}, device_id_type=MESH
            ),
            pltpu.make_async_remote_copy(
                VB.at[part], WB.at[part], hsend.at[it, 3], hrecv.at[it, 3], device_id={"lat": down}, device_id_type=MESH
            ),
        ]

    def merge_edges(it):
        first, count = (0, 5) if it == 0 else (5, 2)
        for g in range(count):
            PK[g, 0:ROWS] = jnp.where(lane24 % 8 < 4, EL[first + g], ER[first + g])

    row8 = iota((8, COLS), 0)

    def pair_rows(t, a_top, a_bot, b_top, b_bot):
        VT[t] = jnp.where(row8 < 4, a_top, pltpu.roll(b_top, 4, 0))
        VB[t] = jnp.where(row8 < 4, pltpu.roll(a_bot, 4, 0), b_bot)

    def halo_rows(t):
        top, bot = WT[t], WB[t]
        first = jnp.where(row8 < 4, top, pltpu.roll(bot, 4, 0))
        second = jnp.where(row8 < 4, pltpu.roll(top, 4, 0), bot)
        return first, second

    rows32 = iota((32, 256), 0)
    global_row = me_lat * ROWS + jnp.where(rows32 < 28, rows32, rows32 - 32)
    inside = (global_row >= 0) & (global_row < NLAT)
    inside8 = inside[24:32, 0:COLS]

    def pair_u(base):
        def one(k):
            pair_rows(
                base + k,
                U[0, k + 1, 0:8, 0:COLS],
                U[0, k + 1, 16:24, 0:COLS],
                U[0, k + 17, 0:8, 0:COLS],
                U[0, k + 17, 16:24, 0:COLS],
            )

        unrolled(16, 4, one)
        pair_rows(base + 16, PK[0, 0:8], PK[0, 16:24], PK[1, 0:8], PK[1, 16:24])

    def fill_u(base):
        first, second = halo_rows(base + 16)
        PK[0, 24:32] = jnp.where(inside8, first, 0.0)
        PK[1, 24:32] = jnp.where(inside8, second, 0.0)

        def one(k):
            first, second = halo_rows(base + k)
            U[0, k + 1, 24:32, 0:COLS] = jnp.where(inside8, first, 0.0)
            U[0, k + 17, 24:32, 0:COLS] = jnp.where(inside8, second, 0.0)
            U[0, k + 1, :, COLS:] = pltpu.roll(PK[0], 124 - 8 * k, 1)
            U[0, k + 17, :, COLS:] = pltpu.roll(PK[1], 124 - 8 * k, 1)

        unrolled(16, 4, one)

    def legendre_setup():
        lane = iota((N, 512), 1)
        order = (iota((N, 512), 0) + me_lat * N).astype(F32)
        aa = lane % 32
        a = (lane // 32) * ROWS + jnp.where(aa < 28, aa, aa - 32)
        a = jnp.clip(a, 0, NLAT - 1)
        theta = (a.astype(F32) + 0.5) * (math.pi / NLAT)
        cosine = jnp.cos(theta)
        sine = jnp.sin(theta)
        t = iota((N, LMAX), 1)
        m_int = iota((N, LMAX), 0) + me_lat * N
        t_f = jnp.maximum(t.astype(F32), 1.0)
        growth = jnp.where((t >= 2) & (t <= m_int), 0.5 * jnp.log((2.0 * t_f + 1.0) / (2.0 * t_f)), 0.0)
        log_diag = jnp.sum(growth, axis=1, keepdims=True) + 0.5 * math.log(3.0)
        log_diag = jnp.where(m_int[:, 0:1] >= 1, log_diag, 0.0)
        diagonal = jnp.exp(log_diag + order * jnp.log(sine))
        start = jnp.sqrt(2.0 * order + 3.0) * cosine * diagonal
        deg = iota((N, LMAX), 1).astype(F32)
        m_f = m_int.astype(F32)
        first = jnp.sqrt(
            jnp.maximum(4.0 * deg * deg - 1.0, 1.0) / jnp.maximum(deg * deg - m_f * m_f, 1.0)
        )
        second = jnp.sqrt(
            jnp.maximum((deg - 1.0) * (deg - 1.0) - m_f * m_f, 0.0)
            / jnp.maximum(4.0 * (deg - 1.0) * (deg - 1.0) - 1.0, 1.0)
        )
        order_i = iota((N, 512), 0) + me_lat * N

        def block(lb, carry):
            one, two = carry
            shift = lax.rem(LMAX - 8 * lb, LMAX)
            f = pltpu.roll(first, shift, 1)[:, 0:COLS]
            s = pltpu.roll(second, shift, 1)[:, 0:COLS]
            for r in range(8):
                degree = lb * 8 + r
                fb = jnp.broadcast_to(f[:, r : r + 1], (N, 512))
                sb = jnp.broadcast_to(s[:, r : r + 1], (N, 512))
                general = fb * (cosine * one - sb * two)
                value = jnp.where(
                    order_i == degree, diagonal, jnp.where(order_i == degree - 1, start, general)
                )
                hi, lo = split(value)
                here = pl.ds(pl.multiple_of(degree * N, N), N)
                Ph[here, :] = hi
                Pl[here, :] = lo
                one, two = value, one
            return one, two

        zeros = jnp.zeros((N, 512), F32)
        return block, (zeros, zeros)

    def exchange(phase, axis, src, dst, peer, sender):
        return pltpu.make_async_remote_copy(
            src,
            dst,
            send_sem.at[phase, peer],
            recv_sem.at[phase, sender],
            device_id={axis: peer},
            device_id_type=MESH,
        )

    def slab(ref, index, size):
        return ref.at[pl.ds(pl.multiple_of(index * size, size), size)]

    def swap_start(phase, axis, me, src, dst, size):
        def one(d, carry):
            peer = lax.rem(me + d, N)
            exchange(phase, axis, slab(src, peer, size), slab(dst, me, size), peer, me).start()
            return carry

        lax.fori_loop(1, N, one, 0)
        mine = pl.ds(pl.multiple_of(me * size, size), size)
        dst[mine, :] = src[mine, :]

    def swap_wait(phase, axis, me, src, dst, size):
        def one(d, carry):
            peer = lax.rem(me + d, N)
            copy = exchange(phase, axis, slab(src, peer, size), slab(dst, peer, size), peer, peer)
            copy.wait_send()
            copy.wait_recv()
            return carry

        lax.fori_loop(1, N, one, 0)

    lane32 = iota((32, COLS), 1)

    def sweep(src, dst, last):
        rows = ROWS if last else 32

        def one(k):
            t0 = U[src, k + 1, :, 0:COLS]
            t1 = U[src, k + 1, :, COLS:]
            r0, r1 = pltpu.roll(t0[0:rows], 1, 1), pltpu.roll(t1[0:rows], 1, 1)
            l0, l1 = pltpu.roll(t0[0:rows], COLS - 1, 1), pltpu.roll(t1[0:rows], COLS - 1, 1)
            first = lane32[0:rows] == 0
            final = lane32[0:rows] == COLS - 1
            around = (
                (jnp.where(first, r1, r0) + jnp.where(final, l1, l0))
                + (pltpu.roll(t0, 1, 0) + pltpu.roll(t0, 31, 0))[0:rows]
                + (U[src, k, 0:rows, 0:COLS] + U[src, k + 2, 0:rows, 0:COLS])
            )
            U[dst, k + 1, 0:rows, 0:COLS] = Ac[k, 0:rows, 0:COLS] + Bc[k, 0:rows, 0:COLS] * around
            if not last:
                around = (
                    (jnp.where(first, r0, r1) + jnp.where(final, l0, l1))
                    + (pltpu.roll(t1, 1, 0) + pltpu.roll(t1, 31, 0))
                    + (U[src, k, :, COLS:] + U[src, k + 2, :, COLS:])
                )
                U[dst, k + 1, :, COLS:] = Ac[k, :, COLS:] + Bc[k, :, COLS:] * around

        unrolled(L, 4, one)

    def coefficient(k, rows, cols, mat, valid):
        st = lookup(mat, shear)
        re = lookup(mat, restoring)
        inv = 1.0 / (6.0 * st + re)
        if valid is not None:
            inv = jnp.where(valid, inv, 0.0)
        Rd[k, rows, cols] = inv
        Bc[k, rows, cols] = st * inv
        Ac[k, rows, cols] = jnp.zeros(inv.shape, F32)

    def main_coefficients():
        unrolled(L, 4, lambda k: coefficient(k, slice(0, ROWS), slice(0, COLS), matf[k], None))

    inside_side = inside[:, 0:COLS]

    def margin_coefficients():
        first, second = halo_rows(33)
        PK[2, 24:32] = first
        PK[3, 24:32] = second

        def one(k):
            first, second = halo_rows(17 + k)
            coefficient(k, slice(ROWS, 32), slice(0, COLS), first, inside8)
            coefficient(k + 16, slice(ROWS, 32), slice(0, COLS), second, inside8)
            for g in range(2):
                side = pltpu.roll(PK[2 + g], 124 - 8 * k, 1)
                coefficient(k + 16 * g, slice(0, 32), slice(COLS, 2 * COLS), side, inside_side)

        unrolled(16, 2, one)
        first, second = halo_rows(34)
        PK[4, 24:32] = second
        loadx[0:ROWS, 0:COLS] = load[...]
        loadx[ROWS:, 0:COLS] = first
        loadx[:, COLS:] = pltpu.roll(PK[4], 124, 1)
        Ac[0] = loadx[...] * Rd[0]

    lane16 = iota((N, COLS), 1)
    diagonal64 = iota((64, LMAX), 0) % N == iota((64, LMAX), 1) % N
    diagonal16 = iota((N, COLS), 0) == iota((N, COLS), 1) % N

    def forward_fourier():
        def pair(step, acc):
            acc_c, acc_s = acc
            ps = [lax.rem(me_lon + 2 * step + q, N) for q in range(2)]
            his, los = zip(*[split(R1[p].reshape(2 * ROWS, COLS)) for p in ps])
            r = dot(jnp.concatenate(his + los, axis=0), FH[...])
            r = r[0 : 4 * ROWS] + r[4 * ROWS :] + dot(jnp.concatenate(his, axis=0), FL[...])
            for q, p in enumerate(ps):
                yc = r[2 * ROWS * q : 2 * ROWS * (q + 1), 0:LMAX]
                ys = r[2 * ROWS * q : 2 * ROWS * (q + 1), LMAX:]
                c = C16[pl.ds(p, 1), :]
                s = S16[pl.ds(p, 1), :]
                acc_c, acc_s = acc_c + (c * yc - s * ys), acc_s + (s * yc + c * ys)
            return acc_c, acc_s

        def wait(d):
            p = lax.rem(me_lon + d, N)
            copy = exchange(0, "lon", dens.at[p], R1.at[p], p, p)
            copy.wait_send()
            copy.wait_recv()

        def one(step, acc):
            wait(2 * step)
            wait(2 * step + 1)
            return pair(step, acc)

        zeros = jnp.zeros((2 * ROWS, LMAX), F32)
        R1[me_lon] = dens[me_lon]
        wait(1)
        acc_c, acc_s = lax.fori_loop(1, N // 2, one, pair(0, (zeros, zeros)))
        for c, acc in ((0, acc_c), (1, acc_s)):
            acc = acc * wrow[...]
            for kk in range(2):
                Z[(2 * c + kk) * 32 : (2 * c + kk) * 32 + ROWS, :] = acc[kk * ROWS : (kk + 1) * ROWS]
        T2[...] = jnp.transpose(Z[...])

    def forward_legendre():
        for t in range(4):
            parts = [R2[(4 * t + ii) * N : (4 * t + ii + 1) * N, :] for ii in range(4)]
            for ck in range(4):
                out = None
                for ii in range(4):
                    turn = ((ii - ck) * 32) % COLS
                    v = parts[ii] if turn == 0 else pltpu.roll(parts[ii], turn, 1)
                    out = v if out is None else jnp.where(lane16 // 32 == ii, v, out)
                hi, lo = split(out)
                AH[ck * N : (ck + 1) * N, t * COLS : (t + 1) * COLS] = hi
                AH[64 + ck * N : 64 + (ck + 1) * N, t * COLS : (t + 1) * COLS] = lo

        def one(d, carry):
            b = lax.rem(me_lon + d, N)
            here = pl.ds(pl.multiple_of(b * LMAX, LMAX), LMAX)
            r = dot_t(AH[...], Ph[here, :])
            r = r[0:64] + r[64:] + dot_t(AH[0:64], Pl[here, :])
            r = jnp.where(diagonal64, r, 0.0)
            out = []
            for ck in range(4):
                half = r[ck * N : ck * N + 8] + r[ck * N + 8 : ck * N + 16]
                total = jnp.sum(half, axis=0, keepdims=True)
                out += [total[:, 0:COLS], total[:, COLS:]]
            T3[pl.ds(pl.multiple_of(b * 8, 8), 8), :] = jnp.concatenate(out, axis=0)

            @pl.when(d < N)
            def _():
                exchange(2, "lon", slab(T3, b, 8), slab(R3, me_lon, 8), b, me_lon).start()

            return carry

        lax.fori_loop(1, N + 1, one, 0)
        mine = pl.ds(pl.multiple_of(me_lon * 8, 8), 8)
        R3[mine, :] = T3[mine, :]

    def expand_green():
        chosen = (iota((N, LMAX), 0) == iota((N, LMAX), 1) // N).astype(F32)
        out = lax.dot_general(
            GR[...], chosen, (((0,), (0,)), ((), ())), precision=lax.Precision.HIGHEST, preferred_element_type=F32
        )
        GX[0] = out[:, 0:COLS]
        GX[1] = out[:, COLS:]

    def layer_sum():
        for t in range(2):
            acc = [jnp.zeros((L, COLS), F32), jnp.zeros((L, COLS), F32)]
            for k in range(L):
                kk, j = k // N, k % N
                g = GX[t, pl.ds(k, L, stride=L), :]
                for c in range(2):
                    row = j * 8 + (2 * c + kk) * 2 + t
                    acc[c] = acc[c] + g * R3[row : row + 1, :]
            for c in range(2):
                for kk in range(2):
                    T4[pl.ds((2 * c + kk) * 2 + t, N, stride=8), :] = acc[c][kk * N : (kk + 1) * N]

    def inverse_legendre():
        x = R4[...]
        hi = x.astype(BF16).astype(F32)
        RH[...] = hi
        RL[...] = x - hi

        def one(step, acc):
            for part in range(4):
                b = step * 4 + part
                for ck in range(4):
                    for t in range(2):
                        row = pl.ds(b * 8 + ck * 2 + t, 1)
                        cols = slice(part * LMAX + t * COLS, part * LMAX + (t + 1) * COLS)
                        for base, ref in ((0, RH), (64, RL)):
                            v = jnp.where(diagonal16, ref[row, :], 0.0)
                            XH[base + ck * N : base + (ck + 1) * N, cols] = v.astype(BF16)
            here = pl.ds(pl.multiple_of(step * 4 * LMAX, LMAX), 4 * LMAX)
            r = dot(XH[...], Ph[here, :])
            return acc + (r[0:64] + r[64:] + dot(XH[0:64], Pl[here, :]))

        Y[...] = lax.fori_loop(0, 4, one, jnp.zeros((64, 512), F32))
        for i in range(N):
            t, ii = i // 4, i % 4
            out = None
            for ck in range(4):
                turn = ((ck - ii) * 32) % COLS
                v = Y[ck * N : (ck + 1) * N, t * COLS : (t + 1) * COLS]
                v = v if turn == 0 else pltpu.roll(v, turn, 1)
                out = v if out is None else jnp.where(lane16 // 32 == ck, v, out)
            T5[i * N : (i + 1) * N, :] = out

    lane8 = iota((8, COLS), 1)

    def inverse_fourier(final):
        X5[...] = jnp.transpose(R5[...])
        height = ROWS if final else 32
        rows = 2 * height
        size = rows if final else 72
        width = COLS if final else 2 * COLS

        def own(base):
            return jnp.concatenate([X5[base + kk * 32 : base + kk * 32 + height, :] for kk in range(2)], axis=0)

        def piece(p):
            return T6.at[p, pl.ds(0, size)], R6.at[me_lon, pl.ds(0, size)], R6.at[p, pl.ds(0, size)]

        def one(step, carry):
            ps = [lax.rem(me_lon + 1 + 2 * step + q, N) for q in range(2)]
            his, los = [], []
            a, b = own(0), own(64)
            for p in ps:
                c = C16[pl.ds(p, 1), :]
                s = S16[pl.ds(p, 1), :]
                hi, lo = split(jnp.concatenate([a * c + b * s, b * c - a * s], axis=1))
                his.append(hi)
                los.append(lo)
            r = dot(jnp.concatenate(his + los, axis=0), WH[:, 0:width])
            both = r[0 : 2 * rows] + r[2 * rows :] + dot(jnp.concatenate(his, axis=0), WL[:, 0:width])
            for q, p in enumerate(ps):
                r = both[q * rows : (q + 1) * rows]
                T6[p, 0:rows, :] = r[:, 0:COLS]
                if not final:
                    side = r[0:8, COLS:]
                    for t in range(1, 8):
                        v = pltpu.roll(r[8 * t : 8 * t + 8, COLS:], 8 * t, 1)
                        side = jnp.where(lane8 // 8 == t, v, side)
                    T6[p, 64:72, :] = side
                src, dst, _ = piece(p)
                if q == 0:
                    exchange(5, "lon", src, dst, p, me_lon).start()
                else:

                    @pl.when(step < N // 2 - 1)
                    def _():
                        exchange(5, "lon", src, dst, p, me_lon).start()

            return carry

        lax.fori_loop(0, N // 2, one, 0)
        R6[me_lon, 0:size] = T6[me_lon, 0:size]

        def wait(d, carry):
            p = lax.rem(me_lon + d, N)
            src, _, dst = piece(p)
            copy = exchange(5, "lon", src, dst, p, p)
            copy.wait_send()
            copy.wait_recv()
            return carry

        lax.fori_loop(1, N, wait, 0)

    def send_density():
        def one(q, carry):
            for kk in range(2):
                k = kk * N + q
                dens[q, kk] = rho[k] * U[0, k + 1, 0:ROWS, 0:COLS]
            return carry

        lax.fori_loop(0, N // 2, lambda h, c: one(2 * h + 1, one(2 * h, c)), 0)

        def start(d, carry):
            p = lax.rem(me_lon + d, N)
            exchange(0, "lon", dens.at[p], R1.at[me_lon], p, me_lon).start()
            return carry

        lax.fori_loop(1, N, start, 0)

    prepare()
    E[0] = pack(lambda k: u_in[k], 0)
    E[1] = pack(lambda k: u_in[k], 1)
    E[2] = pack(lambda k: matf[k], 0)
    E[3] = pack(lambda k: matf[k], 1)
    E[4] = pltpu.roll(load[...], 4, 1)
    tables()
    block, state = legendre_setup()
    state = lax.fori_loop(0, 2, block, state)
    pl.semaphore_wait(barrier, 2 * N - 1)
    edges = edge_copies(0)
    for copy in edges:
        copy.start()
    state = lax.fori_loop(2, 14, block, state)
    for copy in edges:
        copy.wait()
    merge_edges(0)
    pair_u(0)

    def pair_mat(k):
        pair_rows(17 + k, matf[k, 0:8], matf[k, 16:24], matf[k + 16, 0:8], matf[k + 16, 16:24])

    unrolled(16, 4, pair_mat)
    pair_rows(33, PK[2, 0:8], PK[2, 16:24], PK[3, 0:8], PK[3, 16:24])
    pair_rows(34, load[0:8], load[16:24], PK[4, 0:8], PK[4, 16:24])
    rows = row_copies(0)
    for copy in rows:
        copy.start()
    green = pltpu.make_async_remote_copy(
        green_in,
        GR,
        gsem.at[0],
        gsem.at[1],
        device_id={"lat": lax.rem(me_lon + N - 1, N), "lon": me_lat},
        device_id_type=MESH,
    )
    green.start()
    lax.fori_loop(14, 32, block, state)
    main_coefficients()
    for copy in rows:
        copy.wait()
    fill_u(0)
    margin_coefficients()

    for it in range(2):
        if it == 1:
            for copy in rows:
                copy.wait()
            fill_u(35)

            def force(j):
                side = R6[j, 64:72, :]
                for kk in range(2):
                    k = kk * N + j
                    main = R6[j, kk * 32 : (kk + 1) * 32, :]
                    halo = jnp.concatenate(
                        [pltpu.roll(side, 124 - 8 * (4 * kk + g), 1) for g in range(4)], axis=0
                    )
                    Ac[k] = jnp.concatenate([main, halo], axis=1) * Rd[k]

            unrolled(N, 2, force)
            Ac[0] = Ac[0] + loadx[...] * Rd[0]
        for s in range(SWEEPS):
            sweep(s % 2, (s + 1) % 2, s == SWEEPS - 1)
        send_density()
        if it == 0:
            E[5] = pack(lambda k: U[0, k + 1, 0:ROWS, 0:COLS], 0)
            E[6] = pack(lambda k: U[0, k + 1, 0:ROWS, 0:COLS], 1)
        else:

            def store_u(k):
                u_out[k] = U[0, k + 1, 0:ROWS, 0:COLS]

            unrolled(L, 4, store_u)
        forward_fourier()
        swap_start(1, "lat", me_lat, T2, R2, N)
        if it == 0:
            edges = edge_copies(1)
            for copy in edges:
                copy.start()
            green.wait()
            expand_green()
        swap_wait(1, "lat", me_lat, T2, R2, N)
        forward_legendre()
        if it == 0:
            for copy in edges:
                copy.wait()
            merge_edges(1)
            pair_u(35)
            rows = row_copies(1)
            for copy in rows:
                copy.start()
        swap_wait(2, "lon", me_lon, T3, R3, 8)
        layer_sum()
        swap_start(3, "lon", me_lon, T4, R4, 8)
        swap_wait(3, "lon", me_lon, T4, R4, 8)
        inverse_legendre()
        swap_start(4, "lat", me_lat, T5, R5, N)
        swap_wait(4, "lat", me_lat, T5, R5, N)
        inverse_fourier(it == 1)

    def store_pot(j):
        for kk in range(2):
            pot_out[kk * N + j] = R6[j, kk * ROWS : (kk + 1) * ROWS, :]

    unrolled(N, 4, store_pot)


def on_device(displacement, materials, ice_mask, ice_height, shear, restoring, contrast, green):
    vmem = pl.BlockSpec(memory_space=pltpu.VMEM)
    smem = pl.BlockSpec(memory_space=pltpu.SMEM)
    field = jax.ShapeDtypeStruct((L, ROWS, COLS), F32)
    scratch = [
        ((2, L + 2, 32, 256), F32),
        ((L, 32, 256), F32),
        ((L, 32, 256), F32),
        ((L, 32, 256), F32),
        ((L, ROWS, COLS), F32),
        ((N, 2, ROWS, COLS), F32),
        ((N, 2, ROWS, COLS), F32),
        ((COLS, 512), BF16),
        ((COLS, 512), BF16),
        ((512, 256), BF16),
        ((512, 256), BF16),
        ((N, LMAX), F32),
        ((N, LMAX), F32),
        ((2 * ROWS, LMAX), F32),
        ((128, LMAX), F32),
        ((LMAX, COLS), F32),
        ((LMAX, COLS), F32),
        ((128, 512), BF16),
        ((8 * N, COLS), F32),
        ((8 * N, COLS), F32),
        ((8 * N, COLS), F32),
        ((8 * N, COLS), F32),
        ((8 * N, COLS), F32),
        ((8 * N, COLS), F32),
        ((128, 4 * LMAX), BF16),
        ((64, 512), F32),
        ((LMAX, COLS), F32),
        ((LMAX, COLS), F32),
        ((128, LMAX), F32),
        ((N, 72, COLS), F32),
        ((N, 72, COLS), F32),
        ((N, L * L), F32),
        ((2, L * L, COLS), F32),
        ((N * LMAX, 512), BF16),
        ((N * LMAX, 512), BF16),
        ((L, ROWS, COLS), F32),
        ((ROWS, COLS), F32),
        ((32, 256), F32),
        ((7, ROWS, COLS), F32),
        ((7, ROWS, COLS), F32),
        ((7, ROWS, COLS), F32),
        ((5, 32, COLS), F32),
        ((52, 8, COLS), F32),
        ((52, 8, COLS), F32),
        ((52, 8, COLS), F32),
        ((52, 8, COLS), F32),
    ]
    return pl.pallas_call(
        kernel,
        out_shape=(field, field),
        in_specs=[vmem] * 4 + [smem] * 3 + [vmem],
        out_specs=(vmem, vmem),
        scratch_shapes=[pltpu.VMEM(shape, dtype) for shape, dtype in scratch]
        + [
            pltpu.SemaphoreType.DMA((6, N)),
            pltpu.SemaphoreType.DMA((6, N)),
            pltpu.SemaphoreType.DMA((2, 4)),
            pltpu.SemaphoreType.DMA((2, 4)),
            pltpu.SemaphoreType.DMA((2,)),
        ],
        compiler_params=pltpu.CompilerParams(
            collective_id=0, has_side_effects=True, vmem_limit_bytes=60 * 1024 * 1024
        ),
    )(displacement, materials, ice_mask, ice_height, shear, restoring, contrast, green.reshape(N, L * L))


def solution(mesh):
    in_specs = (
        P(None, "lat", "lon"),
        P(None, "lat", "lon"),
        P("lat", "lon"),
        P("lat", "lon"),
        P(),
        P(),
        P(),
        P("lat", None, None),
    )
    out_specs = (P(None, "lat", "lon"), P(None, "lat", "lon"))
    return jax.shard_map(
        on_device, mesh=mesh, in_specs=in_specs, out_specs=out_specs, check_vma=False
    )
```

```python
import functools
import math

import jax
import jax.numpy as jnp
from jax import lax
from jax.experimental import pallas as pl
from jax.experimental.pallas import tpu as pltpu
from jax.sharding import PartitionSpec as P

L = 32
LMAX = 256
NLAT = 384
NLON = 2048
SWEEPS = 4
N = 16
ROWS = 24
COLS = 128
F32 = jnp.float32
BF16 = jnp.bfloat16
MESH = pl.DeviceIdType.MESH


def iota(shape, dim):
    return lax.broadcasted_iota(jnp.int32, shape, dim)


def split(x):
    hi = x.astype(BF16)
    lo = (x - hi.astype(F32)).astype(BF16)
    return hi, lo


def dot(a, b):
    return jnp.dot(a, b, preferred_element_type=F32)


def dot_t(a, b):
    return lax.dot_general(a, b, (((1,), (1,)), ((), ())), preferred_element_type=F32)


def unrolled(total, factor, one):
    def body(step, carry):
        for part in range(factor):
            one(step * factor + part)
        return carry

    lax.fori_loop(0, total // factor, body, 0)


def lookup(mat, table):
    out = jnp.where(mat == 0, table[0], 0.0)
    for material in range(1, 4):
        out = jnp.where(mat == material, table[material], out)
    return out


def kernel(
    u_in,
    mat_in,
    mask_in,
    ice_in,
    shear,
    restoring,
    contrast,
    green_in,
    u_out,
    pot_out,
    U,
    Bc,
    Rd,
    Ac,
    rho,
    dens,
    R1,
    FH,
    FL,
    WH,
    WL,
    C16,
    S16,
    wrow,
    Z,
    T2,
    R2,
    AH,
    Qh,
    Ql,
    T3,
    R3,
    T4,
    R4,
    RH,
    RL,
    XH,
    T5,
    R5,
    X5,
    T6,
    R6,
    mats,
    masks,
    ice,
    GA,
    GP,
    GQ,
    GR,
    GX,
    Ph,
    Pl,
    matf,
    load,
    loadx,
    E,
    EL,
    ER,
    PK,
    VT,
    VB,
    WT,
    WB,
    send_sem,
    recv_sem,
    hsend,
    hrecv,
    gsem,
    insem,
    outsem,
):
    me_lat = lax.axis_index("lat")
    me_lon = lax.axis_index("lon")

    barrier = pltpu.get_barrier_semaphore()

    def greet(d, carry):
        pl.semaphore_signal(barrier, inc=1, device_id={"lon": lax.rem(me_lon + d, N)}, device_id_type=MESH)
        pl.semaphore_signal(barrier, inc=1, device_id={"lat": lax.rem(me_lat + d, N)}, device_id_type=MESH)
        return carry

    lax.fori_loop(1, N, greet, 0)
    pl.semaphore_signal(
        barrier, inc=1, device_id={"lat": me_lon, "lon": lax.rem(me_lat + 1, N)}, device_id_type=MESH
    )

    main = U.at[0, pl.ds(1, L), pl.ds(0, ROWS), pl.ds(0, COLS)]
    loads = [
        pltpu.make_async_copy(mat_in, mats, insem.at[0]),
        pltpu.make_async_copy(u_in, main, insem.at[1]),
        pltpu.make_async_copy(mask_in, masks, insem.at[2]),
        pltpu.make_async_copy(ice_in, ice, insem.at[3]),
        pltpu.make_async_copy(green_in, GA, insem.at[4]),
    ]
    for copy in loads:
        copy.start()

    def tables():
        q = iota((COLS, LMAX), 0)
        m = iota((COLS, LMAX), 1)
        angle = (2.0 * math.pi / NLON) * ((q * m) & (NLON - 1)).astype(F32)
        hi, lo = split(jnp.cos(angle))
        FH[:, 0:LMAX] = hi
        FL[:, 0:LMAX] = lo
        hi, lo = split(jnp.sin(angle))
        FH[:, LMAX:] = hi
        FL[:, LMAX:] = lo
        p = iota((N, LMAX), 0)
        m = iota((N, LMAX), 1)
        angle = (2.0 * math.pi / N) * ((p * m) & (N - 1)).astype(F32)
        C16[...] = jnp.cos(angle)
        S16[...] = jnp.sin(angle)
        lane = iota((LMAX, 2 * COLS), 1)
        m = iota((LMAX, 2 * COLS), 0)
        q = jnp.where(lane < 128, lane, jnp.where(lane < 132, lane - 132 + NLON, lane - 4))
        angle = (2.0 * math.pi / NLON) * ((q * m) & (NLON - 1)).astype(F32)
        hi, lo = split(jnp.cos(angle))
        WH[0:LMAX, :] = hi
        WL[0:LMAX, :] = lo
        hi, lo = split(jnp.sin(angle))
        WH[LMAX:, :] = hi
        WL[LMAX:, :] = lo
        row = iota((ROWS, LMAX), 0) + me_lat * ROWS
        w = jnp.sin((row.astype(F32) + 0.5) * (math.pi / NLAT)) * (2.0 * math.pi / NLON / (4.0 * NLAT))
        wrow[0:ROWS, :] = w
        wrow[ROWS:, :] = w
        Z[...] = jnp.zeros_like(Z)
        for b in range(2):
            U[b, 0] = jnp.zeros((32, 256), F32)
            U[b, L + 1] = jnp.zeros((32, 256), F32)

    def prepare():
        def one(k):
            mat = mats[k]
            matf[k] = mat.astype(F32)
            rho[k] = lookup(mat, contrast)

        unrolled(L, 4, one)
        load[...] = masks[...].astype(F32) * ice[...]

    lane24 = iota((ROWS, COLS), 1)

    def pack(read, g):
        acc = jnp.zeros((ROWS, COLS), F32)
        for kk in range(16):
            acc = jnp.where(lane24 // 8 == kk, pltpu.roll(read(16 * g + kk), (8 * kk + 4) % COLS, 1), acc)
        return acc

    left = lax.rem(me_lon + N - 1, N)
    right = lax.rem(me_lon + 1, N)
    up = lax.rem(me_lat + N - 1, N)
    down = lax.rem(me_lat + 1, N)

    def edge_copies(it):
        first, count = (0, 5) if it == 0 else (5, 2)
        part = pl.ds(first, count)
        return [
            pltpu.make_async_remote_copy(
                E.at[part], ER.at[part], hsend.at[it, 0], hrecv.at[it, 0], device_id={"lon": left}, device_id_type=MESH
            ),
            pltpu.make_async_remote_copy(
                E.at[part], EL.at[part], hsend.at[it, 1], hrecv.at[it, 1], device_id={"lon": right}, device_id_type=MESH
            ),
        ]

    def row_copies(it, corners):
        if it == 0:
            first, count = (33, 3) if corners else (0, 33)
        else:
            first, count = (36, 17)
        part = pl.ds(first, count)
        one = 4 if corners else 2
        return [
            pltpu.make_async_remote_copy(
                VT.at[part],
                WT.at[part],
                hsend.at[it, one],
                hrecv.at[it, one],
                device_id={"lat": up},
                device_id_type=MESH,
            ),
            pltpu.make_async_remote_copy(
                VB.at[part],
                WB.at[part],
                hsend.at[it, one + 1],
                hrecv.at[it, one + 1],
                device_id={"lat": down},
                device_id_type=MESH,
            ),
        ]

    def merge_edges(it):
        first, count = (0, 5) if it == 0 else (5, 2)
        for g in range(count):
            PK[g, 0:ROWS] = jnp.where(lane24 % 8 < 4, EL[first + g], ER[first + g])

    row8 = iota((8, COLS), 0)

    def pair_rows(t, a_top, a_bot, b_top, b_bot):
        VT[t] = jnp.where(row8 < 4, a_top, pltpu.roll(b_top, 4, 0))
        VB[t] = jnp.where(row8 < 4, pltpu.roll(a_bot, 4, 0), b_bot)

    def halo_rows(t):
        top, bot = WT[t], WB[t]
        first = jnp.where(row8 < 4, top, pltpu.roll(bot, 4, 0))
        second = jnp.where(row8 < 4, pltpu.roll(top, 4, 0), bot)
        return first, second

    rows32 = iota((32, 256), 0)
    global_row = me_lat * ROWS + jnp.where(rows32 < 28, rows32, rows32 - 32)
    inside = (global_row >= 0) & (global_row < NLAT)
    inside8 = inside[24:32, 0:COLS]

    def pair_u(base):
        def one(k):
            pair_rows(
                base + k,
                U[0, k + 1, 0:8, 0:COLS],
                U[0, k + 1, 16:24, 0:COLS],
                U[0, k + 17, 0:8, 0:COLS],
                U[0, k + 17, 16:24, 0:COLS],
            )

        unrolled(16, 4, one)

    def pair_packed(t, g):
        pair_rows(t, PK[g, 0:8], PK[g, 16:24], PK[g + 1, 0:8], PK[g + 1, 16:24])

    def fill_u(base, packed):
        first, second = halo_rows(packed)
        PK[0, 24:32] = jnp.where(inside8, first, 0.0)
        PK[1, 24:32] = jnp.where(inside8, second, 0.0)

        def one(k):
            first, second = halo_rows(base + k)
            U[0, k + 1, 24:32, 0:COLS] = jnp.where(inside8, first, 0.0)
            U[0, k + 17, 24:32, 0:COLS] = jnp.where(inside8, second, 0.0)
            U[0, k + 1, :, COLS:] = pltpu.roll(PK[0], 124 - 8 * k, 1)
            U[0, k + 17, :, COLS:] = pltpu.roll(PK[1], 124 - 8 * k, 1)

        unrolled(16, 4, one)

    def legendre_setup():
        lane = iota((N, 512), 1)
        order = (iota((N, 512), 0) + me_lat * N).astype(F32)
        aa = lane % 32
        a = (lane // 32) * ROWS + jnp.where(aa < 28, aa, aa - 32)
        a = jnp.clip(a, 0, NLAT - 1)
        theta = (a.astype(F32) + 0.5) * (math.pi / NLAT)
        cosine = jnp.cos(theta)
        sine = jnp.sin(theta)
        t = iota((N, LMAX), 1)
        m_int = iota((N, LMAX), 0) + me_lat * N
        t_f = jnp.maximum(t.astype(F32), 1.0)
        growth = jnp.where((t >= 2) & (t <= m_int), 0.5 * jnp.log((2.0 * t_f + 1.0) / (2.0 * t_f)), 0.0)
        log_diag = jnp.sum(growth, axis=1, keepdims=True) + 0.5 * math.log(3.0)
        log_diag = jnp.where(m_int[:, 0:1] >= 1, log_diag, 0.0)
        diagonal = jnp.exp(log_diag + order * jnp.log(sine))
        start = jnp.sqrt(2.0 * order + 3.0) * cosine * diagonal
        deg = iota((N, LMAX), 1).astype(F32)
        m_f = m_int.astype(F32)
        first = jnp.sqrt(
            jnp.maximum(4.0 * deg * deg - 1.0, 1.0) / jnp.maximum(deg * deg - m_f * m_f, 1.0)
        )
        second = jnp.sqrt(
            jnp.maximum((deg - 1.0) * (deg - 1.0) - m_f * m_f, 0.0)
            / jnp.maximum(4.0 * (deg - 1.0) * (deg - 1.0) - 1.0, 1.0)
        )
        order_i = iota((N, 512), 0) + me_lat * N

        def block(lb, carry):
            one, two = carry
            shift = lax.rem(LMAX - 8 * lb, LMAX)
            f = pltpu.roll(first, shift, 1)[:, 0:COLS]
            s = pltpu.roll(second, shift, 1)[:, 0:COLS]
            for r in range(8):
                degree = lb * 8 + r
                fb = jnp.broadcast_to(f[:, r : r + 1], (N, 512))
                sb = jnp.broadcast_to(s[:, r : r + 1], (N, 512))
                general = fb * (cosine * one - sb * two)
                value = jnp.where(
                    order_i == degree, diagonal, jnp.where(order_i == degree - 1, start, general)
                )
                hi, lo = split(value)
                here = pl.ds(pl.multiple_of(degree * N, N), N)
                Ph[here, :] = hi
                Pl[here, :] = lo
                one, two = value, one
            return one, two

        zeros = jnp.zeros((N, 512), F32)
        return block, (zeros, zeros)

    def exchange(phase, axis, src, dst, peer, sender):
        return pltpu.make_async_remote_copy(
            src,
            dst,
            send_sem.at[phase, peer],
            recv_sem.at[phase, sender],
            device_id={axis: peer},
            device_id_type=MESH,
        )

    def slab(ref, index, size):
        return ref.at[pl.ds(pl.multiple_of(index * size, size), size)]

    def far_first(d):
        return lax.rem(d + 6, N - 1) + 1

    def swap_start(phase, axis, me, src, dst, size):
        def one(d, carry):
            peer = lax.rem(me + far_first(d), N)
            exchange(phase, axis, slab(src, peer, size), slab(dst, me, size), peer, me).start()
            return carry

        lax.fori_loop(1, N, one, 0)
        mine = pl.ds(pl.multiple_of(me * size, size), size)
        dst[mine, :] = src[mine, :]

    def swap_wait(phase, axis, me, src, dst, size):
        def one(d, carry):
            peer = lax.rem(me + d, N)
            copy = exchange(phase, axis, slab(src, peer, size), slab(dst, peer, size), peer, peer)
            copy.wait_send()
            copy.wait_recv()
            return carry

        lax.fori_loop(1, N, one, 0)

    lane32 = iota((32, COLS), 1)

    def sweep(src, dst, last):
        rows = ROWS if last else 32

        def one(k):
            t0 = U[src, k + 1, :, 0:COLS]
            t1 = U[src, k + 1, :, COLS:]
            r0, r1 = pltpu.roll(t0[0:rows], 1, 1), pltpu.roll(t1[0:rows], 1, 1)
            l0, l1 = pltpu.roll(t0[0:rows], COLS - 1, 1), pltpu.roll(t1[0:rows], COLS - 1, 1)
            first = lane32[0:rows] == 0
            final = lane32[0:rows] == COLS - 1
            around = (
                (jnp.where(first, r1, r0) + jnp.where(final, l1, l0))
                + (pltpu.roll(t0, 1, 0) + pltpu.roll(t0, 31, 0))[0:rows]
                + (U[src, k, 0:rows, 0:COLS] + U[src, k + 2, 0:rows, 0:COLS])
            )
            U[dst, k + 1, 0:rows, 0:COLS] = Ac[k, 0:rows, 0:COLS] + Bc[k, 0:rows, 0:COLS] * around
            if not last:
                around = (
                    (jnp.where(first, r0, r1) + jnp.where(final, l0, l1))
                    + (pltpu.roll(t1, 1, 0) + pltpu.roll(t1, 31, 0))
                    + (U[src, k, :, COLS:] + U[src, k + 2, :, COLS:])
                )
                U[dst, k + 1, :, COLS:] = Ac[k, :, COLS:] + Bc[k, :, COLS:] * around

        unrolled(L, 4, one)

    def coefficient(k, rows, cols, mat, valid):
        st = lookup(mat, shear)
        re = lookup(mat, restoring)
        inv = 1.0 / (6.0 * st + re)
        if valid is not None:
            inv = jnp.where(valid, inv, 0.0)
        Rd[k, rows, cols] = inv
        Bc[k, rows, cols] = st * inv
        Ac[k, rows, cols] = jnp.zeros(inv.shape, F32)

    def main_coefficients():
        unrolled(L, 4, lambda k: coefficient(k, slice(0, ROWS), slice(0, COLS), matf[k], None))

    inside_side = inside[:, 0:COLS]

    def margin_coefficients():
        first, second = halo_rows(34)
        PK[2, 24:32] = first
        PK[3, 24:32] = second

        def one(k):
            first, second = halo_rows(16 + k)
            coefficient(k, slice(ROWS, 32), slice(0, COLS), first, inside8)
            coefficient(k + 16, slice(ROWS, 32), slice(0, COLS), second, inside8)
            for g in range(2):
                side = pltpu.roll(PK[2 + g], 124 - 8 * k, 1)
                coefficient(k + 16 * g, slice(0, 32), slice(COLS, 2 * COLS), side, inside_side)

        unrolled(16, 2, one)
        PK[4, 24:32] = halo_rows(35)[0]
        loadx[0:ROWS, 0:COLS] = load[...]
        loadx[ROWS:, 0:COLS] = halo_rows(32)[0]
        loadx[:, COLS:] = pltpu.roll(PK[4], 124, 1)
        Ac[0] = loadx[...] * Rd[0]

    lane16 = iota((N, COLS), 1)
    diagonal64 = iota((64, LMAX), 0) % N == iota((64, LMAX), 1) % N
    diagonal16 = iota((N, COLS), 0) == iota((N, COLS), 1) % N

    def forward_fourier():
        def pair(step, acc):
            acc_c, acc_s = acc
            ps = [lax.rem(me_lon + 2 * step + q, N) for q in range(2)]
            his, los = zip(*[split(R1[p].reshape(2 * ROWS, COLS)) for p in ps])
            r = dot(jnp.concatenate(his + los, axis=0), FH[...])
            r = r[0 : 4 * ROWS] + r[4 * ROWS :] + dot(jnp.concatenate(his, axis=0), FL[...])
            for q, p in enumerate(ps):
                yc = r[2 * ROWS * q : 2 * ROWS * (q + 1), 0:LMAX]
                ys = r[2 * ROWS * q : 2 * ROWS * (q + 1), LMAX:]
                c = C16[pl.ds(p, 1), :]
                s = S16[pl.ds(p, 1), :]
                acc_c, acc_s = acc_c + (c * yc - s * ys), acc_s + (s * yc + c * ys)
            return acc_c, acc_s

        def wait(d):
            p = lax.rem(me_lon + d, N)
            copy = exchange(0, "lon", dens.at[p], R1.at[p], p, p)
            copy.wait_send()
            copy.wait_recv()

        def one(step, acc):
            wait(2 * step)
            wait(2 * step + 1)
            return pair(step, acc)

        zeros = jnp.zeros((2 * ROWS, LMAX), F32)
        R1[me_lon] = dens[me_lon]
        wait(1)
        acc_c, acc_s = lax.fori_loop(1, N // 2, one, pair(0, (zeros, zeros)))
        for c, acc in ((0, acc_c), (1, acc_s)):
            acc = acc * wrow[...]
            for kk in range(2):
                Z[(2 * c + kk) * 32 : (2 * c + kk) * 32 + ROWS, :] = acc[kk * ROWS : (kk + 1) * ROWS]
        T2[...] = jnp.transpose(Z[...])

    def transpose_legendre():
        def one(b):
            here = pl.ds(pl.multiple_of(b * LMAX, LMAX), LMAX)
            for src, dst in ((Ph, Qh), (Pl, Ql)):
                dst[b] = jnp.transpose(src[here, :])

        unrolled(N, 1, one)

    def forward_legendre():
        for t in range(4):
            parts = [R2[(4 * t + ii) * N : (4 * t + ii + 1) * N, :] for ii in range(4)]
            for ck in range(4):
                out = None
                for ii in range(4):
                    turn = ((ii - ck) * 32) % COLS
                    v = parts[ii] if turn == 0 else pltpu.roll(parts[ii], turn, 1)
                    out = v if out is None else jnp.where(lane16 // 32 == ii, v, out)
                hi, lo = split(out)
                AH[ck * N : (ck + 1) * N, t * COLS : (t + 1) * COLS] = hi
                AH[64 + ck * N : 64 + (ck + 1) * N, t * COLS : (t + 1) * COLS] = lo

        def product(b):
            r = dot(AH[...], Qh[b])
            return r[0:64] + r[64:] + dot(AH[0:64], Ql[b])

        def one(step, carry):
            bs = [lax.rem(me_lon + 1 + 4 * step + q, N) for q in range(4)]
            products = [product(b) for b in bs]
            for q, (b, r) in enumerate(zip(bs, products)):
                r = jnp.where(diagonal64, r, 0.0)
                totals = [
                    jnp.sum(r[ck * N : ck * N + 8] + r[ck * N + 8 : ck * N + 16], axis=0, keepdims=True)
                    for ck in range(4)
                ]
                out = [v[:, t * COLS : (t + 1) * COLS] for t in range(2) for v in totals]
                T3[pl.ds(pl.multiple_of(b * 8, 8), 8), :] = jnp.concatenate(out, axis=0)
                copy = exchange(2, "lon", slab(T3, b, 8), slab(R3, me_lon, 8), b, me_lon)
                if q < 3:
                    copy.start()
                else:
                    pl.when(step < 3)(copy.start)
            return carry

        lax.fori_loop(0, 4, one, 0)
        mine = pl.ds(pl.multiple_of(me_lon * 8, 8), 8)
        R3[mine, :] = T3[mine, :]

    def expand_green():
        chosen = (iota((N, LMAX), 0) == iota((N, LMAX), 1) // N).astype(F32)
        for g in range(4):
            for q in range(4):
                GR[4 * g + q] = GQ[g, :, q * L : (q + 1) * L]
        for k in range(L):
            out = lax.dot_general(
                GR[:, k, :],
                chosen,
                (((0,), (0,)), ((), ())),
                precision=lax.Precision.HIGHEST,
                preferred_element_type=F32,
            )
            GX[0, k * L : (k + 1) * L, :] = out[:, 0:COLS]
            GX[1, k * L : (k + 1) * L, :] = out[:, COLS:]

    def layer_sum():
        for t in range(2):
            acc = [jnp.zeros((L, COLS), F32), jnp.zeros((L, COLS), F32)]
            for k in range(L):
                kk, j = k // N, k % N
                g = GX[t, pl.ds(k, L, stride=L), :]
                for c in range(2):
                    row = j * 8 + t * 4 + 2 * c + kk
                    acc[c] = acc[c] + g * R3[row : row + 1, :]
            for c in range(2):
                for kk in range(2):
                    T4[pl.ds(t * 4 + 2 * c + kk, N, stride=8), :] = acc[c][kk * N : (kk + 1) * N]

    def inverse_legendre():
        x = R4[...]
        hi = x.astype(BF16).astype(F32)
        RH[...] = hi
        RL[...] = x - hi

        def build(b):
            for ck in range(4):
                for t in range(2):
                    row = pl.ds(b * 8 + t * 4 + ck, 1)
                    cols = pl.ds(pl.multiple_of(b * LMAX + t * COLS, COLS), COLS)
                    for base, ref in ((0, RH), (64, RL)):
                        v = jnp.where(diagonal16, ref[row, :], 0.0)
                        XH[base + ck * N : base + (ck + 1) * N, cols] = v.astype(BF16)

        unrolled(N, 2, build)

        def half(chunk):
            lanes = pl.ds(pl.multiple_of(chunk * 2 * COLS, 2 * COLS), 2 * COLS)

            def one(step, acc):
                here = pl.ds(pl.multiple_of(step * 4 * LMAX, 4 * LMAX), 4 * LMAX)
                r = dot(XH[:, here], Ph[here, lanes])
                return acc + (r[0:64] + r[64:] + dot(XH[0:64, here], Pl[here, lanes]))

            y = lax.fori_loop(0, 4, one, jnp.zeros((64, 2 * COLS), F32))
            for i8 in range(8):
                t, ii = i8 // 4, i8 % 4
                out = None
                for ck in range(4):
                    turn = ((ck - ii) * 32) % COLS
                    v = y[ck * N : (ck + 1) * N, t * COLS : (t + 1) * COLS]
                    v = v if turn == 0 else pltpu.roll(v, turn, 1)
                    out = v if out is None else jnp.where(lane16 // 32 == ck, v, out)
                i = chunk * 8 + i8
                T5[pl.ds(pl.multiple_of(i * N, N), N), :] = out

                @pl.when(i != me_lat)
                def _():
                    exchange(4, "lat", slab(T5, i, N), slab(R5, me_lat, N), i, me_lat).start()

        near = me_lat // 8
        half(1 - near)
        half(near)
        mine = pl.ds(pl.multiple_of(me_lat * N, N), N)
        R5[mine, :] = T5[mine, :]

    lane8 = iota((8, COLS), 1)

    def pot_copy(j, kk):
        return pltpu.make_async_copy(
            R6.at[j, pl.ds(kk * ROWS, ROWS)], pot_out.at[kk * N + j], outsem.at[2 * j + kk]
        )

    def inverse_fourier(final):
        X5[...] = jnp.transpose(R5[...])
        height = ROWS if final else 32
        rows = 2 * height
        size = rows if final else 72
        width = COLS if final else 2 * COLS

        def own(base):
            return jnp.concatenate([X5[base + kk * 32 : base + kk * 32 + height, :] for kk in range(2)], axis=0)

        def piece(p):
            return T6.at[p, pl.ds(0, size)], R6.at[me_lon, pl.ds(0, size)], R6.at[p, pl.ds(0, size)]

        def one(step, carry):
            first = far_first(2 * step + 1)
            second = jnp.where(step == N // 2 - 1, 0, far_first(2 * step + 2))
            ps = [lax.rem(me_lon + first, N), lax.rem(me_lon + second, N)]
            his, los = [], []
            a, b = own(0), own(64)
            for p in ps:
                c = C16[pl.ds(p, 1), :]
                s = S16[pl.ds(p, 1), :]
                hi, lo = split(jnp.concatenate([a * c + b * s, b * c - a * s], axis=1))
                his.append(hi)
                los.append(lo)
            r = dot(jnp.concatenate(his + los, axis=0), WH[:, 0:width])
            both = r[0 : 2 * rows] + r[2 * rows :] + dot(jnp.concatenate(his, axis=0), WL[:, 0:width])
            for q, p in enumerate(ps):
                r = both[q * rows : (q + 1) * rows]
                T6[p, 0:rows, :] = r[:, 0:COLS]
                if not final:
                    side = r[0:8, COLS:]
                    for t in range(1, 8):
                        v = pltpu.roll(r[8 * t : 8 * t + 8, COLS:], 8 * t, 1)
                        side = jnp.where(lane8 // 8 == t, v, side)
                    T6[p, 64:72, :] = side
                src, dst, _ = piece(p)
                if q == 0:
                    exchange(5, "lon", src, dst, p, me_lon).start()
                else:

                    @pl.when(step < N // 2 - 1)
                    def _():
                        exchange(5, "lon", src, dst, p, me_lon).start()

            return carry

        lax.fori_loop(0, N // 2, one, 0)
        R6[me_lon, 0:size] = T6[me_lon, 0:size]
        if final:
            for kk in range(2):
                pot_copy(me_lon, kk).start()

        def wait(d, carry):
            p = lax.rem(me_lon + d, N)
            src, _, dst = piece(p)
            copy = exchange(5, "lon", src, dst, p, p)
            copy.wait_send()
            copy.wait_recv()
            if final:
                for kk in range(2):
                    pot_copy(p, kk).start()
            return carry

        lax.fori_loop(1, N, wait, 0)

    def send_density():
        def one(q, carry):
            for kk in range(2):
                k = kk * N + q
                dens[q, kk] = rho[k] * U[0, k + 1, 0:ROWS, 0:COLS]
            return carry

        lax.fori_loop(0, N // 2, lambda h, c: one(2 * h + 1, one(2 * h, c)), 0)

        def start(d, carry):
            p = lax.rem(me_lon + far_first(d), N)
            exchange(0, "lon", dens.at[p], R1.at[me_lon], p, me_lon).start()
            return carry

        lax.fori_loop(1, N, start, 0)

    for copy in loads:
        copy.wait()
    prepare()
    E[0] = pack(lambda k: U[0, k + 1, 0:ROWS, 0:COLS], 0)
    E[1] = pack(lambda k: U[0, k + 1, 0:ROWS, 0:COLS], 1)
    E[2] = pack(lambda k: matf[k], 0)
    E[3] = pack(lambda k: matf[k], 1)
    E[4] = pltpu.roll(load[...], 4, 1)
    pair_u(0)

    def pair_mat(k):
        pair_rows(16 + k, matf[k, 0:8], matf[k, 16:24], matf[k + 16, 0:8], matf[k + 16, 16:24])

    unrolled(16, 4, pair_mat)
    pair_rows(32, load[0:8], load[16:24], load[0:8], load[16:24])
    for g in range(4):
        GP[g] = jnp.concatenate([GA[4 * g + q] for q in range(4)], axis=1)
    tables()
    block, state = legendre_setup()
    state = lax.fori_loop(0, 2, block, state)
    pl.semaphore_wait(barrier, 2 * N - 1)
    edges = edge_copies(0)
    rows = row_copies(0, False)
    for copy in edges + rows:
        copy.start()
    state = lax.fori_loop(2, 12, block, state)
    for copy in edges:
        copy.wait()
    merge_edges(0)
    pair_packed(33, 0)
    pair_packed(34, 2)
    pair_rows(35, PK[4, 0:8], PK[4, 16:24], PK[4, 0:8], PK[4, 16:24])
    corners = row_copies(0, True)
    for copy in corners:
        copy.start()
    lax.fori_loop(12, 32, block, state)
    main_coefficients()
    for copy in rows + corners:
        copy.wait()
    green = pltpu.make_async_remote_copy(
        GP,
        GQ,
        gsem.at[0],
        gsem.at[1],
        device_id={"lat": lax.rem(me_lon + N - 1, N), "lon": me_lat},
        device_id_type=MESH,
    )
    green.start()
    fill_u(0, 33)
    margin_coefficients()

    for it in range(2):
        if it == 1:
            for copy in rows:
                copy.wait()
            fill_u(36, 52)

            def force(j):
                side = R6[j, 64:72, :]
                for kk in range(2):
                    k = kk * N + j
                    main = R6[j, kk * 32 : (kk + 1) * 32, :]
                    halo = jnp.concatenate(
                        [pltpu.roll(side, 124 - 8 * (4 * kk + g), 1) for g in range(4)], axis=0
                    )
                    Ac[k] = jnp.concatenate([main, halo], axis=1) * Rd[k]

            unrolled(N, 2, force)
            Ac[0] = Ac[0] + loadx[...] * Rd[0]
        for s in range(SWEEPS):
            sweep(s % 2, (s + 1) % 2, s == SWEEPS - 1)
        send_density()
        if it == 0:
            E[5] = pack(lambda k: U[0, k + 1, 0:ROWS, 0:COLS], 0)
            E[6] = pack(lambda k: U[0, k + 1, 0:ROWS, 0:COLS], 1)
        else:
            u_copy = pltpu.make_async_copy(main, u_out, outsem.at[2 * N])
            u_copy.start()
        forward_fourier()
        swap_start(1, "lat", me_lat, T2, R2, N)
        if it == 0:
            edges = edge_copies(1)
            for copy in edges:
                copy.start()
            transpose_legendre()
        swap_wait(1, "lat", me_lat, T2, R2, N)
        forward_legendre()
        if it == 0:
            for copy in edges:
                copy.wait()
            merge_edges(1)
            pair_u(36)
            pair_packed(52, 0)
            rows = row_copies(1, False)
            for copy in rows:
                copy.start()
            green.wait()
            expand_green()
        swap_wait(2, "lon", me_lon, T3, R3, 8)
        layer_sum()
        swap_start(3, "lon", me_lon, T4, R4, 8)
        swap_wait(3, "lon", me_lon, T4, R4, 8)
        inverse_legendre()
        swap_wait(4, "lat", me_lat, T5, R5, N)
        inverse_fourier(it == 1)

    def finish(j):
        for kk in range(2):
            pot_copy(j, kk).wait()

    unrolled(N, 4, finish)
    u_copy.wait()


def on_device(displacement, materials, ice_mask, ice_height, shear, restoring, contrast, green):
    hbm = pl.BlockSpec(memory_space=pl.ANY)
    smem = pl.BlockSpec(memory_space=pltpu.SMEM)
    field = jax.ShapeDtypeStruct((L, ROWS, COLS), F32)
    scratch = [
        ((2, L + 2, 32, 256), F32),
        ((L, 32, 256), F32),
        ((L, 32, 256), F32),
        ((L, 32, 256), F32),
        ((L, ROWS, COLS), F32),
        ((N, 2, ROWS, COLS), F32),
        ((N, 2, ROWS, COLS), F32),
        ((COLS, 512), BF16),
        ((COLS, 512), BF16),
        ((512, 256), BF16),
        ((512, 256), BF16),
        ((N, LMAX), F32),
        ((N, LMAX), F32),
        ((2 * ROWS, LMAX), F32),
        ((128, LMAX), F32),
        ((LMAX, COLS), F32),
        ((LMAX, COLS), F32),
        ((128, 512), BF16),
        ((N, 512, LMAX), BF16),
        ((N, 512, LMAX), BF16),
        ((8 * N, COLS), F32),
        ((8 * N, COLS), F32),
        ((8 * N, COLS), F32),
        ((8 * N, COLS), F32),
        ((8 * N, COLS), F32),
        ((8 * N, COLS), F32),
        ((128, N * LMAX), BF16),
        ((LMAX, COLS), F32),
        ((LMAX, COLS), F32),
        ((128, LMAX), F32),
        ((N, 72, COLS), F32),
        ((N, 72, COLS), F32),
        ((L, ROWS, COLS), jnp.int32),
        ((ROWS, COLS), jnp.int32),
        ((ROWS, COLS), F32),
        ((N, L, L), F32),
        ((4, L, COLS), F32),
        ((4, L, COLS), F32),
        ((N, L, L), F32),
        ((2, L * L, COLS), F32),
        ((N * LMAX, 512), BF16),
        ((N * LMAX, 512), BF16),
        ((L, ROWS, COLS), F32),
        ((ROWS, COLS), F32),
        ((32, 256), F32),
        ((7, ROWS, COLS), F32),
        ((7, ROWS, COLS), F32),
        ((7, ROWS, COLS), F32),
        ((5, 32, COLS), F32),
        ((53, 8, COLS), F32),
        ((53, 8, COLS), F32),
        ((53, 8, COLS), F32),
        ((53, 8, COLS), F32),
    ]
    return pl.pallas_call(
        kernel,
        out_shape=(field, field),
        in_specs=[hbm] * 4 + [smem] * 3 + [hbm],
        out_specs=(hbm, hbm),
        scratch_shapes=[pltpu.VMEM(shape, dtype) for shape, dtype in scratch]
        + [
            pltpu.SemaphoreType.DMA((6, N)),
            pltpu.SemaphoreType.DMA((6, N)),
            pltpu.SemaphoreType.DMA((2, 6)),
            pltpu.SemaphoreType.DMA((2, 6)),
            pltpu.SemaphoreType.DMA((2,)),
            pltpu.SemaphoreType.DMA((5,)),
            pltpu.SemaphoreType.DMA((2 * N + 1,)),
        ],
        compiler_params=pltpu.CompilerParams(
            collective_id=0, has_side_effects=True, vmem_limit_bytes=60 * 1024 * 1024
        ),
    )(displacement, materials, ice_mask, ice_height, shear, restoring, contrast, green)


def solution(mesh):
    in_specs = (
        P(None, "lat", "lon"),
        P(None, "lat", "lon"),
        P("lat", "lon"),
        P("lat", "lon"),
        P(),
        P(),
        P(),
        P("lat", None, None),
    )
    out_specs = (P(None, "lat", "lon"), P(None, "lat", "lon"))
    return jax.shard_map(
        on_device, mesh=mesh, in_specs=in_specs, out_specs=out_specs, check_vma=False
    )
```

```python
import functools
import math

import jax
import jax.numpy as jnp
from jax import lax
from jax.experimental import pallas as pl
from jax.experimental.pallas import tpu as pltpu
from jax.sharding import PartitionSpec as P

L = 32
LMAX = 256
NLAT = 384
NLON = 2048
SWEEPS = 4
N = 16
ROWS = 24
COLS = 128
F32 = jnp.float32
BF16 = jnp.bfloat16
MESH = pl.DeviceIdType.MESH


def iota(shape, dim):
    return lax.broadcasted_iota(jnp.int32, shape, dim)


def split(x):
    hi = x.astype(BF16)
    lo = (x - hi.astype(F32)).astype(BF16)
    return hi, lo


def dot(a, b):
    return jnp.dot(a, b, preferred_element_type=F32)


def dot_t(a, b):
    return lax.dot_general(a, b, (((1,), (1,)), ((), ())), preferred_element_type=F32)


def unrolled(total, factor, one):
    def body(step, carry):
        for part in range(factor):
            one(step * factor + part)
        return carry

    lax.fori_loop(0, total // factor, body, 0)


def lookup(mat, table):
    out = jnp.where(mat == 0, table[0], 0.0)
    for material in range(1, 4):
        out = jnp.where(mat == material, table[material], out)
    return out


def kernel(
    u_in,
    mat_in,
    mask_in,
    ice_in,
    shear,
    restoring,
    contrast,
    green_in,
    u_out,
    pot_out,
    U,
    Bc,
    Rd,
    Ac,
    rho,
    dens,
    R1,
    FH,
    FL,
    WH,
    WL,
    C16,
    S16,
    wrow,
    Z,
    T2,
    R2,
    AH,
    Qh,
    Ql,
    T3,
    R3,
    T4,
    R4,
    RH,
    RL,
    XH,
    T5,
    R5,
    X5,
    T6,
    R6,
    mats,
    masks,
    ice,
    GA,
    GP,
    GQ,
    GR,
    GX,
    Ph,
    Pl,
    matf,
    load,
    loadx,
    E,
    EL,
    ER,
    PK,
    VT,
    VB,
    WT,
    WB,
    send_sem,
    recv_sem,
    hsend,
    hrecv,
    gsem,
    insem,
    outsem,
):
    me_lat = lax.axis_index("lat")
    me_lon = lax.axis_index("lon")

    barrier = pltpu.get_barrier_semaphore()

    def greet(d, carry):
        pl.semaphore_signal(barrier, inc=1, device_id={"lon": lax.rem(me_lon + d, N)}, device_id_type=MESH)
        pl.semaphore_signal(barrier, inc=1, device_id={"lat": lax.rem(me_lat + d, N)}, device_id_type=MESH)
        return carry

    lax.fori_loop(1, N, greet, 0)
    pl.semaphore_signal(
        barrier, inc=1, device_id={"lat": me_lon, "lon": lax.rem(me_lat + 1, N)}, device_id_type=MESH
    )

    main = U.at[0, pl.ds(1, L), pl.ds(0, ROWS), pl.ds(0, COLS)]
    loads = [
        pltpu.make_async_copy(mat_in, mats, insem.at[0]),
        pltpu.make_async_copy(u_in, main, insem.at[1]),
        pltpu.make_async_copy(mask_in, masks, insem.at[2]),
        pltpu.make_async_copy(ice_in, ice, insem.at[3]),
        pltpu.make_async_copy(green_in, GA, insem.at[4]),
    ]
    for copy in loads:
        copy.start()

    def tables():
        q = iota((COLS, LMAX), 0)
        m = iota((COLS, LMAX), 1)
        angle = (2.0 * math.pi / NLON) * ((q * m) & (NLON - 1)).astype(F32)
        hi, lo = split(jnp.cos(angle))
        FH[:, 0:LMAX] = hi
        FL[:, 0:LMAX] = lo
        hi, lo = split(jnp.sin(angle))
        FH[:, LMAX:] = hi
        FL[:, LMAX:] = lo
        p = iota((N, LMAX), 0)
        m = iota((N, LMAX), 1)
        angle = (2.0 * math.pi / N) * ((p * m) & (N - 1)).astype(F32)
        C16[...] = jnp.cos(angle)
        S16[...] = jnp.sin(angle)
        lane = iota((LMAX, 2 * COLS), 1)
        m = iota((LMAX, 2 * COLS), 0)
        q = jnp.where(lane < 128, lane, jnp.where(lane < 132, lane - 132 + NLON, lane - 4))
        angle = (2.0 * math.pi / NLON) * ((q * m) & (NLON - 1)).astype(F32)
        hi, lo = split(jnp.cos(angle))
        WH[0:LMAX, :] = hi
        WL[0:LMAX, :] = lo
        hi, lo = split(jnp.sin(angle))
        WH[LMAX:, :] = hi
        WL[LMAX:, :] = lo
        row = iota((ROWS, LMAX), 0) + me_lat * ROWS
        w = jnp.sin((row.astype(F32) + 0.5) * (math.pi / NLAT)) * (2.0 * math.pi / NLON / (4.0 * NLAT))
        wrow[0:ROWS, :] = w
        wrow[ROWS:, :] = w
        Z[...] = jnp.zeros_like(Z)
        for b in range(2):
            U[b, 0] = jnp.zeros((32, 256), F32)
            U[b, L + 1] = jnp.zeros((32, 256), F32)

    def prepare():
        def one(k):
            mat = mats[k]
            matf[k] = mat.astype(F32)
            rho[k] = lookup(mat, contrast)

        unrolled(L, 4, one)
        load[...] = masks[...].astype(F32) * ice[...]

    lane24 = iota((ROWS, COLS), 1)

    def pack(read, g):
        acc = jnp.zeros((ROWS, COLS), F32)
        for kk in range(16):
            acc = jnp.where(lane24 // 8 == kk, pltpu.roll(read(16 * g + kk), (8 * kk + 4) % COLS, 1), acc)
        return acc

    left = lax.rem(me_lon + N - 1, N)
    right = lax.rem(me_lon + 1, N)
    up = lax.rem(me_lat + N - 1, N)
    down = lax.rem(me_lat + 1, N)

    def edge_copies(it):
        first, count = (0, 5) if it == 0 else (5, 2)
        part = pl.ds(first, count)
        return [
            pltpu.make_async_remote_copy(
                E.at[part], ER.at[part], hsend.at[it, 0], hrecv.at[it, 0], device_id={"lon": left}, device_id_type=MESH
            ),
            pltpu.make_async_remote_copy(
                E.at[part], EL.at[part], hsend.at[it, 1], hrecv.at[it, 1], device_id={"lon": right}, device_id_type=MESH
            ),
        ]

    def row_copies(it, corners):
        if it == 0:
            first, count = (33, 3) if corners else (0, 33)
        else:
            first, count = (36, 17)
        part = pl.ds(first, count)
        one = 4 if corners else 2
        return [
            pltpu.make_async_remote_copy(
                VT.at[part],
                WT.at[part],
                hsend.at[it, one],
                hrecv.at[it, one],
                device_id={"lat": up},
                device_id_type=MESH,
            ),
            pltpu.make_async_remote_copy(
                VB.at[part],
                WB.at[part],
                hsend.at[it, one + 1],
                hrecv.at[it, one + 1],
                device_id={"lat": down},
                device_id_type=MESH,
            ),
        ]

    def merge_edges(it):
        first, count = (0, 5) if it == 0 else (5, 2)
        for g in range(count):
            PK[g, 0:ROWS] = jnp.where(lane24 % 8 < 4, EL[first + g], ER[first + g])

    row8 = iota((8, COLS), 0)

    def pair_rows(t, a_top, a_bot, b_top, b_bot):
        VT[t] = jnp.where(row8 < 4, a_top, pltpu.roll(b_top, 4, 0))
        VB[t] = jnp.where(row8 < 4, pltpu.roll(a_bot, 4, 0), b_bot)

    def halo_rows(t):
        top, bot = WT[t], WB[t]
        first = jnp.where(row8 < 4, top, pltpu.roll(bot, 4, 0))
        second = jnp.where(row8 < 4, pltpu.roll(top, 4, 0), bot)
        return first, second

    rows32 = iota((32, 256), 0)
    global_row = me_lat * ROWS + jnp.where(rows32 < 28, rows32, rows32 - 32)
    inside = (global_row >= 0) & (global_row < NLAT)
    inside8 = inside[24:32, 0:COLS]

    def pair_u(base):
        def one(k):
            pair_rows(
                base + k,
                U[0, k + 1, 0:8, 0:COLS],
                U[0, k + 1, 16:24, 0:COLS],
                U[0, k + 17, 0:8, 0:COLS],
                U[0, k + 17, 16:24, 0:COLS],
            )

        unrolled(16, 4, one)

    def pair_packed(t, g):
        pair_rows(t, PK[g, 0:8], PK[g, 16:24], PK[g + 1, 0:8], PK[g + 1, 16:24])

    def fill_u(base, packed):
        first, second = halo_rows(packed)
        PK[0, 24:32] = jnp.where(inside8, first, 0.0)
        PK[1, 24:32] = jnp.where(inside8, second, 0.0)

        def one(k):
            first, second = halo_rows(base + k)
            U[0, k + 1, 24:32, 0:COLS] = jnp.where(inside8, first, 0.0)
            U[0, k + 17, 24:32, 0:COLS] = jnp.where(inside8, second, 0.0)
            U[0, k + 1, :, COLS:] = pltpu.roll(PK[0], 124 - 8 * k, 1)
            U[0, k + 17, :, COLS:] = pltpu.roll(PK[1], 124 - 8 * k, 1)

        unrolled(16, 4, one)

    def legendre_setup():
        lane = iota((N, 512), 1)
        order = (iota((N, 512), 0) + me_lat * N).astype(F32)
        aa = lane % 32
        a = (lane // 32) * ROWS + jnp.where(aa < 28, aa, aa - 32)
        a = jnp.clip(a, 0, NLAT - 1)
        theta = (a.astype(F32) + 0.5) * (math.pi / NLAT)
        cosine = jnp.cos(theta)
        sine = jnp.sin(theta)
        t = iota((N, LMAX), 1)
        m_int = iota((N, LMAX), 0) + me_lat * N
        t_f = jnp.maximum(t.astype(F32), 1.0)
        growth = jnp.where((t >= 2) & (t <= m_int), 0.5 * jnp.log((2.0 * t_f + 1.0) / (2.0 * t_f)), 0.0)
        log_diag = jnp.sum(growth, axis=1, keepdims=True) + 0.5 * math.log(3.0)
        log_diag = jnp.where(m_int[:, 0:1] >= 1, log_diag, 0.0)
        diagonal = jnp.exp(log_diag + order * jnp.log(sine))
        start = jnp.sqrt(2.0 * order + 3.0) * cosine * diagonal
        deg = iota((N, LMAX), 1).astype(F32)
        m_f = m_int.astype(F32)
        first = jnp.sqrt(
            jnp.maximum(4.0 * deg * deg - 1.0, 1.0) / jnp.maximum(deg * deg - m_f * m_f, 1.0)
        )
        second = jnp.sqrt(
            jnp.maximum((deg - 1.0) * (deg - 1.0) - m_f * m_f, 0.0)
            / jnp.maximum(4.0 * (deg - 1.0) * (deg - 1.0) - 1.0, 1.0)
        )
        order_i = iota((N, 512), 0) + me_lat * N

        def block(lb, carry):
            one, two = carry
            shift = lax.rem(LMAX - 8 * lb, LMAX)
            f = pltpu.roll(first, shift, 1)[:, 0:COLS]
            s = pltpu.roll(second, shift, 1)[:, 0:COLS]
            for r in range(8):
                degree = lb * 8 + r
                fb = jnp.broadcast_to(f[:, r : r + 1], (N, 512))
                sb = jnp.broadcast_to(s[:, r : r + 1], (N, 512))
                general = fb * (cosine * one - sb * two)
                value = jnp.where(
                    order_i == degree, diagonal, jnp.where(order_i == degree - 1, start, general)
                )
                hi, lo = split(value)
                here = pl.ds(pl.multiple_of(degree * N, N), N)
                Ph[here, :] = hi
                Pl[here, :] = lo
                one, two = value, one
            return one, two

        zeros = jnp.zeros((N, 512), F32)
        return block, (zeros, zeros)

    def exchange(phase, axis, src, dst, peer, sender):
        if 1 <= phase <= 4:
            sender, slot = 0, 0
        else:
            slot = peer
        return pltpu.make_async_remote_copy(
            src,
            dst,
            send_sem.at[phase, slot],
            recv_sem.at[phase, sender],
            device_id={axis: peer},
            device_id_type=MESH,
        )

    def slab(ref, index, size):
        return ref.at[pl.ds(pl.multiple_of(index * size, size), size)]

    def far_first(d):
        return lax.rem(d + 6, N - 1) + 1

    def swap_start(phase, axis, me, src, dst, size):
        def one(d, carry):
            peer = lax.rem(me + far_first(d), N)
            exchange(phase, axis, slab(src, peer, size), slab(dst, me, size), peer, me).start()
            return carry

        lax.fori_loop(1, N, one, 0)
        mine = pl.ds(pl.multiple_of(me * size, size), size)
        dst[mine, :] = src[mine, :]

    def swap_wait(phase, axis, me, src, dst, size):
        part = pl.ds(0, (N - 1) * size)
        copy = exchange(phase, axis, src.at[part], dst.at[part], lax.rem(me + 1, N), 0)
        copy.wait_recv()
        copy.wait_send()

    lane32 = iota((32, COLS), 1)

    def sweep(src, dst, last):
        rows = ROWS if last else 32

        def one(k):
            t0 = U[src, k + 1, :, 0:COLS]
            t1 = U[src, k + 1, :, COLS:]
            r0, r1 = pltpu.roll(t0[0:rows], 1, 1), pltpu.roll(t1[0:rows], 1, 1)
            l0, l1 = pltpu.roll(t0[0:rows], COLS - 1, 1), pltpu.roll(t1[0:rows], COLS - 1, 1)
            first = lane32[0:rows] == 0
            final = lane32[0:rows] == COLS - 1
            around = (
                (jnp.where(first, r1, r0) + jnp.where(final, l1, l0))
                + (pltpu.roll(t0, 1, 0) + pltpu.roll(t0, 31, 0))[0:rows]
                + (U[src, k, 0:rows, 0:COLS] + U[src, k + 2, 0:rows, 0:COLS])
            )
            U[dst, k + 1, 0:rows, 0:COLS] = Ac[k, 0:rows, 0:COLS] + Bc[k, 0:rows, 0:COLS] * around
            if not last:
                around = (
                    (jnp.where(first, r0, r1) + jnp.where(final, l0, l1))
                    + (pltpu.roll(t1, 1, 0) + pltpu.roll(t1, 31, 0))
                    + (U[src, k, :, COLS:] + U[src, k + 2, :, COLS:])
                )
                U[dst, k + 1, :, COLS:] = Ac[k, :, COLS:] + Bc[k, :, COLS:] * around

        unrolled(L, 4, one)

    def coefficient(k, rows, cols, mat, valid):
        st = lookup(mat, shear)
        re = lookup(mat, restoring)
        inv = 1.0 / (6.0 * st + re)
        if valid is not None:
            inv = jnp.where(valid, inv, 0.0)
        Rd[k, rows, cols] = inv
        Bc[k, rows, cols] = st * inv
        Ac[k, rows, cols] = jnp.zeros(inv.shape, F32)

    def main_coefficients():
        unrolled(L, 4, lambda k: coefficient(k, slice(0, ROWS), slice(0, COLS), matf[k], None))

    inside_side = inside[:, 0:COLS]

    def margin_coefficients():
        first, second = halo_rows(34)
        PK[2, 24:32] = first
        PK[3, 24:32] = second

        def one(k):
            first, second = halo_rows(16 + k)
            coefficient(k, slice(ROWS, 32), slice(0, COLS), first, inside8)
            coefficient(k + 16, slice(ROWS, 32), slice(0, COLS), second, inside8)
            for g in range(2):
                side = pltpu.roll(PK[2 + g], 124 - 8 * k, 1)
                coefficient(k + 16 * g, slice(0, 32), slice(COLS, 2 * COLS), side, inside_side)

        unrolled(16, 2, one)
        PK[4, 24:32] = halo_rows(35)[0]
        loadx[0:ROWS, 0:COLS] = load[...]
        loadx[ROWS:, 0:COLS] = halo_rows(32)[0]
        loadx[:, COLS:] = pltpu.roll(PK[4], 124, 1)
        Ac[0] = loadx[...] * Rd[0]

    lane16 = iota((N, COLS), 1)
    diagonal64 = iota((64, LMAX), 0) % N == iota((64, LMAX), 1) % N
    diagonal16 = iota((N, COLS), 0) == iota((N, COLS), 1) % N

    def forward_fourier():
        def pair(step, acc):
            acc_c, acc_s = acc
            ps = [lax.rem(me_lon + 2 * step + q, N) for q in range(2)]
            his, los = zip(*[split(R1[p].reshape(2 * ROWS, COLS)) for p in ps])
            r = dot(jnp.concatenate(his + los, axis=0), FH[...])
            r = r[0 : 4 * ROWS] + r[4 * ROWS :] + dot(jnp.concatenate(his, axis=0), FL[...])
            for q, p in enumerate(ps):
                yc = r[2 * ROWS * q : 2 * ROWS * (q + 1), 0:LMAX]
                ys = r[2 * ROWS * q : 2 * ROWS * (q + 1), LMAX:]
                c = C16[pl.ds(p, 1), :]
                s = S16[pl.ds(p, 1), :]
                acc_c, acc_s = acc_c + (c * yc - s * ys), acc_s + (s * yc + c * ys)
            return acc_c, acc_s

        def wait(d):
            p = lax.rem(me_lon + d, N)
            copy = exchange(0, "lon", dens.at[p], R1.at[p], p, p)
            copy.wait_send()
            copy.wait_recv()

        def one(step, acc):
            wait(2 * step)
            wait(2 * step + 1)
            return pair(step, acc)

        zeros = jnp.zeros((2 * ROWS, LMAX), F32)
        R1[me_lon] = dens[me_lon]
        wait(1)
        acc_c, acc_s = lax.fori_loop(1, N // 2, one, pair(0, (zeros, zeros)))
        for c, acc in ((0, acc_c), (1, acc_s)):
            acc = acc * wrow[...]
            for kk in range(2):
                Z[(2 * c + kk) * 32 : (2 * c + kk) * 32 + ROWS, :] = acc[kk * ROWS : (kk + 1) * ROWS]
        T2[...] = jnp.transpose(Z[...])

    def transpose_legendre():
        def one(b):
            here = pl.ds(pl.multiple_of(b * LMAX, LMAX), LMAX)
            for src, dst in ((Ph, Qh), (Pl, Ql)):
                dst[b] = jnp.transpose(src[here, :])

        unrolled(N, 1, one)

    def forward_legendre():
        for t in range(4):
            parts = [R2[(4 * t + ii) * N : (4 * t + ii + 1) * N, :] for ii in range(4)]
            for ck in range(4):
                out = None
                for ii in range(4):
                    turn = ((ii - ck) * 32) % COLS
                    v = parts[ii] if turn == 0 else pltpu.roll(parts[ii], turn, 1)
                    out = v if out is None else jnp.where(lane16 // 32 == ii, v, out)
                hi, lo = split(out)
                AH[ck * N : (ck + 1) * N, t * COLS : (t + 1) * COLS] = hi
                AH[64 + ck * N : 64 + (ck + 1) * N, t * COLS : (t + 1) * COLS] = lo

        def product(b):
            r = dot(AH[...], Qh[b])
            return r[0:64] + r[64:] + dot(AH[0:64], Ql[b])

        def one(step, carry):
            bs = [lax.rem(me_lon + 1 + 4 * step + q, N) for q in range(4)]
            products = [product(b) for b in bs]
            for q, (b, r) in enumerate(zip(bs, products)):
                r = jnp.where(diagonal64, r, 0.0)
                totals = [
                    jnp.sum(r[ck * N : ck * N + 8] + r[ck * N + 8 : ck * N + 16], axis=0, keepdims=True)
                    for ck in range(4)
                ]
                out = [v[:, t * COLS : (t + 1) * COLS] for t in range(2) for v in totals]
                T3[pl.ds(pl.multiple_of(b * 8, 8), 8), :] = jnp.concatenate(out, axis=0)
                copy = exchange(2, "lon", slab(T3, b, 8), slab(R3, me_lon, 8), b, me_lon)
                if q < 3:
                    copy.start()
                else:
                    pl.when(step < 3)(copy.start)
            return carry

        lax.fori_loop(0, 4, one, 0)
        mine = pl.ds(pl.multiple_of(me_lon * 8, 8), 8)
        R3[mine, :] = T3[mine, :]

    def expand_green():
        chosen = (iota((N, LMAX), 0) == iota((N, LMAX), 1) // N).astype(F32)
        for g in range(4):
            for q in range(4):
                GR[4 * g + q] = GQ[g, :, q * L : (q + 1) * L]
        for k in range(L):
            out = lax.dot_general(
                GR[:, k, :],
                chosen,
                (((0,), (0,)), ((), ())),
                precision=lax.Precision.HIGHEST,
                preferred_element_type=F32,
            )
            GX[0, pl.ds(k, L, stride=L), :] = out[:, 0:COLS]
            GX[1, pl.ds(k, L, stride=L), :] = out[:, COLS:]

    def layer_sum():
        for t in range(2):
            acc = [jnp.zeros((L, COLS), F32), jnp.zeros((L, COLS), F32)]
            for k in range(L):
                kk, j = k // N, k % N
                g = GX[t, k * L : (k + 1) * L, :]
                for c in range(2):
                    row = j * 8 + t * 4 + 2 * c + kk
                    acc[c] = acc[c] + g * R3[row : row + 1, :]
            for c in range(2):
                for kk in range(2):
                    T4[pl.ds(t * 4 + 2 * c + kk, N, stride=8), :] = acc[c][kk * N : (kk + 1) * N]

    def inverse_legendre():
        x = R4[...]
        hi = x.astype(BF16).astype(F32)
        RH[...] = hi
        RL[...] = x - hi

        def build(b):
            for ck in range(4):
                for t in range(2):
                    row = pl.ds(b * 8 + t * 4 + ck, 1)
                    cols = pl.ds(pl.multiple_of(b * LMAX + t * COLS, COLS), COLS)
                    for base, ref in ((0, RH), (64, RL)):
                        v = jnp.where(diagonal16, ref[row, :], 0.0)
                        XH[base + ck * N : base + (ck + 1) * N, cols] = v.astype(BF16)

        unrolled(N, 2, build)

        def half(chunk):
            lanes = pl.ds(pl.multiple_of(chunk * 2 * COLS, 2 * COLS), 2 * COLS)

            def one(step, acc):
                here = pl.ds(pl.multiple_of(step * 4 * LMAX, 4 * LMAX), 4 * LMAX)
                r = dot(XH[:, here], Ph[here, lanes])
                return acc + (r[0:64] + r[64:] + dot(XH[0:64, here], Pl[here, lanes]))

            y = lax.fori_loop(0, 4, one, jnp.zeros((64, 2 * COLS), F32))
            for i8 in range(8):
                t, ii = i8 // 4, i8 % 4
                out = None
                for ck in range(4):
                    turn = ((ck - ii) * 32) % COLS
                    v = y[ck * N : (ck + 1) * N, t * COLS : (t + 1) * COLS]
                    v = v if turn == 0 else pltpu.roll(v, turn, 1)
                    out = v if out is None else jnp.where(lane16 // 32 == ck, v, out)
                i = chunk * 8 + i8
                T5[pl.ds(pl.multiple_of(i * N, N), N), :] = out

                @pl.when(i != me_lat)
                def _():
                    exchange(4, "lat", slab(T5, i, N), slab(R5, me_lat, N), i, me_lat).start()

        near = me_lat // 8
        half(1 - near)
        half(near)
        mine = pl.ds(pl.multiple_of(me_lat * N, N), N)
        R5[mine, :] = T5[mine, :]

    lane8 = iota((8, COLS), 1)

    def force(j):
        side = R6[j, 64:72, :]
        for kk in range(2):
            k = kk * N + j
            main = R6[j, kk * 32 : (kk + 1) * 32, :]
            halo = jnp.concatenate([pltpu.roll(side, 124 - 8 * (4 * kk + g), 1) for g in range(4)], axis=0)
            Ac[k] = jnp.concatenate([main, halo], axis=1) * Rd[k]

    def pot_copy(j, kk):
        return pltpu.make_async_copy(
            R6.at[j, pl.ds(kk * ROWS, ROWS)], pot_out.at[kk * N + j], outsem.at[2 * j + kk]
        )

    def inverse_fourier(final):
        X5[...] = jnp.transpose(R5[...])
        height = ROWS if final else 32
        rows = 2 * height
        size = rows if final else 72
        width = COLS if final else 2 * COLS

        def own(base):
            return jnp.concatenate([X5[base + kk * 32 : base + kk * 32 + height, :] for kk in range(2)], axis=0)

        def piece(p):
            return T6.at[p, pl.ds(0, size)], R6.at[me_lon, pl.ds(0, size)], R6.at[p, pl.ds(0, size)]

        def one(step, carry):
            first = far_first(2 * step + 1)
            second = jnp.where(step == N // 2 - 1, 0, far_first(2 * step + 2))
            ps = [lax.rem(me_lon + first, N), lax.rem(me_lon + second, N)]
            his, los = [], []
            a, b = own(0), own(64)
            for p in ps:
                c = C16[pl.ds(p, 1), :]
                s = S16[pl.ds(p, 1), :]
                hi, lo = split(jnp.concatenate([a * c + b * s, b * c - a * s], axis=1))
                his.append(hi)
                los.append(lo)
            r = dot(jnp.concatenate(his + los, axis=0), WH[:, 0:width])
            both = r[0 : 2 * rows] + r[2 * rows :] + dot(jnp.concatenate(his, axis=0), WL[:, 0:width])
            for q, p in enumerate(ps):
                r = both[q * rows : (q + 1) * rows]
                T6[p, 0:rows, :] = r[:, 0:COLS]
                if not final:
                    side = r[0:8, COLS:]
                    for t in range(1, 8):
                        v = pltpu.roll(r[8 * t : 8 * t + 8, COLS:], 8 * t, 1)
                        side = jnp.where(lane8 // 8 == t, v, side)
                    T6[p, 64:72, :] = side
                src, dst, _ = piece(p)
                if q == 0:
                    exchange(5, "lon", src, dst, p, me_lon).start()
                else:

                    @pl.when(step < N // 2 - 1)
                    def _():
                        exchange(5, "lon", src, dst, p, me_lon).start()

            return carry

        lax.fori_loop(0, N // 2, one, 0)
        R6[me_lon, 0:size] = T6[me_lon, 0:size]
        if final:
            for kk in range(2):
                pot_copy(me_lon, kk).start()
        else:
            force(me_lon)

        def wait(d, carry):
            p = lax.rem(me_lon + d, N)
            src, _, dst = piece(p)
            copy = exchange(5, "lon", src, dst, p, p)
            copy.wait_send()
            copy.wait_recv()
            if final:
                for kk in range(2):
                    pot_copy(p, kk).start()
            else:
                force(p)
            return carry

        lax.fori_loop(1, N, wait, 0)
        if not final:
            Ac[0] = Ac[0] + loadx[...] * Rd[0]

    def send_density():
        def one(q, carry):
            for kk in range(2):
                k = kk * N + q
                dens[q, kk] = rho[k] * U[0, k + 1, 0:ROWS, 0:COLS]
            return carry

        lax.fori_loop(0, N // 2, lambda h, c: one(2 * h + 1, one(2 * h, c)), 0)

        def start(d, carry):
            p = lax.rem(me_lon + far_first(d), N)
            exchange(0, "lon", dens.at[p], R1.at[me_lon], p, me_lon).start()
            return carry

        lax.fori_loop(1, N, start, 0)

    for copy in loads:
        copy.wait()
    prepare()
    E[0] = pack(lambda k: U[0, k + 1, 0:ROWS, 0:COLS], 0)
    E[1] = pack(lambda k: U[0, k + 1, 0:ROWS, 0:COLS], 1)
    E[2] = pack(lambda k: matf[k], 0)
    E[3] = pack(lambda k: matf[k], 1)
    E[4] = pltpu.roll(load[...], 4, 1)
    pair_u(0)

    def pair_mat(k):
        pair_rows(16 + k, matf[k, 0:8], matf[k, 16:24], matf[k + 16, 0:8], matf[k + 16, 16:24])

    unrolled(16, 4, pair_mat)
    pair_rows(32, load[0:8], load[16:24], load[0:8], load[16:24])
    for g in range(4):
        GP[g] = jnp.concatenate([GA[4 * g + q] for q in range(4)], axis=1)
    tables()
    block, state = legendre_setup()
    state = lax.fori_loop(0, 2, block, state)
    pl.semaphore_wait(barrier, 2 * N - 1)
    edges = edge_copies(0)
    rows = row_copies(0, False)
    for copy in edges + rows:
        copy.start()
    state = lax.fori_loop(2, 12, block, state)
    for copy in edges:
        copy.wait()
    merge_edges(0)
    pair_packed(33, 0)
    pair_packed(34, 2)
    pair_rows(35, PK[4, 0:8], PK[4, 16:24], PK[4, 0:8], PK[4, 16:24])
    corners = row_copies(0, True)
    for copy in corners:
        copy.start()
    lax.fori_loop(12, 32, block, state)
    main_coefficients()
    for copy in rows + corners:
        copy.wait()
    green = pltpu.make_async_remote_copy(
        GP,
        GQ,
        gsem.at[0],
        gsem.at[1],
        device_id={"lat": lax.rem(me_lon + N - 1, N), "lon": me_lat},
        device_id_type=MESH,
    )
    green.start()
    fill_u(0, 33)
    margin_coefficients()

    for it in range(2):
        for s in range(SWEEPS):
            sweep(s % 2, (s + 1) % 2, s == SWEEPS - 1)
        send_density()
        if it == 0:
            E[5] = pack(lambda k: U[0, k + 1, 0:ROWS, 0:COLS], 0)
            E[6] = pack(lambda k: U[0, k + 1, 0:ROWS, 0:COLS], 1)
        else:
            u_copy = pltpu.make_async_copy(main, u_out, outsem.at[2 * N])
            u_copy.start()
        forward_fourier()
        swap_start(1, "lat", me_lat, T2, R2, N)
        if it == 0:
            edges = edge_copies(1)
            for copy in edges:
                copy.start()
            transpose_legendre()
        swap_wait(1, "lat", me_lat, T2, R2, N)
        forward_legendre()
        if it == 0:
            for copy in edges:
                copy.wait()
            merge_edges(1)
            pair_u(36)
            pair_packed(52, 0)
            rows = row_copies(1, False)
            for copy in rows:
                copy.start()
            green.wait()
            expand_green()
        swap_wait(2, "lon", me_lon, T3, R3, 8)
        layer_sum()
        swap_start(3, "lon", me_lon, T4, R4, 8)
        swap_wait(3, "lon", me_lon, T4, R4, 8)
        inverse_legendre()
        if it == 0:
            for copy in rows:
                copy.wait()
            fill_u(36, 52)
        swap_wait(4, "lat", me_lat, T5, R5, N)
        inverse_fourier(it == 1)

    def finish(j):
        for kk in range(2):
            pot_copy(j, kk).wait()

    unrolled(N, 4, finish)
    u_copy.wait()


def on_device(displacement, materials, ice_mask, ice_height, shear, restoring, contrast, green):
    hbm = pl.BlockSpec(memory_space=pl.ANY)
    smem = pl.BlockSpec(memory_space=pltpu.SMEM)
    field = jax.ShapeDtypeStruct((L, ROWS, COLS), F32)
    scratch = [
        ((2, L + 2, 32, 256), F32),
        ((L, 32, 256), F32),
        ((L, 32, 256), F32),
        ((L, 32, 256), F32),
        ((L, ROWS, COLS), F32),
        ((N, 2, ROWS, COLS), F32),
        ((N, 2, ROWS, COLS), F32),
        ((COLS, 512), BF16),
        ((COLS, 512), BF16),
        ((512, 256), BF16),
        ((512, 256), BF16),
        ((N, LMAX), F32),
        ((N, LMAX), F32),
        ((2 * ROWS, LMAX), F32),
        ((128, LMAX), F32),
        ((LMAX, COLS), F32),
        ((LMAX, COLS), F32),
        ((128, 512), BF16),
        ((N, 512, LMAX), BF16),
        ((N, 512, LMAX), BF16),
        ((8 * N, COLS), F32),
        ((8 * N, COLS), F32),
        ((8 * N, COLS), F32),
        ((8 * N, COLS), F32),
        ((8 * N, COLS), F32),
        ((8 * N, COLS), F32),
        ((128, N * LMAX), BF16),
        ((LMAX, COLS), F32),
        ((LMAX, COLS), F32),
        ((128, LMAX), F32),
        ((N, 72, COLS), F32),
        ((N, 72, COLS), F32),
        ((L, ROWS, COLS), jnp.int32),
        ((ROWS, COLS), jnp.int32),
        ((ROWS, COLS), F32),
        ((N, L, L), F32),
        ((4, L, COLS), F32),
        ((4, L, COLS), F32),
        ((N, L, L), F32),
        ((2, L * L, COLS), F32),
        ((N * LMAX, 512), BF16),
        ((N * LMAX, 512), BF16),
        ((L, ROWS, COLS), F32),
        ((ROWS, COLS), F32),
        ((32, 256), F32),
        ((7, ROWS, COLS), F32),
        ((7, ROWS, COLS), F32),
        ((7, ROWS, COLS), F32),
        ((5, 32, COLS), F32),
        ((53, 8, COLS), F32),
        ((53, 8, COLS), F32),
        ((53, 8, COLS), F32),
        ((53, 8, COLS), F32),
    ]
    return pl.pallas_call(
        kernel,
        out_shape=(field, field),
        in_specs=[hbm] * 4 + [smem] * 3 + [hbm],
        out_specs=(hbm, hbm),
        scratch_shapes=[pltpu.VMEM(shape, dtype) for shape, dtype in scratch]
        + [
            pltpu.SemaphoreType.DMA((6, N)),
            pltpu.SemaphoreType.DMA((6, N)),
            pltpu.SemaphoreType.DMA((2, 6)),
            pltpu.SemaphoreType.DMA((2, 6)),
            pltpu.SemaphoreType.DMA((2,)),
            pltpu.SemaphoreType.DMA((5,)),
            pltpu.SemaphoreType.DMA((2 * N + 1,)),
        ],
        compiler_params=pltpu.CompilerParams(
            collective_id=0, has_side_effects=True, vmem_limit_bytes=60 * 1024 * 1024
        ),
    )(displacement, materials, ice_mask, ice_height, shear, restoring, contrast, green)


def solution(mesh):
    in_specs = (
        P(None, "lat", "lon"),
        P(None, "lat", "lon"),
        P("lat", "lon"),
        P("lat", "lon"),
        P(),
        P(),
        P(),
        P("lat", None, None),
    )
    out_specs = (P(None, "lat", "lon"), P(None, "lat", "lon"))
    return jax.shard_map(
        on_device, mesh=mesh, in_specs=in_specs, out_specs=out_specs, check_vma=False
    )
```

```python
import functools
import math

import jax
import jax.numpy as jnp
from jax import lax
from jax.experimental import pallas as pl
from jax.experimental.pallas import tpu as pltpu
from jax.sharding import PartitionSpec as P

L = 32
LMAX = 256
NLAT = 384
NLON = 2048
SWEEPS = 4
N = 16
ROWS = 24
COLS = 128
F32 = jnp.float32
BF16 = jnp.bfloat16
MESH = pl.DeviceIdType.MESH


def iota(shape, dim):
    return lax.broadcasted_iota(jnp.int32, shape, dim)


def split(x):
    hi = x.astype(BF16)
    lo = (x - hi.astype(F32)).astype(BF16)
    return hi, lo


def dot(a, b):
    return jnp.dot(a, b, preferred_element_type=F32)


def dot_t(a, b):
    return lax.dot_general(a, b, (((1,), (1,)), ((), ())), preferred_element_type=F32)


def unrolled(total, factor, one):
    def body(step, carry):
        for part in range(factor):
            one(step * factor + part)
        return carry

    lax.fori_loop(0, total // factor, body, 0)


def lookup(mat, table):
    out = jnp.where(mat == 0, table[0], 0.0)
    for material in range(1, 4):
        out = jnp.where(mat == material, table[material], out)
    return out


def kernel(
    u_in,
    mat_in,
    mask_in,
    ice_in,
    shear,
    restoring,
    contrast,
    green_in,
    u_out,
    pot_out,
    U,
    Bc,
    Rd,
    Ac,
    rho,
    dens,
    R1,
    FH,
    FL,
    WH,
    WL,
    C16,
    S16,
    wrow,
    Z,
    T2,
    R2,
    AH,
    Qh,
    Ql,
    T3,
    R3,
    T4,
    R4,
    RH,
    RL,
    XH,
    T5,
    R5,
    X5,
    T6,
    R6,
    mats,
    masks,
    ice,
    GA,
    GP,
    GQ,
    GR,
    GX,
    Ph,
    Pl,
    matf,
    load,
    loadx,
    E,
    EL,
    ER,
    PK,
    VT,
    VB,
    WT,
    WB,
    send_sem,
    recv_sem,
    hsend,
    hrecv,
    gsem,
    insem,
    outsem,
):
    me_lat = lax.axis_index("lat")
    me_lon = lax.axis_index("lon")

    barrier = pltpu.get_barrier_semaphore()

    def greet(d, carry):
        pl.semaphore_signal(barrier, inc=1, device_id={"lon": lax.rem(me_lon + d, N)}, device_id_type=MESH)
        pl.semaphore_signal(barrier, inc=1, device_id={"lat": lax.rem(me_lat + d, N)}, device_id_type=MESH)
        return carry

    lax.fori_loop(1, N, greet, 0)
    pl.semaphore_signal(
        barrier, inc=1, device_id={"lat": me_lon, "lon": lax.rem(me_lat + 1, N)}, device_id_type=MESH
    )

    main = U.at[0, pl.ds(1, L), pl.ds(0, ROWS), pl.ds(0, COLS)]
    loads = [
        pltpu.make_async_copy(mat_in, mats, insem.at[0]),
        pltpu.make_async_copy(u_in, main, insem.at[1]),
        pltpu.make_async_copy(mask_in, masks, insem.at[2]),
        pltpu.make_async_copy(ice_in, ice, insem.at[3]),
        pltpu.make_async_copy(green_in, GA, insem.at[4]),
    ]
    for copy in loads:
        copy.start()

    def tables():
        q = iota((COLS, LMAX), 0)
        m = iota((COLS, LMAX), 1)
        angle = (2.0 * math.pi / NLON) * ((q * m) & (NLON - 1)).astype(F32)
        hi, lo = split(jnp.cos(angle))
        FH[:, 0:LMAX] = hi
        FL[:, 0:LMAX] = lo
        hi, lo = split(jnp.sin(angle))
        FH[:, LMAX:] = hi
        FL[:, LMAX:] = lo
        p = iota((N, LMAX), 0)
        m = iota((N, LMAX), 1)
        angle = (2.0 * math.pi / N) * ((p * m) & (N - 1)).astype(F32)
        C16[...] = jnp.cos(angle)
        S16[...] = jnp.sin(angle)
        lane = iota((LMAX, 2 * COLS), 1)
        m = iota((LMAX, 2 * COLS), 0)
        q = jnp.where(lane < 128, lane, jnp.where(lane < 132, lane - 132 + NLON, lane - 4))
        angle = (2.0 * math.pi / NLON) * ((q * m) & (NLON - 1)).astype(F32)
        hi, lo = split(jnp.cos(angle))
        WH[0:LMAX, :] = hi
        WL[0:LMAX, :] = lo
        hi, lo = split(jnp.sin(angle))
        WH[LMAX:, :] = hi
        WL[LMAX:, :] = lo
        row = iota((ROWS, LMAX), 0) + me_lat * ROWS
        w = jnp.sin((row.astype(F32) + 0.5) * (math.pi / NLAT)) * (2.0 * math.pi / NLON / (4.0 * NLAT))
        wrow[0:ROWS, :] = w
        wrow[ROWS:, :] = w
        Z[...] = jnp.zeros_like(Z)
        for b in range(2):
            U[b, 0] = jnp.zeros((32, 256), F32)
            U[b, L + 1] = jnp.zeros((32, 256), F32)

    def prepare():
        def one(k):
            mat = mats[k]
            matf[k] = mat.astype(F32)
            rho[k] = lookup(mat, contrast)

        unrolled(L, 4, one)
        load[...] = masks[...].astype(F32) * ice[...]

    lane24 = iota((ROWS, COLS), 1)

    def pack(read, g):
        acc = jnp.zeros((ROWS, COLS), F32)
        for kk in range(16):
            acc = jnp.where(lane24 // 8 == kk, pltpu.roll(read(16 * g + kk), (8 * kk + 4) % COLS, 1), acc)
        return acc

    left = lax.rem(me_lon + N - 1, N)
    right = lax.rem(me_lon + 1, N)
    up = lax.rem(me_lat + N - 1, N)
    down = lax.rem(me_lat + 1, N)

    def edge_copies(it):
        first, count = (0, 5) if it == 0 else (5, 2)
        part = pl.ds(first, count)
        return [
            pltpu.make_async_remote_copy(
                E.at[part], ER.at[part], hsend.at[it, 0], hrecv.at[it, 0], device_id={"lon": left}, device_id_type=MESH
            ),
            pltpu.make_async_remote_copy(
                E.at[part], EL.at[part], hsend.at[it, 1], hrecv.at[it, 1], device_id={"lon": right}, device_id_type=MESH
            ),
        ]

    def row_copies(it, corners):
        if it == 0:
            first, count = (33, 3) if corners else (0, 33)
        else:
            first, count = (36, 17)
        part = pl.ds(first, count)
        one = 4 if corners else 2
        return [
            pltpu.make_async_remote_copy(
                VT.at[part],
                WT.at[part],
                hsend.at[it, one],
                hrecv.at[it, one],
                device_id={"lat": up},
                device_id_type=MESH,
            ),
            pltpu.make_async_remote_copy(
                VB.at[part],
                WB.at[part],
                hsend.at[it, one + 1],
                hrecv.at[it, one + 1],
                device_id={"lat": down},
                device_id_type=MESH,
            ),
        ]

    def merge_edges(it):
        first, count = (0, 5) if it == 0 else (5, 2)
        for g in range(count):
            PK[g, 0:ROWS] = jnp.where(lane24 % 8 < 4, EL[first + g], ER[first + g])

    row8 = iota((8, COLS), 0)

    def pair_rows(t, a_top, a_bot, b_top, b_bot):
        VT[t] = jnp.where(row8 < 4, a_top, pltpu.roll(b_top, 4, 0))
        VB[t] = jnp.where(row8 < 4, pltpu.roll(a_bot, 4, 0), b_bot)

    def halo_rows(t):
        top, bot = WT[t], WB[t]
        first = jnp.where(row8 < 4, top, pltpu.roll(bot, 4, 0))
        second = jnp.where(row8 < 4, pltpu.roll(top, 4, 0), bot)
        return first, second

    rows32 = iota((32, 256), 0)
    global_row = me_lat * ROWS + jnp.where(rows32 < 28, rows32, rows32 - 32)
    inside = (global_row >= 0) & (global_row < NLAT)
    inside8 = inside[24:32, 0:COLS]

    def pair_u(base):
        def one(k):
            pair_rows(
                base + k,
                U[0, k + 1, 0:8, 0:COLS],
                U[0, k + 1, 16:24, 0:COLS],
                U[0, k + 17, 0:8, 0:COLS],
                U[0, k + 17, 16:24, 0:COLS],
            )

        unrolled(16, 4, one)

    def pair_packed(t, g):
        pair_rows(t, PK[g, 0:8], PK[g, 16:24], PK[g + 1, 0:8], PK[g + 1, 16:24])

    def fill_u(base, packed):
        first, second = halo_rows(packed)
        PK[0, 24:32] = jnp.where(inside8, first, 0.0)
        PK[1, 24:32] = jnp.where(inside8, second, 0.0)

        def one(k):
            first, second = halo_rows(base + k)
            U[0, k + 1, 24:32, 0:COLS] = jnp.where(inside8, first, 0.0)
            U[0, k + 17, 24:32, 0:COLS] = jnp.where(inside8, second, 0.0)
            U[0, k + 1, :, COLS:] = pltpu.roll(PK[0], 124 - 8 * k, 1)
            U[0, k + 17, :, COLS:] = pltpu.roll(PK[1], 124 - 8 * k, 1)

        unrolled(16, 4, one)

    def legendre_setup():
        lane = iota((N, 512), 1)
        order = (iota((N, 512), 0) + me_lat * N).astype(F32)
        aa = lane % 32
        a = (lane // 32) * ROWS + jnp.where(aa < 28, aa, aa - 32)
        a = jnp.clip(a, 0, NLAT - 1)
        theta = (a.astype(F32) + 0.5) * (math.pi / NLAT)
        cosine = jnp.cos(theta)
        sine = jnp.sin(theta)
        t = iota((N, LMAX), 1)
        m_int = iota((N, LMAX), 0) + me_lat * N
        t_f = jnp.maximum(t.astype(F32), 1.0)
        growth = jnp.where((t >= 2) & (t <= m_int), 0.5 * jnp.log((2.0 * t_f + 1.0) / (2.0 * t_f)), 0.0)
        log_diag = jnp.sum(growth, axis=1, keepdims=True) + 0.5 * math.log(3.0)
        log_diag = jnp.where(m_int[:, 0:1] >= 1, log_diag, 0.0)
        diagonal = jnp.exp(log_diag + order * jnp.log(sine))
        start = jnp.sqrt(2.0 * order + 3.0) * cosine * diagonal
        deg = iota((N, LMAX), 1).astype(F32)
        m_f = m_int.astype(F32)
        first = jnp.sqrt(
            jnp.maximum(4.0 * deg * deg - 1.0, 1.0) / jnp.maximum(deg * deg - m_f * m_f, 1.0)
        )
        second = jnp.sqrt(
            jnp.maximum((deg - 1.0) * (deg - 1.0) - m_f * m_f, 0.0)
            / jnp.maximum(4.0 * (deg - 1.0) * (deg - 1.0) - 1.0, 1.0)
        )
        order_i = iota((N, 512), 0) + me_lat * N

        def block(lb, carry):
            one, two = carry
            shift = lax.rem(LMAX - 8 * lb, LMAX)
            f = pltpu.roll(first, shift, 1)[:, 0:COLS]
            s = pltpu.roll(second, shift, 1)[:, 0:COLS]
            for r in range(8):
                degree = lb * 8 + r
                fb = jnp.broadcast_to(f[:, r : r + 1], (N, 512))
                sb = jnp.broadcast_to(s[:, r : r + 1], (N, 512))
                general = fb * (cosine * one - sb * two)
                value = jnp.where(
                    order_i == degree, diagonal, jnp.where(order_i == degree - 1, start, general)
                )
                hi, lo = split(value)
                here = pl.ds(pl.multiple_of(degree * N, N), N)
                Ph[here, :] = hi
                Pl[here, :] = lo
                one, two = value, one
            return one, two

        zeros = jnp.zeros((N, 512), F32)
        return block, (zeros, zeros)

    def exchange(phase, axis, src, dst, peer, sender):
        if 1 <= phase <= 4:
            sender, slot = 0, 0
        else:
            slot = peer
        return pltpu.make_async_remote_copy(
            src,
            dst,
            send_sem.at[phase, slot],
            recv_sem.at[phase, sender],
            device_id={axis: peer},
            device_id_type=MESH,
        )

    def slab(ref, index, size):
        return ref.at[pl.ds(pl.multiple_of(index * size, size), size)]

    def far_first(d):
        return lax.rem(d + 6, N - 1) + 1

    def arrival(d):
        return lax.rem(me_lon + N - far_first(d), N)

    def swap_start(phase, axis, me, src, dst, size):
        def one(d, carry):
            peer = lax.rem(me + far_first(d), N)
            exchange(phase, axis, slab(src, peer, size), slab(dst, me, size), peer, me).start()
            return carry

        lax.fori_loop(1, N, one, 0)
        mine = pl.ds(pl.multiple_of(me * size, size), size)
        dst[mine, :] = src[mine, :]

    def swap_wait(phase, axis, me, src, dst, size):
        part = pl.ds(0, (N - 1) * size)
        copy = exchange(phase, axis, src.at[part], dst.at[part], lax.rem(me + 1, N), 0)
        copy.wait_recv()
        copy.wait_send()

    lane32 = iota((32, COLS), 1)

    def sweep(src, dst, last):
        rows = ROWS if last else 32

        def one(k):
            t0 = U[src, k + 1, :, 0:COLS]
            t1 = U[src, k + 1, :, COLS:]
            r0, r1 = pltpu.roll(t0[0:rows], 1, 1), pltpu.roll(t1[0:rows], 1, 1)
            l0, l1 = pltpu.roll(t0[0:rows], COLS - 1, 1), pltpu.roll(t1[0:rows], COLS - 1, 1)
            first = lane32[0:rows] == 0
            final = lane32[0:rows] == COLS - 1
            around = (
                (jnp.where(first, r1, r0) + jnp.where(final, l1, l0))
                + (pltpu.roll(t0, 1, 0) + pltpu.roll(t0, 31, 0))[0:rows]
                + (U[src, k, 0:rows, 0:COLS] + U[src, k + 2, 0:rows, 0:COLS])
            )
            U[dst, k + 1, 0:rows, 0:COLS] = Ac[k, 0:rows, 0:COLS] + Bc[k, 0:rows, 0:COLS] * around
            if not last:
                around = (
                    (jnp.where(first, r0, r1) + jnp.where(final, l0, l1))
                    + (pltpu.roll(t1, 1, 0) + pltpu.roll(t1, 31, 0))
                    + (U[src, k, :, COLS:] + U[src, k + 2, :, COLS:])
                )
                U[dst, k + 1, :, COLS:] = Ac[k, :, COLS:] + Bc[k, :, COLS:] * around

        unrolled(L, 4, one)

    def coefficient(k, rows, cols, mat, valid):
        st = lookup(mat, shear)
        re = lookup(mat, restoring)
        inv = 1.0 / (6.0 * st + re)
        if valid is not None:
            inv = jnp.where(valid, inv, 0.0)
        Rd[k, rows, cols] = inv
        Bc[k, rows, cols] = st * inv
        Ac[k, rows, cols] = jnp.zeros(inv.shape, F32)

    def main_coefficients():
        unrolled(L, 4, lambda k: coefficient(k, slice(0, ROWS), slice(0, COLS), matf[k], None))

    inside_side = inside[:, 0:COLS]

    def margin_coefficients():
        first, second = halo_rows(34)
        PK[2, 24:32] = first
        PK[3, 24:32] = second

        def one(k):
            first, second = halo_rows(16 + k)
            coefficient(k, slice(ROWS, 32), slice(0, COLS), first, inside8)
            coefficient(k + 16, slice(ROWS, 32), slice(0, COLS), second, inside8)
            for g in range(2):
                side = pltpu.roll(PK[2 + g], 124 - 8 * k, 1)
                coefficient(k + 16 * g, slice(0, 32), slice(COLS, 2 * COLS), side, inside_side)

        unrolled(16, 2, one)
        PK[4, 24:32] = halo_rows(35)[0]
        loadx[0:ROWS, 0:COLS] = load[...]
        loadx[ROWS:, 0:COLS] = halo_rows(32)[0]
        loadx[:, COLS:] = pltpu.roll(PK[4], 124, 1)
        Ac[0] = loadx[...] * Rd[0]

    lane16 = iota((N, COLS), 1)
    diagonal64 = iota((64, LMAX), 0) % N == iota((64, LMAX), 1) % N
    diagonal16 = iota((N, COLS), 0) == iota((N, COLS), 1) % N

    def forward_fourier():
        def pair(step, acc):
            acc_c, acc_s = acc
            ps = [jnp.where(step == 0, me_lon, arrival(2 * step)), arrival(2 * step + 1)]
            his, los = zip(*[split(R1[p].reshape(2 * ROWS, COLS)) for p in ps])
            r = dot(jnp.concatenate(his + los, axis=0), FH[...])
            r = r[0 : 4 * ROWS] + r[4 * ROWS :] + dot(jnp.concatenate(his, axis=0), FL[...])
            for q, p in enumerate(ps):
                yc = r[2 * ROWS * q : 2 * ROWS * (q + 1), 0:LMAX]
                ys = r[2 * ROWS * q : 2 * ROWS * (q + 1), LMAX:]
                c = C16[pl.ds(p, 1), :]
                s = S16[pl.ds(p, 1), :]
                acc_c, acc_s = acc_c + (c * yc - s * ys), acc_s + (s * yc + c * ys)
            return acc_c, acc_s

        def wait(d):
            p = arrival(d)
            copy = exchange(0, "lon", dens.at[p], R1.at[p], p, p)
            copy.wait_send()
            copy.wait_recv()

        def one(step, acc):
            wait(2 * step)
            wait(2 * step + 1)
            return pair(step, acc)

        zeros = jnp.zeros((2 * ROWS, LMAX), F32)
        R1[me_lon] = dens[me_lon]
        wait(1)
        acc_c, acc_s = lax.fori_loop(1, N // 2, one, pair(0, (zeros, zeros)))
        for c, acc in ((0, acc_c), (1, acc_s)):
            acc = acc * wrow[...]
            for kk in range(2):
                Z[(2 * c + kk) * 32 : (2 * c + kk) * 32 + ROWS, :] = acc[kk * ROWS : (kk + 1) * ROWS]
        T2[...] = jnp.transpose(Z[...])

    def transpose_legendre():
        def one(b):
            here = pl.ds(pl.multiple_of(b * LMAX, LMAX), LMAX)
            for src, dst in ((Ph, Qh), (Pl, Ql)):
                dst[b] = jnp.transpose(src[here, :])

        unrolled(N, 1, one)

    def forward_legendre():
        for t in range(4):
            parts = [R2[(4 * t + ii) * N : (4 * t + ii + 1) * N, :] for ii in range(4)]
            for ck in range(4):
                out = None
                for ii in range(4):
                    turn = ((ii - ck) * 32) % COLS
                    v = parts[ii] if turn == 0 else pltpu.roll(parts[ii], turn, 1)
                    out = v if out is None else jnp.where(lane16 // 32 == ii, v, out)
                hi, lo = split(out)
                AH[ck * N : (ck + 1) * N, t * COLS : (t + 1) * COLS] = hi
                AH[64 + ck * N : 64 + (ck + 1) * N, t * COLS : (t + 1) * COLS] = lo

        def product(b):
            r = dot(AH[...], Qh[b])
            return r[0:64] + r[64:] + dot(AH[0:64], Ql[b])

        def one(step, carry):
            bs = [lax.rem(me_lon + 1 + 4 * step + q, N) for q in range(4)]
            products = [product(b) for b in bs]
            for q, (b, r) in enumerate(zip(bs, products)):
                r = jnp.where(diagonal64, r, 0.0)
                totals = [
                    jnp.sum(r[ck * N : ck * N + 8] + r[ck * N + 8 : ck * N + 16], axis=0, keepdims=True)
                    for ck in range(4)
                ]
                out = [v[:, t * COLS : (t + 1) * COLS] for t in range(2) for v in totals]
                T3[pl.ds(pl.multiple_of(b * 8, 8), 8), :] = jnp.concatenate(out, axis=0)
                copy = exchange(2, "lon", slab(T3, b, 8), slab(R3, me_lon, 8), b, me_lon)
                if q < 3:
                    copy.start()
                else:
                    pl.when(step < 3)(copy.start)
            return carry

        lax.fori_loop(0, 4, one, 0)
        mine = pl.ds(pl.multiple_of(me_lon * 8, 8), 8)
        R3[mine, :] = T3[mine, :]

    def expand_green():
        chosen = (iota((N, LMAX), 0) == iota((N, LMAX), 1) // N).astype(F32)
        for g in range(4):
            for q in range(4):
                GR[4 * g + q] = GQ[g, :, q * L : (q + 1) * L]
        for k in range(L):
            out = lax.dot_general(
                GR[:, k, :],
                chosen,
                (((0,), (0,)), ((), ())),
                precision=lax.Precision.HIGHEST,
                preferred_element_type=F32,
            )
            GX[0, pl.ds(k, L, stride=L), :] = out[:, 0:COLS]
            GX[1, pl.ds(k, L, stride=L), :] = out[:, COLS:]

    def layer_sum():
        for t in range(2):
            acc = [jnp.zeros((L, COLS), F32), jnp.zeros((L, COLS), F32)]
            for k in range(L):
                kk, j = k // N, k % N
                g = GX[t, k * L : (k + 1) * L, :]
                for c in range(2):
                    row = j * 8 + t * 4 + 2 * c + kk
                    acc[c] = acc[c] + g * R3[row : row + 1, :]
            for c in range(2):
                for kk in range(2):
                    T4[pl.ds(t * 4 + 2 * c + kk, N, stride=8), :] = acc[c][kk * N : (kk + 1) * N]

    def inverse_legendre():
        x = R4[...]
        hi = x.astype(BF16).astype(F32)
        RH[...] = hi
        RL[...] = x - hi

        def build(b):
            for ck in range(4):
                for t in range(2):
                    row = pl.ds(b * 8 + t * 4 + ck, 1)
                    cols = pl.ds(pl.multiple_of(b * LMAX + t * COLS, COLS), COLS)
                    for base, ref in ((0, RH), (64, RL)):
                        v = jnp.where(diagonal16, ref[row, :], 0.0)
                        XH[base + ck * N : base + (ck + 1) * N, cols] = v.astype(BF16)

        unrolled(N, 2, build)

        def half(chunk):
            lanes = pl.ds(pl.multiple_of(chunk * 2 * COLS, 2 * COLS), 2 * COLS)

            def one(step, acc):
                here = pl.ds(pl.multiple_of(step * 4 * LMAX, 4 * LMAX), 4 * LMAX)
                r = dot(XH[:, here], Ph[here, lanes])
                return acc + (r[0:64] + r[64:] + dot(XH[0:64, here], Pl[here, lanes]))

            y = lax.fori_loop(0, 4, one, jnp.zeros((64, 2 * COLS), F32))
            for i8 in range(8):
                t, ii = i8 // 4, i8 % 4
                out = None
                for ck in range(4):
                    turn = ((ck - ii) * 32) % COLS
                    v = y[ck * N : (ck + 1) * N, t * COLS : (t + 1) * COLS]
                    v = v if turn == 0 else pltpu.roll(v, turn, 1)
                    out = v if out is None else jnp.where(lane16 // 32 == ck, v, out)
                i = chunk * 8 + i8
                T5[pl.ds(pl.multiple_of(i * N, N), N), :] = out

                @pl.when(i != me_lat)
                def _():
                    exchange(4, "lat", slab(T5, i, N), slab(R5, me_lat, N), i, me_lat).start()

        near = me_lat // 8
        half(1 - near)
        half(near)
        mine = pl.ds(pl.multiple_of(me_lat * N, N), N)
        R5[mine, :] = T5[mine, :]

    lane8 = iota((8, COLS), 1)

    def force(j):
        side = R6[j, 64:72, :]
        for kk in range(2):
            k = kk * N + j
            main = R6[j, kk * 32 : (kk + 1) * 32, :]
            halo = jnp.concatenate([pltpu.roll(side, 124 - 8 * (4 * kk + g), 1) for g in range(4)], axis=0)
            Ac[k] = jnp.concatenate([main, halo], axis=1) * Rd[k]

    def pot_copy(j, kk):
        return pltpu.make_async_copy(
            R6.at[j, pl.ds(kk * ROWS, ROWS)], pot_out.at[kk * N + j], outsem.at[2 * j + kk]
        )

    def inverse_fourier(final):
        X5[...] = jnp.transpose(R5[...])
        height = ROWS if final else 32
        rows = 2 * height
        size = rows if final else 72
        width = COLS if final else 2 * COLS

        def own(base):
            return jnp.concatenate([X5[base + kk * 32 : base + kk * 32 + height, :] for kk in range(2)], axis=0)

        def piece(p):
            return T6.at[p, pl.ds(0, size)], R6.at[me_lon, pl.ds(0, size)], R6.at[p, pl.ds(0, size)]

        def one(step, carry):
            first = far_first(2 * step + 1)
            second = jnp.where(step == N // 2 - 1, 0, far_first(2 * step + 2))
            ps = [lax.rem(me_lon + first, N), lax.rem(me_lon + second, N)]
            his, los = [], []
            a, b = own(0), own(64)
            for p in ps:
                c = C16[pl.ds(p, 1), :]
                s = S16[pl.ds(p, 1), :]
                hi, lo = split(jnp.concatenate([a * c + b * s, b * c - a * s], axis=1))
                his.append(hi)
                los.append(lo)
            r = dot(jnp.concatenate(his + los, axis=0), WH[:, 0:width])
            both = r[0 : 2 * rows] + r[2 * rows :] + dot(jnp.concatenate(his, axis=0), WL[:, 0:width])
            for q, p in enumerate(ps):
                r = both[q * rows : (q + 1) * rows]
                T6[p, 0:rows, :] = r[:, 0:COLS]
                if not final:
                    side = r[0:8, COLS:]
                    for t in range(1, 8):
                        v = pltpu.roll(r[8 * t : 8 * t + 8, COLS:], 8 * t, 1)
                        side = jnp.where(lane8 // 8 == t, v, side)
                    T6[p, 64:72, :] = side
                src, dst, _ = piece(p)
                if q == 0:
                    exchange(5, "lon", src, dst, p, me_lon).start()
                else:

                    @pl.when(step < N // 2 - 1)
                    def _():
                        exchange(5, "lon", src, dst, p, me_lon).start()

            return carry

        lax.fori_loop(0, N // 2, one, 0)
        R6[me_lon, 0:size] = T6[me_lon, 0:size]
        if final:
            for kk in range(2):
                pot_copy(me_lon, kk).start()
        else:
            force(me_lon)

        def wait(d, carry):
            p = arrival(d)
            src, _, dst = piece(p)
            copy = exchange(5, "lon", src, dst, p, p)
            copy.wait_send()
            copy.wait_recv()
            if final:
                for kk in range(2):
                    pot_copy(p, kk).start()
            else:
                force(p)
            return carry

        lax.fori_loop(1, N, wait, 0)
        if not final:
            Ac[0] = Ac[0] + loadx[...] * Rd[0]

    def send_density():
        def one(q, carry):
            for kk in range(2):
                k = kk * N + q
                dens[q, kk] = rho[k] * U[0, k + 1, 0:ROWS, 0:COLS]
            return carry

        lax.fori_loop(0, N // 2, lambda h, c: one(2 * h + 1, one(2 * h, c)), 0)

        def start(d, carry):
            p = lax.rem(me_lon + far_first(d), N)
            exchange(0, "lon", dens.at[p], R1.at[me_lon], p, me_lon).start()
            return carry

        lax.fori_loop(1, N, start, 0)

    for copy in loads:
        copy.wait()
    prepare()
    E[0] = pack(lambda k: U[0, k + 1, 0:ROWS, 0:COLS], 0)
    E[1] = pack(lambda k: U[0, k + 1, 0:ROWS, 0:COLS], 1)
    E[2] = pack(lambda k: matf[k], 0)
    E[3] = pack(lambda k: matf[k], 1)
    E[4] = pltpu.roll(load[...], 4, 1)
    pair_u(0)

    def pair_mat(k):
        pair_rows(16 + k, matf[k, 0:8], matf[k, 16:24], matf[k + 16, 0:8], matf[k + 16, 16:24])

    unrolled(16, 4, pair_mat)
    pair_rows(32, load[0:8], load[16:24], load[0:8], load[16:24])
    for g in range(4):
        GP[g] = jnp.concatenate([GA[4 * g + q] for q in range(4)], axis=1)
    tables()
    block, state = legendre_setup()
    state = lax.fori_loop(0, 2, block, state)
    pl.semaphore_wait(barrier, 2 * N - 1)
    edges = edge_copies(0)
    rows = row_copies(0, False)
    for copy in edges + rows:
        copy.start()
    state = lax.fori_loop(2, 12, block, state)
    for copy in edges:
        copy.wait()
    merge_edges(0)
    pair_packed(33, 0)
    pair_packed(34, 2)
    pair_rows(35, PK[4, 0:8], PK[4, 16:24], PK[4, 0:8], PK[4, 16:24])
    corners = row_copies(0, True)
    for copy in corners:
        copy.start()
    lax.fori_loop(12, 32, block, state)
    main_coefficients()
    for copy in rows + corners:
        copy.wait()
    green = pltpu.make_async_remote_copy(
        GP,
        GQ,
        gsem.at[0],
        gsem.at[1],
        device_id={"lat": lax.rem(me_lon + N - 1, N), "lon": me_lat},
        device_id_type=MESH,
    )
    green.start()
    fill_u(0, 33)
    margin_coefficients()

    for it in range(2):
        for s in range(SWEEPS):
            sweep(s % 2, (s + 1) % 2, s == SWEEPS - 1)
        send_density()
        if it == 0:
            E[5] = pack(lambda k: U[0, k + 1, 0:ROWS, 0:COLS], 0)
            E[6] = pack(lambda k: U[0, k + 1, 0:ROWS, 0:COLS], 1)
        else:
            u_copy = pltpu.make_async_copy(main, u_out, outsem.at[2 * N])
            u_copy.start()
        forward_fourier()
        swap_start(1, "lat", me_lat, T2, R2, N)
        if it == 0:
            edges = edge_copies(1)
            for copy in edges:
                copy.start()
            transpose_legendre()
        swap_wait(1, "lat", me_lat, T2, R2, N)
        forward_legendre()
        if it == 0:
            for copy in edges:
                copy.wait()
            merge_edges(1)
            pair_u(36)
            pair_packed(52, 0)
            rows = row_copies(1, False)
            for copy in rows:
                copy.start()
            green.wait()
            expand_green()
        swap_wait(2, "lon", me_lon, T3, R3, 8)
        layer_sum()
        swap_start(3, "lon", me_lon, T4, R4, 8)
        swap_wait(3, "lon", me_lon, T4, R4, 8)
        inverse_legendre()
        if it == 0:
            for copy in rows:
                copy.wait()
            fill_u(36, 52)
        swap_wait(4, "lat", me_lat, T5, R5, N)
        inverse_fourier(it == 1)

    def finish(j):
        for kk in range(2):
            pot_copy(j, kk).wait()

    unrolled(N, 4, finish)
    u_copy.wait()


def on_device(displacement, materials, ice_mask, ice_height, shear, restoring, contrast, green):
    hbm = pl.BlockSpec(memory_space=pl.ANY)
    smem = pl.BlockSpec(memory_space=pltpu.SMEM)
    field = jax.ShapeDtypeStruct((L, ROWS, COLS), F32)
    scratch = [
        ((2, L + 2, 32, 256), F32),
        ((L, 32, 256), F32),
        ((L, 32, 256), F32),
        ((L, 32, 256), F32),
        ((L, ROWS, COLS), F32),
        ((N, 2, ROWS, COLS), F32),
        ((N, 2, ROWS, COLS), F32),
        ((COLS, 512), BF16),
        ((COLS, 512), BF16),
        ((512, 256), BF16),
        ((512, 256), BF16),
        ((N, LMAX), F32),
        ((N, LMAX), F32),
        ((2 * ROWS, LMAX), F32),
        ((128, LMAX), F32),
        ((LMAX, COLS), F32),
        ((LMAX, COLS), F32),
        ((128, 512), BF16),
        ((N, 512, LMAX), BF16),
        ((N, 512, LMAX), BF16),
        ((8 * N, COLS), F32),
        ((8 * N, COLS), F32),
        ((8 * N, COLS), F32),
        ((8 * N, COLS), F32),
        ((8 * N, COLS), F32),
        ((8 * N, COLS), F32),
        ((128, N * LMAX), BF16),
        ((LMAX, COLS), F32),
        ((LMAX, COLS), F32),
        ((128, LMAX), F32),
        ((N, 72, COLS), F32),
        ((N, 72, COLS), F32),
        ((L, ROWS, COLS), jnp.int32),
        ((ROWS, COLS), jnp.int32),
        ((ROWS, COLS), F32),
        ((N, L, L), F32),
        ((4, L, COLS), F32),
        ((4, L, COLS), F32),
        ((N, L, L), F32),
        ((2, L * L, COLS), F32),
        ((N * LMAX, 512), BF16),
        ((N * LMAX, 512), BF16),
        ((L, ROWS, COLS), F32),
        ((ROWS, COLS), F32),
        ((32, 256), F32),
        ((7, ROWS, COLS), F32),
        ((7, ROWS, COLS), F32),
        ((7, ROWS, COLS), F32),
        ((5, 32, COLS), F32),
        ((53, 8, COLS), F32),
        ((53, 8, COLS), F32),
        ((53, 8, COLS), F32),
        ((53, 8, COLS), F32),
    ]
    return pl.pallas_call(
        kernel,
        out_shape=(field, field),
        in_specs=[hbm] * 4 + [smem] * 3 + [hbm],
        out_specs=(hbm, hbm),
        scratch_shapes=[pltpu.VMEM(shape, dtype) for shape, dtype in scratch]
        + [
            pltpu.SemaphoreType.DMA((6, N)),
            pltpu.SemaphoreType.DMA((6, N)),
            pltpu.SemaphoreType.DMA((2, 6)),
            pltpu.SemaphoreType.DMA((2, 6)),
            pltpu.SemaphoreType.DMA((2,)),
            pltpu.SemaphoreType.DMA((5,)),
            pltpu.SemaphoreType.DMA((2 * N + 1,)),
        ],
        compiler_params=pltpu.CompilerParams(
            collective_id=0, has_side_effects=True, vmem_limit_bytes=60 * 1024 * 1024
        ),
    )(displacement, materials, ice_mask, ice_height, shear, restoring, contrast, green)


def solution(mesh):
    in_specs = (
        P(None, "lat", "lon"),
        P(None, "lat", "lon"),
        P("lat", "lon"),
        P("lat", "lon"),
        P(),
        P(),
        P(),
        P("lat", None, None),
    )
    out_specs = (P(None, "lat", "lon"), P(None, "lat", "lon"))
    return jax.shard_map(
        on_device, mesh=mesh, in_specs=in_specs, out_specs=out_specs, check_vma=False
    )
```

```python
import functools
import math

import jax
import jax.numpy as jnp
from jax import lax
from jax.experimental import pallas as pl
from jax.experimental.pallas import tpu as pltpu
from jax.sharding import PartitionSpec as P

L = 32
LMAX = 256
NLAT = 384
NLON = 2048
SWEEPS = 4
N = 16
ROWS = 24
COLS = 128
F32 = jnp.float32
BF16 = jnp.bfloat16
MESH = pl.DeviceIdType.MESH


def iota(shape, dim):
    return lax.broadcasted_iota(jnp.int32, shape, dim)


def split(x):
    hi = x.astype(BF16)
    lo = (x - hi.astype(F32)).astype(BF16)
    return hi, lo


def dot(a, b):
    return jnp.dot(a, b, preferred_element_type=F32)


def dot_t(a, b):
    return lax.dot_general(a, b, (((1,), (1,)), ((), ())), preferred_element_type=F32)


def unrolled(total, factor, one):
    def body(step, carry):
        for part in range(factor):
            one(step * factor + part)
        return carry

    lax.fori_loop(0, total // factor, body, 0)


def lookup(mat, table):
    out = jnp.where(mat == 0, table[0], 0.0)
    for material in range(1, 4):
        out = jnp.where(mat == material, table[material], out)
    return out


def kernel(
    u_in,
    mat_in,
    mask_in,
    ice_in,
    shear,
    restoring,
    contrast,
    green_in,
    u_out,
    pot_out,
    U,
    Bc,
    Rd,
    Ac,
    rho,
    dens,
    R1,
    FH,
    FL,
    WH,
    WL,
    C16,
    S16,
    wrow,
    Z,
    T2,
    R2,
    AH,
    Qh,
    Ql,
    T3,
    R3,
    T4,
    R4,
    RH,
    RL,
    XH,
    T5,
    R5,
    X5,
    T6,
    R6,
    mats,
    masks,
    ice,
    GA,
    GP,
    GQ,
    GR,
    GX,
    Ph,
    Pl,
    matf,
    load,
    loadx,
    E,
    EL,
    ER,
    PK,
    VT,
    VB,
    WT,
    WB,
    send_sem,
    recv_sem,
    hsend,
    hrecv,
    gsem,
    insem,
    outsem,
):
    me_lat = lax.axis_index("lat")
    me_lon = lax.axis_index("lon")

    barrier = pltpu.get_barrier_semaphore()

    def greet(d, carry):
        pl.semaphore_signal(barrier, inc=1, device_id={"lon": lax.rem(me_lon + d, N)}, device_id_type=MESH)
        pl.semaphore_signal(barrier, inc=1, device_id={"lat": lax.rem(me_lat + d, N)}, device_id_type=MESH)
        return carry

    lax.fori_loop(1, N, greet, 0)
    pl.semaphore_signal(
        barrier, inc=1, device_id={"lat": me_lon, "lon": lax.rem(me_lat + 1, N)}, device_id_type=MESH
    )

    main = U.at[0, pl.ds(1, L), pl.ds(0, ROWS), pl.ds(0, COLS)]
    loads = [
        pltpu.make_async_copy(mat_in, mats, insem.at[0]),
        pltpu.make_async_copy(u_in, main, insem.at[1]),
        pltpu.make_async_copy(mask_in, masks, insem.at[2]),
        pltpu.make_async_copy(ice_in, ice, insem.at[3]),
        pltpu.make_async_copy(green_in, GA, insem.at[4]),
    ]
    for copy in loads:
        copy.start()

    def tables():
        q = iota((COLS, LMAX), 0)
        m = iota((COLS, LMAX), 1)
        angle = (2.0 * math.pi / NLON) * ((q * m) & (NLON - 1)).astype(F32)
        hi, lo = split(jnp.cos(angle))
        FH[:, 0:LMAX] = hi
        FL[:, 0:LMAX] = lo
        hi, lo = split(jnp.sin(angle))
        FH[:, LMAX:] = hi
        FL[:, LMAX:] = lo
        p = iota((N, LMAX), 0)
        m = iota((N, LMAX), 1)
        angle = (2.0 * math.pi / N) * ((p * m) & (N - 1)).astype(F32)
        C16[...] = jnp.cos(angle)
        S16[...] = jnp.sin(angle)
        lane = iota((LMAX, 2 * COLS), 1)
        m = iota((LMAX, 2 * COLS), 0)
        q = jnp.where(lane < 128, lane, jnp.where(lane < 132, lane - 132 + NLON, lane - 4))
        angle = (2.0 * math.pi / NLON) * ((q * m) & (NLON - 1)).astype(F32)
        hi, lo = split(jnp.cos(angle))
        WH[0:LMAX, :] = hi
        WL[0:LMAX, :] = lo
        hi, lo = split(jnp.sin(angle))
        WH[LMAX:, :] = hi
        WL[LMAX:, :] = lo
        row = iota((ROWS, LMAX), 0) + me_lat * ROWS
        w = jnp.sin((row.astype(F32) + 0.5) * (math.pi / NLAT)) * (2.0 * math.pi / NLON / (4.0 * NLAT))
        wrow[0:ROWS, :] = w
        wrow[ROWS:, :] = w
        Z[...] = jnp.zeros_like(Z)
        for b in range(2):
            U[b, 0] = jnp.zeros((32, 256), F32)
            U[b, L + 1] = jnp.zeros((32, 256), F32)

    def prepare():
        def one(k):
            mat = mats[k]
            matf[k] = mat.astype(F32)
            rho[k] = lookup(mat, contrast)

        unrolled(L, 4, one)
        load[...] = masks[...].astype(F32) * ice[...]

    lane24 = iota((ROWS, COLS), 1)

    def pack(read, g):
        acc = jnp.zeros((ROWS, COLS), F32)
        for kk in range(16):
            acc = jnp.where(lane24 // 8 == kk, pltpu.roll(read(16 * g + kk), (8 * kk + 4) % COLS, 1), acc)
        return acc

    left = lax.rem(me_lon + N - 1, N)
    right = lax.rem(me_lon + 1, N)
    up = lax.rem(me_lat + N - 1, N)
    down = lax.rem(me_lat + 1, N)

    def edge_copies(it):
        first, count = (0, 5) if it == 0 else (5, 2)
        part = pl.ds(first, count)
        return [
            pltpu.make_async_remote_copy(
                E.at[part], ER.at[part], hsend.at[it, 0], hrecv.at[it, 0], device_id={"lon": left}, device_id_type=MESH
            ),
            pltpu.make_async_remote_copy(
                E.at[part], EL.at[part], hsend.at[it, 1], hrecv.at[it, 1], device_id={"lon": right}, device_id_type=MESH
            ),
        ]

    def row_copies(it, corners):
        if it == 0:
            first, count = (33, 3) if corners else (0, 33)
        else:
            first, count = (36, 17)
        part = pl.ds(first, count)
        one = 4 if corners else 2
        return [
            pltpu.make_async_remote_copy(
                VT.at[part],
                WT.at[part],
                hsend.at[it, one],
                hrecv.at[it, one],
                device_id={"lat": up},
                device_id_type=MESH,
            ),
            pltpu.make_async_remote_copy(
                VB.at[part],
                WB.at[part],
                hsend.at[it, one + 1],
                hrecv.at[it, one + 1],
                device_id={"lat": down},
                device_id_type=MESH,
            ),
        ]

    def merge_edges(it):
        first, count = (0, 5) if it == 0 else (5, 2)
        for g in range(count):
            PK[g, 0:ROWS] = jnp.where(lane24 % 8 < 4, EL[first + g], ER[first + g])

    row8 = iota((8, COLS), 0)

    def pair_rows(t, a_top, a_bot, b_top, b_bot):
        VT[t] = jnp.where(row8 < 4, a_top, pltpu.roll(b_top, 4, 0))
        VB[t] = jnp.where(row8 < 4, pltpu.roll(a_bot, 4, 0), b_bot)

    def halo_rows(t):
        top, bot = WT[t], WB[t]
        first = jnp.where(row8 < 4, top, pltpu.roll(bot, 4, 0))
        second = jnp.where(row8 < 4, pltpu.roll(top, 4, 0), bot)
        return first, second

    rows32 = iota((32, 256), 0)
    global_row = me_lat * ROWS + jnp.where(rows32 < 28, rows32, rows32 - 32)
    inside = (global_row >= 0) & (global_row < NLAT)
    inside8 = inside[24:32, 0:COLS]

    def pair_u(base):
        def one(k):
            pair_rows(
                base + k,
                U[0, k + 1, 0:8, 0:COLS],
                U[0, k + 1, 16:24, 0:COLS],
                U[0, k + 17, 0:8, 0:COLS],
                U[0, k + 17, 16:24, 0:COLS],
            )

        unrolled(16, 4, one)

    def pair_packed(t, g):
        pair_rows(t, PK[g, 0:8], PK[g, 16:24], PK[g + 1, 0:8], PK[g + 1, 16:24])

    def fill_u(base, packed):
        first, second = halo_rows(packed)
        PK[0, 24:32] = jnp.where(inside8, first, 0.0)
        PK[1, 24:32] = jnp.where(inside8, second, 0.0)

        def one(k):
            first, second = halo_rows(base + k)
            U[0, k + 1, 24:32, 0:COLS] = jnp.where(inside8, first, 0.0)
            U[0, k + 17, 24:32, 0:COLS] = jnp.where(inside8, second, 0.0)
            U[0, k + 1, :, COLS:] = pltpu.roll(PK[0], 124 - 8 * k, 1)
            U[0, k + 17, :, COLS:] = pltpu.roll(PK[1], 124 - 8 * k, 1)

        unrolled(16, 4, one)

    def legendre_setup():
        lane = iota((N, 512), 1)
        order = (iota((N, 512), 0) + me_lat * N).astype(F32)
        aa = lane % 32
        a = (lane // 32) * ROWS + jnp.where(aa < 28, aa, aa - 32)
        a = jnp.clip(a, 0, NLAT - 1)
        theta = (a.astype(F32) + 0.5) * (math.pi / NLAT)
        cosine = jnp.cos(theta)
        sine = jnp.sin(theta)
        t = iota((N, LMAX), 1)
        m_int = iota((N, LMAX), 0) + me_lat * N
        t_f = jnp.maximum(t.astype(F32), 1.0)
        growth = jnp.where((t >= 2) & (t <= m_int), 0.5 * jnp.log((2.0 * t_f + 1.0) / (2.0 * t_f)), 0.0)
        log_diag = jnp.sum(growth, axis=1, keepdims=True) + 0.5 * math.log(3.0)
        log_diag = jnp.where(m_int[:, 0:1] >= 1, log_diag, 0.0)
        diagonal = jnp.exp(log_diag + order * jnp.log(sine))
        start = jnp.sqrt(2.0 * order + 3.0) * cosine * diagonal
        deg = iota((N, LMAX), 1).astype(F32)
        m_f = m_int.astype(F32)
        first = jnp.sqrt(
            jnp.maximum(4.0 * deg * deg - 1.0, 1.0) / jnp.maximum(deg * deg - m_f * m_f, 1.0)
        )
        second = jnp.sqrt(
            jnp.maximum((deg - 1.0) * (deg - 1.0) - m_f * m_f, 0.0)
            / jnp.maximum(4.0 * (deg - 1.0) * (deg - 1.0) - 1.0, 1.0)
        )
        order_i = iota((N, 512), 0) + me_lat * N

        def block(lb, carry):
            one, two = carry
            shift = lax.rem(LMAX - 8 * lb, LMAX)
            f = pltpu.roll(first, shift, 1)[:, 0:COLS]
            s = pltpu.roll(second, shift, 1)[:, 0:COLS]
            for r in range(8):
                degree = lb * 8 + r
                fb = jnp.broadcast_to(f[:, r : r + 1], (N, 512))
                sb = jnp.broadcast_to(s[:, r : r + 1], (N, 512))
                general = fb * (cosine * one - sb * two)
                value = jnp.where(
                    order_i == degree, diagonal, jnp.where(order_i == degree - 1, start, general)
                )
                hi, lo = split(value)
                here = pl.ds(pl.multiple_of(degree * N, N), N)
                Ph[here, :] = hi
                Pl[here, :] = lo
                one, two = value, one
            return one, two

        zeros = jnp.zeros((N, 512), F32)
        return block, (zeros, zeros)

    def exchange(phase, axis, src, dst, peer, sender):
        if 1 <= phase <= 4:
            sender, slot = 0, 0
        else:
            slot = peer
        return pltpu.make_async_remote_copy(
            src,
            dst,
            send_sem.at[phase, slot],
            recv_sem.at[phase, sender],
            device_id={axis: peer},
            device_id_type=MESH,
        )

    def slab(ref, index, size):
        return ref.at[pl.ds(pl.multiple_of(index * size, size), size)]

    def far_first(d):
        return lax.rem(d + 6, N - 1) + 1

    def arrival(d):
        return lax.rem(me_lon + N - far_first(d), N)

    def swap_start(phase, axis, me, src, dst, size):
        for d in range(1, N):
            peer = lax.rem(me + (d + 6) % (N - 1) + 1, N)
            exchange(phase, axis, slab(src, peer, size), slab(dst, me, size), peer, me).start()
        mine = pl.ds(pl.multiple_of(me * size, size), size)
        dst[mine, :] = src[mine, :]

    def swap_wait(phase, axis, me, src, dst, size):
        part = pl.ds(0, (N - 1) * size)
        copy = exchange(phase, axis, src.at[part], dst.at[part], lax.rem(me + 1, N), 0)
        copy.wait_recv()
        copy.wait_send()

    lane32 = iota((32, COLS), 1)

    def sweep(src, dst, last):
        rows = ROWS if last else 32

        def one(k):
            t0 = U[src, k + 1, :, 0:COLS]
            t1 = U[src, k + 1, :, COLS:]
            r0, r1 = pltpu.roll(t0[0:rows], 1, 1), pltpu.roll(t1[0:rows], 1, 1)
            l0, l1 = pltpu.roll(t0[0:rows], COLS - 1, 1), pltpu.roll(t1[0:rows], COLS - 1, 1)
            first = lane32[0:rows] == 0
            final = lane32[0:rows] == COLS - 1
            around = (
                (jnp.where(first, r1, r0) + jnp.where(final, l1, l0))
                + (pltpu.roll(t0, 1, 0) + pltpu.roll(t0, 31, 0))[0:rows]
                + (U[src, k, 0:rows, 0:COLS] + U[src, k + 2, 0:rows, 0:COLS])
            )
            U[dst, k + 1, 0:rows, 0:COLS] = Ac[k, 0:rows, 0:COLS] + Bc[k, 0:rows, 0:COLS] * around
            if not last:
                around = (
                    (jnp.where(first, r0, r1) + jnp.where(final, l0, l1))
                    + (pltpu.roll(t1, 1, 0) + pltpu.roll(t1, 31, 0))
                    + (U[src, k, :, COLS:] + U[src, k + 2, :, COLS:])
                )
                U[dst, k + 1, :, COLS:] = Ac[k, :, COLS:] + Bc[k, :, COLS:] * around

        unrolled(L, 4, one)

    def coefficient(k, rows, cols, mat, valid):
        st = lookup(mat, shear)
        re = lookup(mat, restoring)
        inv = 1.0 / (6.0 * st + re)
        if valid is not None:
            inv = jnp.where(valid, inv, 0.0)
        Rd[k, rows, cols] = inv
        Bc[k, rows, cols] = st * inv
        Ac[k, rows, cols] = jnp.zeros(inv.shape, F32)

    def main_coefficients():
        unrolled(L, 4, lambda k: coefficient(k, slice(0, ROWS), slice(0, COLS), matf[k], None))

    inside_side = inside[:, 0:COLS]

    def margin_coefficients():
        first, second = halo_rows(34)
        PK[2, 24:32] = first
        PK[3, 24:32] = second

        def one(k):
            first, second = halo_rows(16 + k)
            coefficient(k, slice(ROWS, 32), slice(0, COLS), first, inside8)
            coefficient(k + 16, slice(ROWS, 32), slice(0, COLS), second, inside8)
            for g in range(2):
                side = pltpu.roll(PK[2 + g], 124 - 8 * k, 1)
                coefficient(k + 16 * g, slice(0, 32), slice(COLS, 2 * COLS), side, inside_side)

        unrolled(16, 2, one)
        PK[4, 24:32] = halo_rows(35)[0]
        loadx[0:ROWS, 0:COLS] = load[...]
        loadx[ROWS:, 0:COLS] = halo_rows(32)[0]
        loadx[:, COLS:] = pltpu.roll(PK[4], 124, 1)
        Ac[0] = loadx[...] * Rd[0]

    lane16 = iota((N, COLS), 1)
    diagonal64 = iota((64, LMAX), 0) % N == iota((64, LMAX), 1) % N
    diagonal16 = iota((N, COLS), 0) == iota((N, COLS), 1) % N

    def forward_fourier():
        def pair(step, acc):
            acc_c, acc_s = acc
            ps = [jnp.where(step == 0, me_lon, arrival(2 * step)), arrival(2 * step + 1)]
            his, los = zip(*[split(R1[p].reshape(2 * ROWS, COLS)) for p in ps])
            r = dot(jnp.concatenate(his + los, axis=0), FH[...])
            r = r[0 : 4 * ROWS] + r[4 * ROWS :] + dot(jnp.concatenate(his, axis=0), FL[...])
            for q, p in enumerate(ps):
                yc = r[2 * ROWS * q : 2 * ROWS * (q + 1), 0:LMAX]
                ys = r[2 * ROWS * q : 2 * ROWS * (q + 1), LMAX:]
                c = C16[pl.ds(p, 1), :]
                s = S16[pl.ds(p, 1), :]
                acc_c, acc_s = acc_c + (c * yc - s * ys), acc_s + (s * yc + c * ys)
            return acc_c, acc_s

        def wait(d):
            p = arrival(d)
            copy = exchange(0, "lon", dens.at[p], R1.at[p], p, p)
            copy.wait_send()
            copy.wait_recv()

        def one(step, acc):
            wait(2 * step)
            wait(2 * step + 1)
            return pair(step, acc)

        zeros = jnp.zeros((2 * ROWS, LMAX), F32)
        R1[me_lon] = dens[me_lon]
        wait(1)
        acc_c, acc_s = lax.fori_loop(1, N // 2, one, pair(0, (zeros, zeros)))
        for c, acc in ((0, acc_c), (1, acc_s)):
            acc = acc * wrow[...]
            for kk in range(2):
                Z[(2 * c + kk) * 32 : (2 * c + kk) * 32 + ROWS, :] = acc[kk * ROWS : (kk + 1) * ROWS]
        T2[...] = jnp.transpose(Z[...])

    def transpose_legendre():
        def one(b):
            here = pl.ds(pl.multiple_of(b * LMAX, LMAX), LMAX)
            for src, dst in ((Ph, Qh), (Pl, Ql)):
                dst[b] = jnp.transpose(src[here, :])

        unrolled(N, 1, one)

    def forward_legendre():
        for t in range(4):
            parts = [R2[(4 * t + ii) * N : (4 * t + ii + 1) * N, :] for ii in range(4)]
            for ck in range(4):
                out = None
                for ii in range(4):
                    turn = ((ii - ck) * 32) % COLS
                    v = parts[ii] if turn == 0 else pltpu.roll(parts[ii], turn, 1)
                    out = v if out is None else jnp.where(lane16 // 32 == ii, v, out)
                hi, lo = split(out)
                AH[ck * N : (ck + 1) * N, t * COLS : (t + 1) * COLS] = hi
                AH[64 + ck * N : 64 + (ck + 1) * N, t * COLS : (t + 1) * COLS] = lo

        def product(b):
            r = dot(AH[...], Qh[b])
            return r[0:64] + r[64:] + dot(AH[0:64], Ql[b])

        def one(step, carry):
            bs = [lax.rem(me_lon + 1 + 4 * step + q, N) for q in range(4)]
            products = [product(b) for b in bs]
            for q, (b, r) in enumerate(zip(bs, products)):
                r = jnp.where(diagonal64, r, 0.0)
                totals = [
                    jnp.sum(r[ck * N : ck * N + 8] + r[ck * N + 8 : ck * N + 16], axis=0, keepdims=True)
                    for ck in range(4)
                ]
                out = [v[:, t * COLS : (t + 1) * COLS] for t in range(2) for v in totals]
                T3[pl.ds(pl.multiple_of(b * 8, 8), 8), :] = jnp.concatenate(out, axis=0)
                copy = exchange(2, "lon", slab(T3, b, 8), slab(R3, me_lon, 8), b, me_lon)
                if q < 3:
                    copy.start()
                else:
                    pl.when(step < 3)(copy.start)
            return carry

        lax.fori_loop(0, 4, one, 0)
        mine = pl.ds(pl.multiple_of(me_lon * 8, 8), 8)
        R3[mine, :] = T3[mine, :]

    def expand_green():
        chosen = (iota((N, LMAX), 0) == iota((N, LMAX), 1) // N).astype(F32)
        for g in range(4):
            for q in range(4):
                GR[4 * g + q] = GQ[g, :, q * L : (q + 1) * L]
        for k in range(L):
            out = lax.dot_general(
                GR[:, k, :],
                chosen,
                (((0,), (0,)), ((), ())),
                precision=lax.Precision.HIGHEST,
                preferred_element_type=F32,
            )
            GX[0, pl.ds(k, L, stride=L), :] = out[:, 0:COLS]
            GX[1, pl.ds(k, L, stride=L), :] = out[:, COLS:]

    def layer_sum():
        for t in range(2):
            acc = [jnp.zeros((L, COLS), F32), jnp.zeros((L, COLS), F32)]
            for k in range(L):
                kk, j = k // N, k % N
                g = GX[t, k * L : (k + 1) * L, :]
                for c in range(2):
                    row = j * 8 + t * 4 + 2 * c + kk
                    acc[c] = acc[c] + g * R3[row : row + 1, :]
            for c in range(2):
                for kk in range(2):
                    T4[pl.ds(t * 4 + 2 * c + kk, N, stride=8), :] = acc[c][kk * N : (kk + 1) * N]

    def inverse_legendre():
        x = R4[...]
        hi = x.astype(BF16).astype(F32)
        RH[...] = hi
        RL[...] = x - hi

        def build(b):
            for ck in range(4):
                for t in range(2):
                    row = pl.ds(b * 8 + t * 4 + ck, 1)
                    cols = pl.ds(pl.multiple_of(b * LMAX + t * COLS, COLS), COLS)
                    for base, ref in ((0, RH), (64, RL)):
                        v = jnp.where(diagonal16, ref[row, :], 0.0)
                        XH[base + ck * N : base + (ck + 1) * N, cols] = v.astype(BF16)

        unrolled(N, 2, build)

        def half(chunk):
            lanes = pl.ds(pl.multiple_of(chunk * 2 * COLS, 2 * COLS), 2 * COLS)

            def one(step, acc):
                here = pl.ds(pl.multiple_of(step * 4 * LMAX, 4 * LMAX), 4 * LMAX)
                r = dot(XH[:, here], Ph[here, lanes])
                return acc + (r[0:64] + r[64:] + dot(XH[0:64, here], Pl[here, lanes]))

            y = lax.fori_loop(0, 4, one, jnp.zeros((64, 2 * COLS), F32))
            for i8 in range(8):
                t, ii = i8 // 4, i8 % 4
                out = None
                for ck in range(4):
                    turn = ((ck - ii) * 32) % COLS
                    v = y[ck * N : (ck + 1) * N, t * COLS : (t + 1) * COLS]
                    v = v if turn == 0 else pltpu.roll(v, turn, 1)
                    out = v if out is None else jnp.where(lane16 // 32 == ck, v, out)
                i = chunk * 8 + i8
                T5[pl.ds(pl.multiple_of(i * N, N), N), :] = out

                @pl.when(i != me_lat)
                def _():
                    exchange(4, "lat", slab(T5, i, N), slab(R5, me_lat, N), i, me_lat).start()

        near = me_lat // 8
        half(1 - near)
        half(near)
        mine = pl.ds(pl.multiple_of(me_lat * N, N), N)
        R5[mine, :] = T5[mine, :]

    lane8 = iota((8, COLS), 1)

    def force(j):
        side = R6[j, 64:72, :]
        for kk in range(2):
            k = kk * N + j
            main = R6[j, kk * 32 : (kk + 1) * 32, :]
            halo = jnp.concatenate([pltpu.roll(side, 124 - 8 * (4 * kk + g), 1) for g in range(4)], axis=0)
            Ac[k] = jnp.concatenate([main, halo], axis=1) * Rd[k]

    def pot_copy(j, kk):
        return pltpu.make_async_copy(
            R6.at[j, pl.ds(kk * ROWS, ROWS)], pot_out.at[kk * N + j], outsem.at[2 * j + kk]
        )

    def inverse_fourier(final):
        X5[...] = jnp.transpose(R5[...])
        height = ROWS if final else 32
        rows = 2 * height
        size = rows if final else 72
        width = COLS if final else 2 * COLS

        def own(base):
            return jnp.concatenate([X5[base + kk * 32 : base + kk * 32 + height, :] for kk in range(2)], axis=0)

        def piece(p):
            return T6.at[p, pl.ds(0, size)], R6.at[me_lon, pl.ds(0, size)], R6.at[p, pl.ds(0, size)]

        def one(step, carry):
            first = far_first(2 * step + 1)
            second = jnp.where(step == N // 2 - 1, 0, far_first(2 * step + 2))
            ps = [lax.rem(me_lon + first, N), lax.rem(me_lon + second, N)]
            his, los = [], []
            a, b = own(0), own(64)
            for p in ps:
                c = C16[pl.ds(p, 1), :]
                s = S16[pl.ds(p, 1), :]
                hi, lo = split(jnp.concatenate([a * c + b * s, b * c - a * s], axis=1))
                his.append(hi)
                los.append(lo)
            r = dot(jnp.concatenate(his + los, axis=0), WH[:, 0:width])
            both = r[0 : 2 * rows] + r[2 * rows :] + dot(jnp.concatenate(his, axis=0), WL[:, 0:width])
            for q, p in enumerate(ps):
                r = both[q * rows : (q + 1) * rows]
                T6[p, 0:rows, :] = r[:, 0:COLS]
                if not final:
                    side = r[0:8, COLS:]
                    for t in range(1, 8):
                        v = pltpu.roll(r[8 * t : 8 * t + 8, COLS:], 8 * t, 1)
                        side = jnp.where(lane8 // 8 == t, v, side)
                    T6[p, 64:72, :] = side
                src, dst, _ = piece(p)
                if q == 0:
                    exchange(5, "lon", src, dst, p, me_lon).start()
                else:

                    @pl.when(step < N // 2 - 1)
                    def _():
                        exchange(5, "lon", src, dst, p, me_lon).start()

            return carry

        lax.fori_loop(0, N // 2, one, 0)
        R6[me_lon, 0:size] = T6[me_lon, 0:size]
        if final:
            for kk in range(2):
                pot_copy(me_lon, kk).start()
        else:
            force(me_lon)

        def wait(d, carry):
            p = arrival(d)
            src, _, dst = piece(p)
            copy = exchange(5, "lon", src, dst, p, p)
            copy.wait_send()
            copy.wait_recv()
            if final:
                for kk in range(2):
                    pot_copy(p, kk).start()
            else:
                force(p)
            return carry

        lax.fori_loop(1, N, wait, 0)
        if not final:
            Ac[0] = Ac[0] + loadx[...] * Rd[0]

    def send_density():
        def one(q, carry):
            for kk in range(2):
                k = kk * N + q
                dens[q, kk] = rho[k] * U[0, k + 1, 0:ROWS, 0:COLS]
            return carry

        lax.fori_loop(0, N // 2, lambda h, c: one(2 * h + 1, one(2 * h, c)), 0)

        for d in range(1, N):
            p = lax.rem(me_lon + (d + 6) % (N - 1) + 1, N)
            exchange(0, "lon", dens.at[p], R1.at[me_lon], p, me_lon).start()

    for copy in loads:
        copy.wait()
    prepare()
    E[0] = pack(lambda k: U[0, k + 1, 0:ROWS, 0:COLS], 0)
    E[1] = pack(lambda k: U[0, k + 1, 0:ROWS, 0:COLS], 1)
    E[2] = pack(lambda k: matf[k], 0)
    E[3] = pack(lambda k: matf[k], 1)
    E[4] = pltpu.roll(load[...], 4, 1)
    pair_u(0)

    def pair_mat(k):
        pair_rows(16 + k, matf[k, 0:8], matf[k, 16:24], matf[k + 16, 0:8], matf[k + 16, 16:24])

    unrolled(16, 4, pair_mat)
    pair_rows(32, load[0:8], load[16:24], load[0:8], load[16:24])
    for g in range(4):
        GP[g] = jnp.concatenate([GA[4 * g + q] for q in range(4)], axis=1)
    tables()
    block, state = legendre_setup()
    state = lax.fori_loop(0, 2, block, state)
    pl.semaphore_wait(barrier, 2 * N - 1)
    edges = edge_copies(0)
    rows = row_copies(0, False)
    for copy in edges + rows:
        copy.start()
    state = lax.fori_loop(2, 12, block, state)
    for copy in edges:
        copy.wait()
    merge_edges(0)
    pair_packed(33, 0)
    pair_packed(34, 2)
    pair_rows(35, PK[4, 0:8], PK[4, 16:24], PK[4, 0:8], PK[4, 16:24])
    corners = row_copies(0, True)
    for copy in corners:
        copy.start()
    lax.fori_loop(12, 32, block, state)
    main_coefficients()
    for copy in rows + corners:
        copy.wait()
    green = pltpu.make_async_remote_copy(
        GP,
        GQ,
        gsem.at[0],
        gsem.at[1],
        device_id={"lat": lax.rem(me_lon + N - 1, N), "lon": me_lat},
        device_id_type=MESH,
    )
    green.start()
    fill_u(0, 33)
    margin_coefficients()

    for it in range(2):
        for s in range(SWEEPS):
            sweep(s % 2, (s + 1) % 2, s == SWEEPS - 1)
        send_density()
        if it == 0:
            E[5] = pack(lambda k: U[0, k + 1, 0:ROWS, 0:COLS], 0)
            E[6] = pack(lambda k: U[0, k + 1, 0:ROWS, 0:COLS], 1)
        else:
            u_copy = pltpu.make_async_copy(main, u_out, outsem.at[2 * N])
            u_copy.start()
        forward_fourier()
        swap_start(1, "lat", me_lat, T2, R2, N)
        if it == 0:
            edges = edge_copies(1)
            for copy in edges:
                copy.start()
            transpose_legendre()
        swap_wait(1, "lat", me_lat, T2, R2, N)
        forward_legendre()
        if it == 0:
            for copy in edges:
                copy.wait()
            merge_edges(1)
            pair_u(36)
            pair_packed(52, 0)
            rows = row_copies(1, False)
            for copy in rows:
                copy.start()
            green.wait()
            expand_green()
        swap_wait(2, "lon", me_lon, T3, R3, 8)
        layer_sum()
        swap_start(3, "lon", me_lon, T4, R4, 8)
        swap_wait(3, "lon", me_lon, T4, R4, 8)
        inverse_legendre()
        if it == 0:
            for copy in rows:
                copy.wait()
            fill_u(36, 52)
        swap_wait(4, "lat", me_lat, T5, R5, N)
        inverse_fourier(it == 1)

    def finish(j):
        for kk in range(2):
            pot_copy(j, kk).wait()

    unrolled(N, 4, finish)
    u_copy.wait()


def on_device(displacement, materials, ice_mask, ice_height, shear, restoring, contrast, green):
    hbm = pl.BlockSpec(memory_space=pl.ANY)
    smem = pl.BlockSpec(memory_space=pltpu.SMEM)
    field = jax.ShapeDtypeStruct((L, ROWS, COLS), F32)
    scratch = [
        ((2, L + 2, 32, 256), F32),
        ((L, 32, 256), F32),
        ((L, 32, 256), F32),
        ((L, 32, 256), F32),
        ((L, ROWS, COLS), F32),
        ((N, 2, ROWS, COLS), F32),
        ((N, 2, ROWS, COLS), F32),
        ((COLS, 512), BF16),
        ((COLS, 512), BF16),
        ((512, 256), BF16),
        ((512, 256), BF16),
        ((N, LMAX), F32),
        ((N, LMAX), F32),
        ((2 * ROWS, LMAX), F32),
        ((128, LMAX), F32),
        ((LMAX, COLS), F32),
        ((LMAX, COLS), F32),
        ((128, 512), BF16),
        ((N, 512, LMAX), BF16),
        ((N, 512, LMAX), BF16),
        ((8 * N, COLS), F32),
        ((8 * N, COLS), F32),
        ((8 * N, COLS), F32),
        ((8 * N, COLS), F32),
        ((8 * N, COLS), F32),
        ((8 * N, COLS), F32),
        ((128, N * LMAX), BF16),
        ((LMAX, COLS), F32),
        ((LMAX, COLS), F32),
        ((128, LMAX), F32),
        ((N, 72, COLS), F32),
        ((N, 72, COLS), F32),
        ((L, ROWS, COLS), jnp.int32),
        ((ROWS, COLS), jnp.int32),
        ((ROWS, COLS), F32),
        ((N, L, L), F32),
        ((4, L, COLS), F32),
        ((4, L, COLS), F32),
        ((N, L, L), F32),
        ((2, L * L, COLS), F32),
        ((N * LMAX, 512), BF16),
        ((N * LMAX, 512), BF16),
        ((L, ROWS, COLS), F32),
        ((ROWS, COLS), F32),
        ((32, 256), F32),
        ((7, ROWS, COLS), F32),
        ((7, ROWS, COLS), F32),
        ((7, ROWS, COLS), F32),
        ((5, 32, COLS), F32),
        ((53, 8, COLS), F32),
        ((53, 8, COLS), F32),
        ((53, 8, COLS), F32),
        ((53, 8, COLS), F32),
    ]
    return pl.pallas_call(
        kernel,
        out_shape=(field, field),
        in_specs=[hbm] * 4 + [smem] * 3 + [hbm],
        out_specs=(hbm, hbm),
        scratch_shapes=[pltpu.VMEM(shape, dtype) for shape, dtype in scratch]
        + [
            pltpu.SemaphoreType.DMA((6, N)),
            pltpu.SemaphoreType.DMA((6, N)),
            pltpu.SemaphoreType.DMA((2, 6)),
            pltpu.SemaphoreType.DMA((2, 6)),
            pltpu.SemaphoreType.DMA((2,)),
            pltpu.SemaphoreType.DMA((5,)),
            pltpu.SemaphoreType.DMA((2 * N + 1,)),
        ],
        compiler_params=pltpu.CompilerParams(
            collective_id=0, has_side_effects=True, vmem_limit_bytes=60 * 1024 * 1024
        ),
    )(displacement, materials, ice_mask, ice_height, shear, restoring, contrast, green)


def solution(mesh):
    in_specs = (
        P(None, "lat", "lon"),
        P(None, "lat", "lon"),
        P("lat", "lon"),
        P("lat", "lon"),
        P(),
        P(),
        P(),
        P("lat", None, None),
    )
    out_specs = (P(None, "lat", "lon"), P(None, "lat", "lon"))
    return jax.shard_map(
        on_device, mesh=mesh, in_specs=in_specs, out_specs=out_specs, check_vma=False
    )
```
